32 devices in a mesh: lev: 4 (over z), lat: 4 (over y, core), lon: 2 (over x).
Axes of the slice: x: 2, y: 2, z: 4, core: 2. Of those that a mesh axis runs over, the one named last changes fastest.
Arguments:
- latent: bfloat16 [256, 128, 256], P(None, 'lat', 'lon'), may hold values from -6 to 6
- conv_weight: bfloat16 [16, 128, 9, 256], P('lev'), may hold values from -0.125 to 0.125
- mid_weight: bfloat16 [16, 128, 128], P('lev'), may hold values from -0.5 to 0.5
- out_weight: bfloat16 [16, 48, 128], P('lev'), may hold values from -0.5 to 0.5
- vertical_inner_matrix: bfloat16 [1024, 768], replicated, may hold values from -0.21875 to 0.21875
- vertical_outer_matrix: bfloat16 [768, 1024], replicated, may hold values from -0.1875 to 0.1875
- obs_values: float32 [4, 2, 256, 768], P('lat', 'lon'), may hold values from -6 to 6
- obs_weight: float32 [768], replicated, may hold values from 0.25 to 4
- obs_index: int32 [4, 2, 256], P('lat', 'lon'), may hold values from 0 to 4095
- obs_count: int32 [4, 2], P('lat', 'lon'), may hold values from 64 to 256
Outputs:
- latent_grad: float32 [256, 128, 256], P('lev', 'lat', 'lon')
The draws below stay inside these ranges and needn't reach their ends.
Inputs may be any that keep to these rules, and one draw needn't show every extreme that they name: `obs_index`: row-major index of a cell within its tile of 32 x 128 cells; indices may repeat. `obs_count`: slots from this number on hold no observation.
All inputs are finite; a program needn't handle non-finite values.
Results may differ from the reference program's by a relative error of at most 0.007.
Values may be sent and summed in bfloat16 or wider, within the bound.
No kernel may reach another device: no remote copies, remote signals or barrier semaphores. Data moves between devices by JAX's collectives and lax.ppermute only.
A program may use at most 192 MiB of HBM per device.

```python
import math
import jax
import jax.numpy as jnp
from jax import lax

LATENT = 256
DEC_HID = 128
LEVCH = 48
MLP_HID = 1024
LAT_DEV = 32
LON_DEV = 128
OBS = 256
GROUPS = 16
VERTICAL_QUANTA = 768
LAT = 128
LON = 256
N_LAT = 4
N_LON = 2


def set_ends(drawn, rng, least, high):
    index_at = [jax.random.randint(jax.random.fold_in(rng, axis), (), 0, length) for axis, length in enumerate(drawn.shape)]
    longest = drawn.shape.index(max(drawn.shape))
    next_to = index_at[:longest] + [(index_at[longest] + 1) % drawn.shape[longest]] + index_at[longest + 1:]
    return drawn.at[tuple(index_at)].set(least).at[tuple(next_to)].set(high)


def steps_of(own_key, dims, cuts, smallest, high):
    level, own = 1.0, jax.random.fold_in(own_key, 6)
    for dim, blocks in cuts:
        steps = jnp.exp(jax.random.uniform(jax.random.fold_in(own, dim), (blocks,), jnp.float32, smallest / len(cuts), high / len(cuts)))
        level = level * jnp.repeat(steps, dims[dim] // blocks).reshape([-1 if axis == dim else 1 for axis in range(len(dims))])
    return level


def noise(key, extent, spread, limit, split=(), kind=jnp.bfloat16):
    array = spread * jax.random.normal(key, extent, jnp.float32)
    if split:
        array = array * steps_of(key, extent, split, -0.22, 0.18)
    return jnp.clip(array, -limit, limit).astype(kind)


def setup_inputs(seed: int = 0) -> dict:
    streams_of = jax.random.split(jax.random.key(seed), 11)
    return {
        "latent": noise(streams_of[0], (LATENT, LAT, LON), 1.0, 6.0, ((1, 4), (2, 2))),
        "conv_weight": noise(streams_of[1], (GROUPS, DEC_HID, 9, LATENT), (9 * LATENT) ** -0.5, 0.125, ((0, 4),)),
        "mid_weight": noise(streams_of[2], (GROUPS, DEC_HID, DEC_HID), DEC_HID ** -0.5, 0.5, ((0, 4),)),
        "out_weight": noise(streams_of[3], (GROUPS, LEVCH, DEC_HID), DEC_HID ** -0.5, 0.5, ((0, 4),)),
        "vertical_inner_matrix": noise(streams_of[4], (MLP_HID, VERTICAL_QUANTA), VERTICAL_QUANTA ** -0.5, 0.21875),
        "vertical_outer_matrix": noise(streams_of[5], (VERTICAL_QUANTA, MLP_HID), MLP_HID ** -0.5, 0.1875),
        "obs_values": noise(streams_of[6], (N_LAT, N_LON, OBS, VERTICAL_QUANTA), 1.0, 6.0, ((0, 4), (1, 2)), jnp.float32),
        "obs_weight": jnp.clip(jnp.exp(jax.random.uniform(streams_of[7], (VERTICAL_QUANTA,), jnp.float32, math.log(0.25), math.log(4.0))), 0.25, 4.0),
        "obs_index": set_ends(jax.random.randint(streams_of[8], (N_LAT, N_LON, OBS), 0, LAT_DEV * LON_DEV), jax.random.fold_in(streams_of[8], 1), 0, (LAT_DEV * LON_DEV) - 1).astype(jnp.int32),
        "obs_count": set_ends(jax.random.randint(streams_of[9], (N_LAT, N_LON), OBS // 4, OBS + 1), jax.random.fold_in(streams_of[9], 1), OBS // 4, OBS).astype(jnp.int32),
    }


KAPPA = 0.7978845608028654
CUBIC = 0.044715


def gelu_slope(pre):
    tanh_v = jnp.tanh(KAPPA * (pre + CUBIC * pre * pre * pre))
    value = 0.5 * pre * (1.0 + tanh_v)
    slope = 0.5 * (1.0 + tanh_v) + 0.5 * pre * (1.0 - tanh_v * tanh_v) * KAPPA * (1.0 + 3.0 * CUBIC * pre * pre)
    return value, slope


def extend(field):
    wrapped = jnp.concatenate([field[..., -1:], field, field[..., :1]], -1)
    zero_fill = jnp.zeros(wrapped.shape[:-2] + (1, wrapped.shape[-1]), wrapped.dtype)
    return jnp.concatenate([zero_fill, wrapped, zero_fill], -2)


def reference(latent, conv_weight, mid_weight, out_weight, vertical_inner_matrix, vertical_outer_matrix, obs_values, obs_weight, obs_index, obs_count):
    objective_amount = LAT * LON
    padded = extend(latent)
    stacked = jnp.stack([padded[:, a:a + LAT, b:b + LON] for a in range(3) for b in range(3)], 0).reshape(9 * LATENT, objective_amount)

    def forward(weights):
        kernel, middle, outer = weights
        pre_one = jnp.dot(kernel.reshape(DEC_HID, 9 * LATENT), stacked, preferred_element_type=jnp.float32)
        act_one, slope_one = gelu_slope(pre_one)
        pre_two = jnp.dot(middle, act_one.astype(jnp.bfloat16), preferred_element_type=jnp.float32)
        act_two, slope_two = gelu_slope(pre_two)
        decoded_layers = jnp.dot(outer, act_two.astype(jnp.bfloat16), preferred_element_type=jnp.float32).astype(jnp.bfloat16)
        return decoded_layers, slope_one, slope_two

    decoded_layers = lax.map(lambda w: forward(w)[0], (conv_weight, mid_weight, out_weight)).reshape(VERTICAL_QUANTA, objective_amount)
    pre_col = jnp.dot(vertical_inner_matrix, decoded_layers, preferred_element_type=jnp.float32)
    vertical_hidden_response, vertical_derivative_factor = gelu_slope(pre_col)
    predicted_vector = decoded_layers.astype(jnp.float32) + jnp.dot(vertical_outer_matrix, vertical_hidden_response.astype(jnp.bfloat16), preferred_element_type=jnp.float32)

    tile_row = lax.broadcasted_iota(jnp.int32, (N_LAT, N_LON, OBS), 0)
    tile_col = lax.broadcasted_iota(jnp.int32, (N_LAT, N_LON, OBS), 1)
    slot = lax.broadcasted_iota(jnp.int32, (N_LAT, N_LON, OBS), 2)
    measurement_sites = ((tile_row * LAT_DEV + obs_index // LON_DEV) * LON + tile_col * LON_DEV + obs_index % LON_DEV).reshape(-1).astype(jnp.int32)
    live = (slot < obs_count[:, :, None]).astype(jnp.float32).reshape(-1)
    measurement_entries = jnp.take(predicted_vector, measurement_sites, axis=1)
    measurement_residual = (measurement_entries - obs_values.reshape(-1, VERTICAL_QUANTA).T) * live[None, :] * obs_weight[:, None]
    prediction_adjoint = jnp.zeros((VERTICAL_QUANTA, objective_amount), jnp.float32).at[:, measurement_sites].add(measurement_residual)

    hidden_response_adjoint = (jnp.dot(vertical_outer_matrix.T, prediction_adjoint.astype(jnp.bfloat16), preferred_element_type=jnp.float32) * vertical_derivative_factor).astype(jnp.bfloat16)
    gridded_adjoint = (prediction_adjoint + jnp.dot(vertical_inner_matrix.T, hidden_response_adjoint, preferred_element_type=jnp.float32)).astype(jnp.bfloat16)
    grad_groups = gridded_adjoint.reshape(GROUPS, LEVCH, objective_amount)

    def backward(carry, items):
        kernel, middle, outer, grad_f = items
        fields_g, slope_one, slope_two = forward((kernel, middle, outer))
        grad_two = (jnp.dot(outer.T, grad_f, preferred_element_type=jnp.float32) * slope_two).astype(jnp.bfloat16)
        grad_one = (jnp.dot(middle.T, grad_two, preferred_element_type=jnp.float32) * slope_one).astype(jnp.bfloat16)
        rim = extend(grad_one.reshape(DEC_HID, LAT, LON))
        taps = jnp.stack([rim[:, 2 - a:2 - a + LAT, 2 - b:2 - b + LON] for a in range(3) for b in range(3)], 1).reshape(DEC_HID, 9, objective_amount)
        term = jnp.einsum("okc,okp->cp", kernel.astype(jnp.float32), taps.astype(jnp.float32))
        return carry + term, None

    summed, _ = lax.scan(backward, jnp.zeros((LATENT, objective_amount), jnp.float32), (conv_weight, mid_weight, out_weight, grad_groups))
    return (latent.astype(jnp.float32).reshape(LATENT, objective_amount) + summed).reshape(LATENT, LAT, LON)
```

```python
import functools

import jax
import jax.numpy as jnp
from jax import lax
from jax.experimental import pallas as pl
from jax.experimental.pallas import tpu as pltpu
from jax.sharding import PartitionSpec as P

KAPPA = 0.7978845608028654
CUBIC = 0.044715
F32 = jnp.float32
BF16 = jnp.bfloat16


def gelu(pre):
    tanh_v = jnp.tanh(KAPPA * (pre + CUBIC * pre * pre * pre))
    return 0.5 * pre * (1.0 + tanh_v)


def gelu_slope(pre):
    square = pre * pre
    tanh_v = jnp.tanh(KAPPA * (pre + CUBIC * square * pre))
    value = 0.5 * pre * (1.0 + tanh_v)
    slope = 0.5 * (1.0 + tanh_v) + 0.5 * pre * (1.0 - tanh_v * tanh_v) * KAPPA * (
        1.0 + 3.0 * CUBIC * square
    )
    return value, slope


def nn(a, b):
    return lax.dot_general(a, b, (((1,), (0,)), ((), ())), preferred_element_type=F32)


def nt(a, b):
    return lax.dot_general(a, b, (((1,), (1,)), ((), ())), preferred_element_type=F32)


def tn(a, b):
    return lax.dot_general(a, b, (((0,), (0,)), ((), ())), preferred_element_type=F32)


def call(kernel, out_shape, in_specs, flops, **kwargs):
    bytes_out = sum(s.size * s.dtype.itemsize for s in jax.tree.leaves(out_shape))
    return pl.pallas_call(
        kernel,
        out_shape=out_shape,
        in_specs=in_specs,
        out_specs=jax.tree.map(lambda _: VM, out_shape),
        cost_estimate=pl.CostEstimate(
            flops=flops, bytes_accessed=4 * bytes_out, transcendentals=0
        ),
        **kwargs,
    )


VM = pl.BlockSpec(memory_space=pltpu.VMEM)
SM = pl.BlockSpec(memory_space=pltpu.SMEM)


def own_kernel(idx_ref, table_ref, valid_ref, w_ref, out_ref, x_ref):
    taps, slots = idx_ref.shape

    def body(i, carry):
        base = pl.multiple_of(i * 8, 8)
        for t in range(taps):
            for j in range(8):
                row = idx_ref[t, base + j]
                x_ref[t, pl.ds(base + j, 1), :] = table_ref[pl.ds(row, 1), :]
        return carry

    lax.fori_loop(0, slots // 8, body, 0)
    acc = None
    for t in range(taps):
        x = (x_ref[t] * valid_ref[:, t : t + 1]).astype(BF16)
        part = nt(w_ref[t], x)
        acc = part if acc is None else acc + part
    out_ref[...] = acc


def decode_kernel(
    idx_ref, pre_ref, halo_ref, w_ref, mid_ref, outw_ref, one_ref, two_ref, field_ref
):
    taps, slots = idx_ref.shape
    groups, hidden, _ = mid_ref.shape
    levels = outw_ref.shape[1]
    width = halo_ref.shape[1]
    acc = pre_ref[...]
    cells = lax.broadcasted_iota(jnp.int32, (width, slots), 0)
    for t in range(taps):
        hot = (cells == idx_ref[t : t + 1, :]).astype(F32).astype(BF16)
        x = nn(halo_ref[...], hot).astype(BF16)
        acc = acc + nn(w_ref[t], x)
    one_ref[...] = acc
    act = gelu(acc).astype(BF16)
    for g in range(groups):
        two = nn(mid_ref[g], act[g * hidden : (g + 1) * hidden])
        two_ref[g * hidden : (g + 1) * hidden, :] = two
        field_ref[g * levels : (g + 1) * levels, :] = nn(
            outw_ref[g], gelu(two).astype(BF16)
        ).astype(BF16)


def slope_kernel(one_ref, two_ref, s1_ref, s2_ref):
    s1_ref[...] = gelu_slope(one_ref[...])[1]
    s2_ref[...] = gelu_slope(two_ref[...])[1]


def column_kernel(
    lev_count,
    lev_ref,
    inner_ref,
    inner_own_ref,
    outer_ref,
    obs_ref,
    weight_ref,
    live_ref,
    s1_ref,
    s2_ref,
    w_ref,
    mid_ref,
    outw_ref,
    *rest,
):
    blocks = rest[:lev_count]
    outs = rest[lev_count : 2 * lev_count]
    f_ref, mis_ref, g_ref = rest[2 * lev_count :]
    lev = lev_ref[0]
    own = blocks[0].shape[0]
    for k in range(lev_count):
        at = pl.multiple_of(lax.rem(lev + k, lev_count) * own, 16)
        f_ref[pl.ds(at, own), :] = blocks[k][...]
    pre_col = nn(inner_ref[...], f_ref[...])
    act, slope = gelu_slope(pre_col)
    forecast = f_ref[...].astype(F32) + nn(outer_ref[...], act.astype(BF16))
    misfit = (forecast - obs_ref[...]) * live_ref[...] * weight_ref[...]
    mis_ref[...] = misfit
    grad_act = (tn(outer_ref[...], misfit.astype(BF16)) * slope).astype(BF16)
    mine = mis_ref[pl.ds(pl.multiple_of(lev * own, 16), own), :]
    grad_fields = (mine + nn(inner_own_ref[...], grad_act)).astype(BF16)
    groups, hidden, _ = mid_ref.shape
    levels = outw_ref.shape[1]
    ones = []
    for g in range(groups):
        span = slice(g * hidden, (g + 1) * hidden)
        two = (
            tn(outw_ref[g], grad_fields[g * levels : (g + 1) * levels]) * s2_ref[span, :]
        ).astype(BF16)
        ones.append((tn(mid_ref[g], two) * s1_ref[span, :]).astype(BF16))
    grad_one = jnp.concatenate(ones, 0)
    taps = w_ref.shape[0]
    portion = w_ref.shape[2] // lev_count
    for t in range(taps):
        patch = tn(w_ref[t], grad_one).astype(BF16)
        for d in range(lev_count):
            g_ref[d, t] = patch[d * portion : (d + 1) * portion]
    for k in range(lev_count):
        outs[k][...] = g_ref[lax.rem(lev + k, lev_count)]


def edge_kernel(rows, cols, row_ref, col_ref, rowc_ref, colc_ref, *rest):
    blocks, (sum_ref, rowout_ref, colout_ref) = rest[:-3], rest[-3:]
    total = blocks[0][...].astype(F32)
    for block in blocks[1:]:
        total = total + block[...].astype(F32)
    sum_ref[...] = total
    slots = row_ref.shape[1]
    wide = colout_ref.shape[2]
    row, col, rowc, colc = row_ref[...], col_ref[...], rowc_ref[...], colc_ref[...]
    cells = lax.broadcasted_iota(jnp.int32, (slots, cols), 1)
    lines = lax.broadcasted_iota(jnp.int32, (slots, wide), 1)
    for e, (edge, a) in enumerate(((0, 0), (rows - 1, 2))):
        acc = None
        for b in range(3):
            part = jnp.where(row == edge, total[3 * a + b], 0.0).astype(BF16)
            hot = (colc + (b - 1) == cells).astype(F32).astype(BF16)
            part = nn(part, hot)
            acc = part if acc is None else acc + part
        rowout_ref[e] = acc
    for e, (edge, b) in enumerate(((0, 0), (cols - 1, 2))):
        acc = None
        for a in range(3):
            part = jnp.where(col == edge, total[3 * a + b], 0.0).astype(BF16)
            hot = (rowc + a == lines).astype(F32).astype(BF16)
            part = nn(part, hot)
            acc = part if acc is None else acc + part
        colout_ref[e] = acc


def scatter_kernel(rows, cols, lev_ref, row_ref, colc_ref, sum_ref, own_ref, out_ref):
    slots = row_ref.shape[1]
    portion = out_ref.shape[0]
    cells = lax.broadcasted_iota(jnp.int32, (slots, cols), 1)
    hots = [(colc_ref[...] + (b - 1) == cells).astype(F32).astype(BF16) for b in range(3)]
    lines = lax.broadcasted_iota(jnp.int32, (rows, slots), 0)
    masks = [row_ref[...] + (a - 1) == lines for a in range(3)]
    step = 8
    for c0 in range(0, portion, step):
        acc = None
        for b in range(3):
            parts = []
            for c in range(c0, c0 + step):
                part = jnp.zeros((rows, slots), F32)
                for a in range(3):
                    line = jnp.broadcast_to(sum_ref[3 * a + b, c : c + 1, :], (rows, slots))
                    part = jnp.where(masks[a], line, part)
                parts.append(part.astype(BF16))
            part = nn(jnp.concatenate(parts, 0), hots[b])
            acc = part if acc is None else acc + part
        out_ref[c0 : c0 + step] = (
            acc.reshape(step, rows, cols) + own_ref[c0 : c0 + step].astype(F32)
        )


def shift(x, axis, by, wrap=True):
    size = lax.axis_size(axis)
    pairs = [(i, (i + by) % size) for i in range(size) if wrap or 0 <= i + by < size]
    return lax.ppermute(x, axis, pairs)


def swap_sides(first, last, axis):
    size = lax.axis_size(axis)
    if size == 2:
        both = shift(jnp.stack([first, last]), axis, 1)
        return both[0], both[1]
    return shift(first, axis, -1), shift(last, axis, 1)


def per_device(
    latent,
    conv_weight,
    mid_weight,
    out_weight,
    inner,
    outer,
    obs_values,
    obs_weight,
    obs_index,
    obs_count,
):
    chans, rows, cols = latent.shape
    groups, hidden, taps, _ = conv_weight.shape
    levels = out_weight.shape[1]
    slots = obs_index.shape[-1]
    own = groups * levels
    lev = lax.axis_index("lev")
    lev_count = lax.axis_size("lev")
    lev_arr = lev.reshape(1).astype(jnp.int32)
    portion = chans // lev_count

    above = shift(latent[:, rows - 1, :], "lat", 1, wrap=False)
    below = shift(latent[:, 0, :], "lat", -1, wrap=False)

    def column(at):
        return jnp.concatenate([above[:, at : at + 1], latent[:, :, at], below[:, at : at + 1]], 1)

    right, left = swap_sides(column(0), column(cols - 1), "lon")
    width = -(-(2 * cols + 2 * (rows + 2)) // 128) * 128
    halo = jnp.concatenate(
        [
            above,
            below,
            left,
            right,
            jnp.zeros((chans, width - 2 * cols - 2 * (rows + 2)), latent.dtype),
        ],
        1,
    )

    index = obs_index[0, 0]
    row, col = index // cols, index % cols
    at_row = row[None, :] + jnp.arange(3, dtype=jnp.int32).repeat(3)[:, None] - 1
    at_col = col[None, :] + jnp.tile(jnp.arange(3, dtype=jnp.int32), 3)[:, None] - 1
    in_row = (at_row >= 0) & (at_row < rows)
    in_col = (at_col >= 0) & (at_col < cols)
    inside = in_row & in_col
    cell = jnp.where(inside, at_row * cols + at_col, 0).astype(jnp.int32)
    rim = jnp.where(at_row < 0, at_col, cols + at_col)
    rim = jnp.where(at_col < 0, 2 * cols + at_row + 1, rim)
    rim = jnp.where(at_col >= cols, 2 * cols + rows + 2 + at_row + 1, rim)
    rim = jnp.where(inside, -1, rim).astype(jnp.int32)
    valid = inside.T.astype(F32)
    live = (jnp.arange(slots, dtype=jnp.int32) < obs_count[0, 0]).astype(F32)[None, :]

    table = jnp.transpose(latent, (1, 2, 0)).reshape(rows * cols, chans).astype(F32)
    w = jnp.transpose(conv_weight, (2, 0, 1, 3)).reshape(taps, groups * hidden, chans)
    wide = groups * hidden
    flops = 2 * taps * wide * chans * slots
    pre_own = call(
        own_kernel,
        jax.ShapeDtypeStruct((wide, slots), F32),
        [SM, VM, VM, VM],
        flops * 2,
        scratch_shapes=[pltpu.VMEM((taps, slots, chans), F32)],
    )(cell, table, valid, w)
    act_shape = jax.ShapeDtypeStruct((wide, slots), F32)
    one, two, fields = call(
        decode_kernel,
        (act_shape, act_shape, jax.ShapeDtypeStruct((own, slots), BF16)),
        [VM] * 6,
        flops * 2,
    )(rim, pre_own, halo, w, mid_weight, out_weight)

    blocks = [fields] + [shift(fields, "lev", -k) for k in range(1, lev_count)]
    slope_one, slope_two = call(slope_kernel, (act_shape, act_shape), [VM] * 2, flops)(one, two)

    inner_own = lax.dynamic_slice_in_dim(inner, lev * own, own, 1).T
    patch_shape = jax.ShapeDtypeStruct((taps, portion, slots), BF16)
    patches = call(
        functools.partial(column_kernel, lev_count),
        (patch_shape,) * lev_count,
        [SM] + [VM] * (11 + lev_count),
        flops * 4,
        scratch_shapes=[
            pltpu.VMEM((own * lev_count, slots), BF16),
            pltpu.VMEM((own * lev_count, slots), F32),
            pltpu.VMEM((lev_count, taps, portion, slots), BF16),
        ],
    )(
        lev_arr,
        inner,
        inner_own,
        outer,
        obs_values[0, 0].T,
        obs_weight[:, None],
        live,
        slope_one,
        slope_two,
        w,
        mid_weight,
        out_weight,
        *blocks,
    )
    parts = [patches[0]] + [shift(patches[k], "lev", k) for k in range(1, lev_count)]

    row_l, col_l = row[None, :], col[None, :]
    row_s, col_s = row[:, None], col[:, None]
    total, row_edge, col_edge = call(
        functools.partial(edge_kernel, rows, cols),
        (
            jax.ShapeDtypeStruct((taps, portion, slots), F32),
            jax.ShapeDtypeStruct((2, portion, cols), F32),
            jax.ShapeDtypeStruct((2, portion, 128), F32),
        ),
        [VM] * (4 + lev_count),
        flops // 8,
    )(row_l, col_l, row_s, col_s, *parts)
    mine = lax.dynamic_slice_in_dim(latent, lev * portion, portion, 0)
    result = call(
        functools.partial(scatter_kernel, rows, cols),
        jax.ShapeDtypeStruct((portion, rows, cols), F32),
        [SM] + [VM] * 4,
        flops // 4,
    )(lev_arr, row_l, col_s, total, mine)

    to_last, to_first = swap_sides(
        col_edge[0][:, : rows + 2], col_edge[1][:, : rows + 2], "lon"
    )

    def sides(at):
        return (
            jnp.pad(to_first[:, at : at + 1], ((0, 0), (0, cols - 1)))
            + jnp.pad(to_last[:, at : at + 1], ((0, 0), (cols - 1, 0)))
        )

    to_bottom = shift(row_edge[0] + sides(0), "lat", -1, wrap=False)
    to_top = shift(row_edge[1] + sides(rows + 1), "lat", 1, wrap=False)
    result = result.at[:, :, 0].add(to_first[:, 1 : rows + 1])
    result = result.at[:, :, cols - 1].add(to_last[:, 1 : rows + 1])
    result = result.at[:, 0, :].add(to_top)
    return result.at[:, rows - 1, :].add(to_bottom)


def solution(mesh):
    return jax.shard_map(
        per_device,
        mesh=mesh,
        in_specs=(
            P(None, "lat", "lon"),
            P("lev", None, None, None),
            P("lev", None, None),
            P("lev", None, None),
            P(),
            P(),
            P("lat", "lon", None, None),
            P(),
            P("lat", "lon", None),
            P("lat", "lon"),
        ),
        out_specs=P("lev", "lat", "lon"),
        check_vma=False,
    )
```

```python
import functools

import jax
import jax.numpy as jnp
from jax import lax
from jax.experimental import pallas as pl
from jax.experimental.pallas import tpu as pltpu
from jax.sharding import PartitionSpec as P

KAPPA = 0.7978845608028654
CUBIC = 0.044715
F32 = jnp.float32
BF16 = jnp.bfloat16


def gelu(pre):
    tanh_v = jnp.tanh(KAPPA * (pre + CUBIC * pre * pre * pre))
    return 0.5 * pre * (1.0 + tanh_v)


def gelu_slope(pre):
    square = pre * pre
    tanh_v = jnp.tanh(KAPPA * (pre + CUBIC * square * pre))
    value = 0.5 * pre * (1.0 + tanh_v)
    slope = 0.5 * (1.0 + tanh_v) + 0.5 * pre * (1.0 - tanh_v * tanh_v) * KAPPA * (
        1.0 + 3.0 * CUBIC * square
    )
    return value, slope


def nn(a, b):
    return lax.dot_general(a, b, (((1,), (0,)), ((), ())), preferred_element_type=F32)


def nt(a, b):
    return lax.dot_general(a, b, (((1,), (1,)), ((), ())), preferred_element_type=F32)


def tn(a, b):
    return lax.dot_general(a, b, (((0,), (0,)), ((), ())), preferred_element_type=F32)


def split(index, cols):
    if cols & (cols - 1):
        return index // cols, index % cols
    bits = cols.bit_length() - 1
    return index >> bits, index & (cols - 1)


def hot(mask):
    return mask.astype(F32).astype(BF16)


def upright(index_ref):
    slots = index_ref.shape[1]
    return jnp.broadcast_to(index_ref[...], (128, slots)).T


def call(kernel, out_shape, in_specs, flops, **kwargs):
    bytes_out = sum(s.size * s.dtype.itemsize for s in jax.tree.leaves(out_shape))
    return pl.pallas_call(
        kernel,
        out_shape=out_shape,
        in_specs=in_specs,
        out_specs=jax.tree.map(lambda _: VM, out_shape),
        cost_estimate=pl.CostEstimate(
            flops=flops, bytes_accessed=4 * bytes_out, transcendentals=0
        ),
        **kwargs,
    )


VM = pl.BlockSpec(memory_space=pltpu.VMEM)
SM = pl.BlockSpec(memory_space=pltpu.SMEM)


def strip_kernel(lat_ref, top_ref, bottom_ref, side_ref, wide_ref, keep_ref):
    chans, rows, cols = lat_ref.shape
    wide_ref[...] = lat_ref[...].reshape(chans * rows, cols).astype(F32)
    which = lax.broadcasted_iota(jnp.int32, (8, cols), 0)
    lane = lax.broadcasted_iota(jnp.int32, (8, cols), 1)
    pick = hot(((which == 0) & (lane == 0)) | ((which == 1) & (lane == cols - 1)))
    for r in range(rows):
        line = wide_ref[pl.ds(r, chans, stride=rows), :].astype(BF16)
        ends = nt(pick, line)
        keep_ref[0, r : r + 1, :] = ends[0:1]
        keep_ref[1, r : r + 1, :] = ends[1:2]
        if r == 0:
            top_ref[...] = line.T
        if r == rows - 1:
            bottom_ref[...] = line.T
    side_ref[...] = keep_ref[...].astype(BF16)


def gather_kernel(index_sm, index_ref, lat_ref, out_ref, wide_ref, table_ref, x_ref):
    chans, rows, cols = lat_ref.shape
    slots = index_ref.shape[1]
    halves = chans // 128
    lead = cols + 8
    wide_ref[...] = lat_ref[...].reshape(chans * rows, cols).astype(F32)
    for r in range(rows):
        line = wide_ref[pl.ds(r, chans, stride=rows), :].astype(BF16).T.astype(F32)
        for b in range(3):
            for h in range(halves):
                at = (lead + r * cols - b + 1) * 8 + halves * b + h
                table_ref[pl.ds(at, cols, stride=8), :] = line[:, h * 128 : (h + 1) * 128]

    def body(i, carry):
        for j in range(8):
            s = i * 8 + j
            base = (index_sm[0, s] + (lead - cols)) * 8
            for a in range(3):
                x_ref[a, pl.ds(pl.multiple_of(s * 8, 8), 8), :] = table_ref[
                    pl.ds(pl.multiple_of(base + a * cols * 8, 8), 8), :
                ]
        return carry

    lax.fori_loop(0, slots // 8, body, 0)
    row, col = split(upright(index_ref), cols)
    for a in range(3):
        for b in range(3):
            at_row, at_col = row + (a - 1), col + (b - 1)
            inside = (at_row >= 0) & (at_row < rows) & (at_col >= 0) & (at_col < cols)
            for h in range(halves):
                x = x_ref[a, pl.ds(halves * b + h, slots, stride=8), :]
                out_ref[3 * a + b, :, h * 128 : (h + 1) * 128] = jnp.where(inside, x, 0.0).astype(
                    BF16
                )


def decode_kernel(
    rows,
    cols,
    index_ref,
    x_ref,
    above_ref,
    below_ref,
    left_ref,
    right_ref,
    w_ref,
    mid_ref,
    outw_ref,
    one_ref,
    two_ref,
    field_ref,
    halo_ref,
):
    slots = index_ref.shape[1]
    groups, hidden, _ = mid_ref.shape
    levels = outw_ref.shape[1]
    width = halo_ref.shape[0]
    tall = (width - 2 * cols) // 2
    halo_ref[...] = jnp.zeros_like(halo_ref)
    halo_ref[0:cols, :] = above_ref[...]
    halo_ref[cols : 2 * cols, :] = below_ref[...]
    halo_ref[2 * cols : 2 * cols + rows + 2, :] = left_ref[...]
    halo_ref[2 * cols + tall : 2 * cols + tall + rows + 2, :] = right_ref[...]
    row, col = split(upright(index_ref), cols)
    cells = lax.broadcasted_iota(jnp.int32, (slots, width), 1)
    acc = None
    for a in range(3):
        for b in range(3):
            at_row, at_col = row + (a - 1), col + (b - 1)
            rim = jnp.where(at_row < 0, at_col, jnp.where(at_row >= rows, cols + at_col, -1))
            rim = jnp.where(at_col < 0, 2 * cols + at_row + 1, rim)
            rim = jnp.where(at_col >= cols, 2 * cols + tall + at_row + 1, rim)
            rim = jnp.concatenate([rim] * (width // 128), 1)
            x = x_ref[3 * a + b] + nn(hot(cells == rim), halo_ref[...]).astype(BF16)
            part = nt(w_ref[3 * a + b], x)
            acc = part if acc is None else acc + part
    one_ref[...] = acc
    act = gelu(acc).astype(BF16)
    for g in range(groups):
        two = nn(mid_ref[g], act[g * hidden : (g + 1) * hidden])
        two_ref[g * hidden : (g + 1) * hidden, :] = two
        field_ref[g * levels : (g + 1) * levels, :] = nn(
            outw_ref[g], gelu(two).astype(BF16)
        ).astype(BF16)


def prepare_kernel(
    lev_ref,
    count_ref,
    one_ref,
    two_ref,
    obs_ref,
    weight_ref,
    inner_ref,
    outer_ref,
    s1_ref,
    s2_ref,
    obst_ref,
    scale_ref,
    innert_ref,
    outert_ref,
    turn_ref,
):
    s1_ref[...] = gelu_slope(one_ref[...])[1]
    s2_ref[...] = gelu_slope(two_ref[...])[1]
    obst_ref[...] = obs_ref[...].T
    slots = obs_ref.shape[0]
    levels = weight_ref.shape[1]
    weight = jnp.broadcast_to(weight_ref[...], (128, levels)).T
    live = lax.broadcasted_iota(jnp.int32, (levels, 128), 1)
    for h in range(slots // 128):
        scale_ref[:, h * 128 : (h + 1) * 128] = jnp.where(
            live + h * 128 < count_ref[0, 0], weight, 0.0
        )
    turn_ref[...] = inner_ref[...].T
    own = innert_ref.shape[0]
    innert_ref[...] = turn_ref[pl.ds(pl.multiple_of(lev_ref[0] * own, 16), own), :]
    outert_ref[...] = outer_ref[...].T


def column_kernel(
    lev_count,
    lev_ref,
    inner_ref,
    innert_ref,
    outer_ref,
    outert_ref,
    obst_ref,
    scale_ref,
    s1_ref,
    s2_ref,
    w_ref,
    mid_ref,
    outw_ref,
    *rest,
):
    blocks = rest[:lev_count]
    outs = rest[lev_count : 2 * lev_count]
    f_ref, mis_ref, g_ref = rest[2 * lev_count :]
    lev = lev_ref[0]
    own = blocks[0].shape[0]
    for k in range(lev_count):
        at = pl.multiple_of(lax.rem(lev + k, lev_count) * own, 16)
        f_ref[pl.ds(at, own), :] = blocks[k][...]
    pre_col = nn(inner_ref[...], f_ref[...])
    act, slope = gelu_slope(pre_col)
    forecast = f_ref[...].astype(F32) + nn(outer_ref[...], act.astype(BF16))
    misfit = (forecast - obst_ref[...]) * scale_ref[...]
    mis_ref[...] = misfit
    grad_act = (nn(outert_ref[...], misfit.astype(BF16)) * slope).astype(BF16)
    mine = mis_ref[pl.ds(pl.multiple_of(lev * own, 16), own), :]
    grad_fields = (mine + nn(innert_ref[...], grad_act)).astype(BF16)
    groups, hidden, _ = mid_ref.shape
    levels = outw_ref.shape[1]
    ones = []
    for g in range(groups):
        span = slice(g * hidden, (g + 1) * hidden)
        two = (
            tn(outw_ref[g], grad_fields[g * levels : (g + 1) * levels]) * s2_ref[span, :]
        ).astype(BF16)
        ones.append((tn(mid_ref[g], two) * s1_ref[span, :]).astype(BF16))
    grad_one = jnp.concatenate(ones, 0)
    taps = w_ref.shape[0]
    portion = w_ref.shape[2] // lev_count
    for t in range(taps):
        patch = tn(w_ref[t], grad_one).astype(BF16)
        for d in range(lev_count):
            g_ref[d, t] = patch[d * portion : (d + 1) * portion]
    for k in range(lev_count):
        outs[k][...] = g_ref[lax.rem(lev + k, lev_count)]


def edge_kernel(rows, cols, index_ref, *rest):
    blocks, (rowout_ref, colout_ref) = rest[:-2], rest[-2:]
    row, col = split(index_ref[...], cols)
    rowc, colc = split(upright(index_ref), cols)
    slots = row.shape[1]
    cells = lax.broadcasted_iota(jnp.int32, (slots, cols), 1)
    lines = lax.broadcasted_iota(jnp.int32, (slots, 128), 1)
    for k, block in enumerate(blocks):
        for e, (edge, a) in enumerate(((0, 0), (rows - 1, 2))):
            acc = None
            for b in range(3):
                part = jnp.where(row == edge, block[3 * a + b].astype(F32), 0.0).astype(BF16)
                part = nn(part, hot(colc + (b - 1) == cells))
                acc = part if acc is None else acc + part
            rowout_ref[e, k] = acc.astype(BF16)
        acc = None
        for e, (edge, b) in enumerate(((0, 0), (cols - 1, 2))):
            for a in range(3):
                part = jnp.where(col == edge, block[3 * a + b].astype(F32), 0.0).astype(BF16)
                part = nn(part, hot(rowc + (a + 64 * e) == lines))
                acc = part if acc is None else acc + part
        colout_ref[k] = acc.astype(BF16)


def corner_kernel(rows, cols, rowin_ref, left_ref, right_ref, up_ref, down_ref, side_ref):
    from_left = left_ref[...].astype(F32)
    from_right = right_ref[...].astype(F32)
    lane = lax.broadcasted_iota(jnp.int32, up_ref.shape, 2)
    for e, (at, ref) in enumerate(((0, up_ref), (rows + 1, down_ref))):
        line = rowin_ref[e].astype(F32)
        line = line + jnp.where(lane == 0, from_left[:, :, 64 + at : 65 + at], 0.0)
        line = line + jnp.where(lane == cols - 1, from_right[:, :, at : at + 1], 0.0)
        ref[...] = line.astype(BF16)
    spot = lax.broadcasted_iota(jnp.int32, side_ref.shape, 2)
    side_ref[...] = jnp.where(spot < 64, right_ref[...].astype(F32), left_ref[...].astype(F32)).astype(BF16)


def final_kernel(rows, cols, count, index_ref, own_ref, *rest):
    blocks, edges, (out_ref, sum_ref, edge_ref) = rest[:count], rest[count:-3], rest[-3:]
    total = blocks[0][...].astype(F32)
    for block in blocks[1:]:
        total = total + block[...].astype(F32)
    sum_ref[...] = total
    total = edges[0][...].astype(F32)
    for edge in edges[1:]:
        total = total + edge[...].astype(F32)
    edge_ref[...] = total
    row, _ = split(index_ref[...], cols)
    _, colc = split(upright(index_ref), cols)
    slots = row.shape[1]
    portion = out_ref.shape[0]
    cells = lax.broadcasted_iota(jnp.int32, (slots, cols), 1)
    hots = [hot(colc + (b - 1) == cells) for b in range(3)]
    lines = lax.broadcasted_iota(jnp.int32, (rows, slots), 0)
    masks = [row + (a - 1) == lines for a in range(3)]
    spot = lax.broadcasted_iota(jnp.int32, (rows, 128), 1)
    line = lax.broadcasted_iota(jnp.int32, (rows, 128), 0)
    picks = [spot == line + 1, spot == line + 65]
    lane = lax.broadcasted_iota(jnp.int32, (rows, cols), 1)
    high = lax.broadcasted_iota(jnp.int32, (rows, cols), 0)
    step = 8
    for c0 in range(0, portion, step):
        acc = None
        for b in range(3):
            parts = []
            for c in range(c0, c0 + step):
                part = jnp.zeros((rows, slots), F32)
                for a in range(3):
                    values = jnp.broadcast_to(sum_ref[3 * a + b, c : c + 1, :], (rows, slots))
                    part = jnp.where(masks[a], values, part)
                parts.append(part.astype(BF16))
            part = nn(jnp.concatenate(parts, 0), hots[b])
            acc = part if acc is None else acc + part
        for c in range(c0, c0 + step):
            field = acc[(c - c0) * rows : (c - c0 + 1) * rows] + own_ref[c].astype(F32)
            above = jnp.broadcast_to(edge_ref[0, c : c + 1, :], (rows, cols))
            below = jnp.broadcast_to(edge_ref[1, c : c + 1, :], (rows, cols))
            side = jnp.broadcast_to(edge_ref[2, c : c + 1, :], (rows, 128))
            last = jnp.sum(jnp.where(picks[0], side, 0.0), 1, keepdims=True)
            first = jnp.sum(jnp.where(picks[1], side, 0.0), 1, keepdims=True)
            field = field + jnp.where(high == 0, above, 0.0)
            field = field + jnp.where(high == rows - 1, below, 0.0)
            field = field + jnp.where(lane == 0, first, 0.0)
            out_ref[c] = field + jnp.where(lane == cols - 1, last, 0.0)


def shift(x, axis, by, wrap=True):
    size = lax.axis_size(axis)
    pairs = [(i, (i + by) % size) for i in range(size) if wrap or 0 <= i + by < size]
    return lax.ppermute(x, axis, pairs)


def from_sides(x, axis):
    if lax.axis_size(axis) == 2:
        other = shift(x, axis, 1)
        return other, other
    return shift(x, axis, 1), shift(x, axis, -1)


def per_device(
    latent,
    conv_weight,
    mid_weight,
    out_weight,
    inner,
    outer,
    obs_values,
    obs_weight,
    obs_index,
    obs_count,
):
    chans, rows, cols = latent.shape
    groups, hidden, taps, _ = conv_weight.shape
    levels = out_weight.shape[1]
    slots = obs_index.shape[-1]
    own = groups * levels
    wide = groups * hidden
    lev = lax.axis_index("lev")
    lev_count = lax.axis_size("lev")
    lev_arr = lev.reshape(1).astype(jnp.int32)
    portion = chans // lev_count
    index = obs_index.reshape(1, slots)
    flops = 2 * taps * wide * chans * slots

    strip = jax.ShapeDtypeStruct((cols, chans), BF16)
    top, bottom, ends = call(
        strip_kernel,
        (strip, strip, jax.ShapeDtypeStruct((2, rows, chans), BF16)),
        [VM],
        flops // 4,
        scratch_shapes=[
            pltpu.VMEM((chans * rows, cols), F32),
            pltpu.VMEM((2, rows, chans), F32),
        ],
    )(latent)
    above = shift(bottom, "lat", 1, wrap=False)
    below = shift(top, "lat", -1, wrap=False)
    columns = jnp.stack(
        [
            jnp.concatenate([above[at : at + 1], ends[e], below[at : at + 1]], 0)
            for e, at in enumerate((0, cols - 1))
        ]
    )
    from_left, from_right = from_sides(columns, "lon")

    x = call(
        gather_kernel,
        jax.ShapeDtypeStruct((taps, slots, chans), BF16),
        [SM, VM, VM],
        flops,
        scratch_shapes=[
            pltpu.VMEM((chans * rows, cols), F32),
            pltpu.VMEM((((rows + 2) * cols + 16) * 8, 128), F32),
            pltpu.VMEM((3, slots * 8, 128), F32),
        ],
    )(index, index, latent)
    w = jnp.transpose(conv_weight, (2, 0, 1, 3)).reshape(taps, wide, chans)
    act_shape = jax.ShapeDtypeStruct((wide, slots), F32)
    one, two, fields = call(
        functools.partial(decode_kernel, rows, cols),
        (act_shape, act_shape, jax.ShapeDtypeStruct((own, slots), BF16)),
        [VM] * 9,
        flops * 2,
        scratch_shapes=[pltpu.VMEM((2 * cols + 128, chans), BF16)],
    )(index, x, above, below, from_left[1], from_right[0], w, mid_weight, out_weight)

    blocks = [fields] + [shift(fields, "lev", -k) for k in range(1, lev_count)]
    column_shape = jax.ShapeDtypeStruct((own * lev_count, slots), F32)
    turned = call(
        prepare_kernel,
        (
            act_shape,
            act_shape,
            column_shape,
            column_shape,
            jax.ShapeDtypeStruct((own, inner.shape[0]), BF16),
            jax.ShapeDtypeStruct((outer.shape[1], outer.shape[0]), BF16),
        ),
        [SM, SM] + [VM] * 6,
        flops,
        scratch_shapes=[pltpu.VMEM((inner.shape[1], inner.shape[0]), BF16)],
    )(lev_arr, obs_count, one, two, obs_values[0, 0], obs_weight[None, :], inner, outer)
    slope_one, slope_two, obs_turned, scale, inner_turned, outer_turned = turned

    patch_shape = jax.ShapeDtypeStruct((taps, portion, slots), BF16)
    patches = call(
        functools.partial(column_kernel, lev_count),
        (patch_shape,) * lev_count,
        [SM] + [VM] * (11 + lev_count),
        flops * 4,
        scratch_shapes=[
            pltpu.VMEM((own * lev_count, slots), BF16),
            pltpu.VMEM((own * lev_count, slots), F32),
            pltpu.VMEM((lev_count, taps, portion, slots), BF16),
        ],
    )(
        lev_arr,
        inner,
        inner_turned,
        outer,
        outer_turned,
        obs_turned,
        scale,
        slope_one,
        slope_two,
        w,
        mid_weight,
        out_weight,
        *blocks,
    )
    parts = [patches[0]] + [shift(patches[k], "lev", k) for k in range(1, lev_count)]

    line_shape = jax.ShapeDtypeStruct((lev_count, portion, cols), BF16)
    side_shape = jax.ShapeDtypeStruct((lev_count, portion, 128), BF16)
    row_edge, col_edge = call(
        functools.partial(edge_kernel, rows, cols),
        (jax.ShapeDtypeStruct((2, lev_count, portion, cols), BF16), side_shape),
        [VM] * (1 + lev_count),
        flops // 8,
    )(index, *patches)
    from_left, from_right = from_sides(col_edge, "lon")
    up, down, side = call(
        functools.partial(corner_kernel, rows, cols),
        (line_shape, line_shape, side_shape),
        [VM] * 3,
        flops // 64,
    )(row_edge, from_left, from_right)
    onto_first = shift(down, "lat", 1, wrap=False)
    onto_last = shift(up, "lat", -1, wrap=False)
    rims = [jnp.stack([onto_first[k], onto_last[k], side[k]]) for k in range(lev_count)]
    rims = [rims[0]] + [shift(rims[k], "lev", k) for k in range(1, lev_count)]

    mine = lax.dynamic_slice_in_dim(latent, lev * portion, portion, 0)
    return call(
        functools.partial(final_kernel, rows, cols, lev_count),
        jax.ShapeDtypeStruct((portion, rows, cols), F32),
        [VM] * (2 + 2 * lev_count),
        flops // 4,
        scratch_shapes=[
            pltpu.VMEM((taps, portion, slots), F32),
            pltpu.VMEM((3, portion, 128), F32),
        ],
    )(index, mine, *parts, *rims)


def solution(mesh):
    return jax.shard_map(
        per_device,
        mesh=mesh,
        in_specs=(
            P(None, "lat", "lon"),
            P("lev", None, None, None),
            P("lev", None, None),
            P("lev", None, None),
            P(),
            P(),
            P("lat", "lon", None, None),
            P(),
            P("lat", "lon", None),
            P("lat", "lon"),
        ),
        out_specs=P("lev", "lat", "lon"),
        check_vma=False,
    )
```

```python
import functools

import jax
import jax.numpy as jnp
from jax import lax
from jax.experimental import pallas as pl
from jax.experimental.pallas import tpu as pltpu
from jax.sharding import PartitionSpec as P

KAPPA = 0.7978845608028654
CUBIC = 0.044715
F32 = jnp.float32
BF16 = jnp.bfloat16


def gelu(pre):
    tanh_v = jnp.tanh(KAPPA * (pre + CUBIC * pre * pre * pre))
    return 0.5 * pre * (1.0 + tanh_v)


def gelu_slope(pre):
    square = pre * pre
    tanh_v = jnp.tanh(KAPPA * (pre + CUBIC * square * pre))
    value = 0.5 * pre * (1.0 + tanh_v)
    slope = 0.5 * (1.0 + tanh_v) + 0.5 * pre * (1.0 - tanh_v * tanh_v) * KAPPA * (
        1.0 + 3.0 * CUBIC * square
    )
    return value, slope


def nn(a, b):
    return lax.dot_general(a, b, (((1,), (0,)), ((), ())), preferred_element_type=F32)


def nt(a, b):
    return lax.dot_general(a, b, (((1,), (1,)), ((), ())), preferred_element_type=F32)


def tn(a, b):
    return lax.dot_general(a, b, (((0,), (0,)), ((), ())), preferred_element_type=F32)


def split(index, cols):
    if cols & (cols - 1):
        return index // cols, index % cols
    bits = cols.bit_length() - 1
    return index >> bits, index & (cols - 1)


def hot(mask):
    return mask.astype(F32).astype(BF16)


def upright(index_ref):
    slots = index_ref.shape[1]
    return jnp.broadcast_to(index_ref[...], (128, slots)).T


def call(kernel, out_shape, in_specs, flops, mib, **kwargs):
    bytes_out = sum(s.size * s.dtype.itemsize for s in jax.tree.leaves(out_shape))
    return pl.pallas_call(
        kernel,
        out_shape=out_shape,
        in_specs=in_specs,
        out_specs=jax.tree.map(lambda _: VM, out_shape),
        cost_estimate=pl.CostEstimate(
            flops=flops, bytes_accessed=4 * bytes_out, transcendentals=0
        ),
        compiler_params=pltpu.CompilerParams(vmem_limit_bytes=mib << 20),
        **kwargs,
    )


EARLY = 5

VM = pl.BlockSpec(memory_space=pltpu.VMEM)
SM = pl.BlockSpec(memory_space=pltpu.SMEM)
ANY = pl.BlockSpec(memory_space=pl.ANY)


def turn_kernel(lat_ref, tile_ref, top_ref, bottom_ref, side_ref, wide_ref, keep_ref):
    chans, rows, cols = lat_ref.shape
    wide_ref[...] = lat_ref[...].reshape(chans * rows, cols).astype(F32)
    for r in range(rows):
        line = wide_ref[pl.ds(r, chans, stride=rows), :].astype(BF16).T
        tile_ref[r * cols : (r + 1) * cols, :] = line
        keep_ref[0, r : r + 1, :] = line[0:1].astype(F32)
        keep_ref[1, r : r + 1, :] = line[cols - 1 : cols].astype(F32)
        if r == 0:
            top_ref[...] = line
        if r == rows - 1:
            bottom_ref[...] = line
    side_ref[...] = keep_ref[...].astype(BF16)


def gather_kernel(rows, cols, index_sm, index_ref, tile_ref, out_ref, table_ref, x_ref):
    chans = tile_ref.shape[1]
    slots = index_ref.shape[1]
    halves = chans // 128
    lead = cols + 8
    for r in range(rows):
        line = tile_ref[r * cols : (r + 1) * cols, :].astype(F32)
        for b in range(3):
            for h in range(halves):
                at = (lead + r * cols - b + 1) * 8 + halves * b + h
                table_ref[pl.ds(at, cols, stride=8), :] = line[:, h * 128 : (h + 1) * 128]

    def body(i, carry):
        for j in range(8):
            s = i * 8 + j
            base = (index_sm[0, s] + (lead - cols)) * 8
            for a in range(3):
                x_ref[a, pl.ds(pl.multiple_of(s * 8, 8), 8), :] = table_ref[
                    pl.ds(pl.multiple_of(base + a * cols * 8, 8), 8), :
                ]
        return carry

    lax.fori_loop(0, slots // 8, body, 0)
    row, col = split(upright(index_ref), cols)
    for a in range(3):
        for b in range(3):
            at_row, at_col = row + (a - 1), col + (b - 1)
            inside = (at_row >= 0) & (at_row < rows) & (at_col >= 0) & (at_col < cols)
            for h in range(halves):
                x = x_ref[a, pl.ds(halves * b + h, slots, stride=8), :]
                out_ref[3 * a + b, :, h * 128 : (h + 1) * 128] = jnp.where(inside, x, 0.0).astype(
                    BF16
                )


def decode_kernel(
    rows,
    cols,
    index_ref,
    x_ref,
    above_ref,
    below_ref,
    left_ref,
    right_ref,
    w_ref,
    mid_ref,
    outw_ref,
    one_ref,
    two_ref,
    field_ref,
    halo_ref,
):
    slots = index_ref.shape[1]
    groups, hidden, _ = mid_ref.shape
    levels = outw_ref.shape[1]
    width = halo_ref.shape[0]
    tall = (width - 2 * cols) // 2
    halo_ref[...] = jnp.zeros_like(halo_ref)
    halo_ref[0:cols, :] = above_ref[...]
    halo_ref[cols : 2 * cols, :] = below_ref[...]
    halo_ref[2 * cols : 2 * cols + rows + 2, :] = left_ref[1]
    halo_ref[2 * cols + tall : 2 * cols + tall + rows + 2, :] = right_ref[0]
    row, col = split(upright(index_ref), cols)
    cells = lax.broadcasted_iota(jnp.int32, (slots, width), 1)
    acc = None
    for a in range(3):
        for b in range(3):
            at_row, at_col = row + (a - 1), col + (b - 1)
            rim = jnp.where(at_row < 0, at_col, jnp.where(at_row >= rows, cols + at_col, -1))
            rim = jnp.where(at_col < 0, 2 * cols + at_row + 1, rim)
            rim = jnp.where(at_col >= cols, 2 * cols + tall + at_row + 1, rim)
            rim = jnp.concatenate([rim] * (width // 128), 1)
            x = x_ref[3 * a + b] + nn(hot(cells == rim), halo_ref[...]).astype(BF16)
            part = nt(w_ref[3 * a + b], x)
            acc = part if acc is None else acc + part
    one_ref[...] = acc
    act = gelu(acc).astype(BF16)
    for g in range(groups):
        two = nn(mid_ref[g], act[g * hidden : (g + 1) * hidden])
        two_ref[g * hidden : (g + 1) * hidden, :] = two
        field_ref[g * levels : (g + 1) * levels, :] = nn(
            outw_ref[g], gelu(two).astype(BF16)
        ).astype(BF16)


def prepare_kernel(
    lev_ref,
    count_ref,
    one_ref,
    two_ref,
    obs_ref,
    weight_ref,
    inner_ref,
    outer_ref,
    s1_ref,
    s2_ref,
    obst_ref,
    scale_ref,
    innert_ref,
    outert_ref,
    turn_ref,
):
    s1_ref[...] = gelu_slope(one_ref[...])[1]
    s2_ref[...] = gelu_slope(two_ref[...])[1]
    obst_ref[...] = obs_ref[...].T
    slots = obs_ref.shape[0]
    levels = weight_ref.shape[1]
    weight = jnp.broadcast_to(weight_ref[...], (128, levels)).T
    live = lax.broadcasted_iota(jnp.int32, (levels, 128), 1)
    for h in range(slots // 128):
        scale_ref[:, h * 128 : (h + 1) * 128] = jnp.where(
            live + h * 128 < count_ref[0, 0], weight, 0.0
        )
    turn_ref[...] = inner_ref[...].T
    own = innert_ref.shape[0]
    innert_ref[...] = turn_ref[pl.ds(pl.multiple_of(lev_ref[0] * own, 16), own), :]
    outert_ref[...] = outer_ref[...].T


def column_kernel(
    lev_count,
    lev_ref,
    inner_ref,
    innert_ref,
    outer_ref,
    outert_ref,
    obst_ref,
    scale_ref,
    s1_ref,
    s2_ref,
    w_ref,
    mid_ref,
    outw_ref,
    *rest,
):
    blocks = rest[:lev_count]
    early = rest[lev_count : 2 * lev_count]
    late = rest[2 * lev_count : 3 * lev_count]
    f_ref, mis_ref, g_ref = rest[3 * lev_count :]
    lev = lev_ref[0]
    own = blocks[0].shape[0]
    for k in range(lev_count):
        at = pl.multiple_of(lax.rem(lev + k, lev_count) * own, 16)
        f_ref[pl.ds(at, own), :] = blocks[k][...]
    pre_col = nn(inner_ref[...], f_ref[...])
    act, slope = gelu_slope(pre_col)
    forecast = f_ref[...].astype(F32) + nn(outer_ref[...], act.astype(BF16))
    misfit = (forecast - obst_ref[...]) * scale_ref[...]
    mis_ref[...] = misfit
    grad_act = (nn(outert_ref[...], misfit.astype(BF16)) * slope).astype(BF16)
    mine = mis_ref[pl.ds(pl.multiple_of(lev * own, 16), own), :]
    grad_fields = (mine + nn(innert_ref[...], grad_act)).astype(BF16)
    groups, hidden, _ = mid_ref.shape
    levels = outw_ref.shape[1]
    ones = []
    for g in range(groups):
        span = slice(g * hidden, (g + 1) * hidden)
        two = (
            tn(outw_ref[g], grad_fields[g * levels : (g + 1) * levels]) * s2_ref[span, :]
        ).astype(BF16)
        ones.append((tn(mid_ref[g], two) * s1_ref[span, :]).astype(BF16))
    grad_one = jnp.concatenate(ones, 0)
    taps = w_ref.shape[0]
    portion = w_ref.shape[2] // lev_count
    for t in range(taps):
        patch = tn(w_ref[t], grad_one).astype(BF16)
        for d in range(lev_count):
            g_ref[d, t] = patch[d * portion : (d + 1) * portion]
    for k in range(lev_count):
        to = lax.rem(lev + k, lev_count)
        early[k][...] = g_ref[to, 0:EARLY]
        late[k][...] = g_ref[to, EARLY:taps]


def edge_kernel(rows, cols, index_ref, *rest):
    blocks, (rowout_ref, colout_ref) = rest[:-2], rest[-2:]
    half = len(blocks) // 2
    row, col = split(index_ref[...], cols)
    rowc, colc = split(upright(index_ref), cols)
    slots = row.shape[1]
    cells = lax.broadcasted_iota(jnp.int32, (slots, cols), 1)
    lines = lax.broadcasted_iota(jnp.int32, (slots, 128), 1)
    for k in range(half):
        block = [blocks[k].at[t] for t in range(EARLY)]
        block += [blocks[half + k].at[t] for t in range(9 - EARLY)]
        for e, (edge, a) in enumerate(((0, 0), (rows - 1, 2))):
            acc = None
            for b in range(3):
                part = jnp.where(row == edge, block[3 * a + b][...].astype(F32), 0.0).astype(BF16)
                part = nn(part, hot(colc + (b - 1) == cells))
                acc = part if acc is None else acc + part
            rowout_ref[e, k] = acc.astype(BF16)
        acc = None
        for e, (edge, b) in enumerate(((0, 0), (cols - 1, 2))):
            for a in range(3):
                part = jnp.where(col == edge, block[3 * a + b][...].astype(F32), 0.0).astype(BF16)
                part = nn(part, hot(rowc + (a + 64 * e) == lines))
                acc = part if acc is None else acc + part
        colout_ref[k] = acc.astype(BF16)


def corner_kernel(rows, cols, rowin_ref, left_ref, right_ref, up_ref, down_ref):
    lane = lax.broadcasted_iota(jnp.int32, up_ref.shape, 2)
    for e, (at, ref) in enumerate(((0, up_ref), (rows + 1, down_ref))):
        line = rowin_ref[e].astype(F32)
        line = line + jnp.where(lane == 0, left_ref[:, :, 64 + at : 65 + at].astype(F32), 0.0)
        line = line + jnp.where(
            lane == cols - 1, right_ref[:, :, at : at + 1].astype(F32), 0.0
        )
        ref[...] = line.astype(BF16)


def join_kernel(count, *refs):
    late, (top_ref, bottom_ref, left_ref, right_ref) = refs[:count], refs[count : count + 4]
    outs = refs[count + 4 :]
    taps, portion, _ = late[0].shape
    spot = lax.broadcasted_iota(jnp.int32, (portion, 128), 1)
    for k in range(count):
        outs[k][0:taps] = late[k][...]
        outs[k][taps, :, 0:128] = top_ref[k]
        outs[k][taps, :, 128:256] = bottom_ref[k]
        side = jnp.where(spot < 64, right_ref[k].astype(F32), left_ref[k].astype(F32))
        outs[k][taps + 1, :, 0:128] = side.astype(BF16)
        outs[k][taps + 1, :, 128:256] = jnp.zeros_like(top_ref[k])


def final_kernel(rows, cols, count, lev_ref, index_ref, latent_ref, *rest):
    early, late = rest[:count], rest[count : 2 * count]
    out_ref, own_ref, sum_ref, edge_ref, sem = rest[2 * count :]
    portion = out_ref.shape[0]
    fetch = pltpu.make_async_copy(
        latent_ref.at[pl.ds(pl.multiple_of(lev_ref[0] * portion, 8), portion)], own_ref, sem
    )
    fetch.start()
    total = early[0][...].astype(F32)
    for block in early[1:]:
        total = total + block[...].astype(F32)
    sum_ref[0:EARLY] = total
    total = late[0][...].astype(F32)
    for block in late[1:]:
        total = total + block[...].astype(F32)
    sum_ref[EARLY:] = total[: 9 - EARLY]
    edge_ref[0] = total[9 - EARLY, :, 0:128]
    edge_ref[1] = total[9 - EARLY, :, 128:256]
    edge_ref[2] = total[10 - EARLY, :, 0:128]
    fetch.wait()
    row, _ = split(index_ref[...], cols)
    _, colc = split(upright(index_ref), cols)
    slots = row.shape[1]
    cells = lax.broadcasted_iota(jnp.int32, (slots, cols), 1)
    hots = [hot(colc + (b - 1) == cells) for b in range(3)]
    lines = lax.broadcasted_iota(jnp.int32, (rows, slots), 0)
    masks = [row + (a - 1) == lines for a in range(3)]
    spot = lax.broadcasted_iota(jnp.int32, (rows, 128), 1)
    line = lax.broadcasted_iota(jnp.int32, (rows, 128), 0)
    picks = [spot == line + 1, spot == line + 65]
    lane = lax.broadcasted_iota(jnp.int32, (rows, cols), 1)
    high = lax.broadcasted_iota(jnp.int32, (rows, cols), 0)
    step = 8
    for c0 in range(0, portion, step):
        acc = None
        for b in range(3):
            parts = []
            for c in range(c0, c0 + step):
                part = jnp.zeros((rows, slots), F32)
                for a in range(3):
                    values = jnp.broadcast_to(sum_ref[3 * a + b, c : c + 1, :], (rows, slots))
                    part = jnp.where(masks[a], values, part)
                parts.append(part.astype(BF16))
            part = nn(jnp.concatenate(parts, 0), hots[b])
            acc = part if acc is None else acc + part
        for c in range(c0, c0 + step):
            field = acc[(c - c0) * rows : (c - c0 + 1) * rows] + own_ref[c].astype(F32)
            above = jnp.broadcast_to(edge_ref[0, c : c + 1, :], (rows, cols))
            below = jnp.broadcast_to(edge_ref[1, c : c + 1, :], (rows, cols))
            side = jnp.broadcast_to(edge_ref[2, c : c + 1, :], (rows, 128))
            last = jnp.sum(jnp.where(picks[0], side, 0.0), 1, keepdims=True)
            first = jnp.sum(jnp.where(picks[1], side, 0.0), 1, keepdims=True)
            field = field + jnp.where(high == 0, above, 0.0)
            field = field + jnp.where(high == rows - 1, below, 0.0)
            field = field + jnp.where(lane == 0, first, 0.0)
            out_ref[c] = field + jnp.where(lane == cols - 1, last, 0.0)


def shift(x, axis, by, wrap=True):
    size = lax.axis_size(axis)
    pairs = [(i, (i + by) % size) for i in range(size) if wrap or 0 <= i + by < size]
    return lax.ppermute(x, axis, pairs)


def from_sides(x, axis):
    if lax.axis_size(axis) == 2:
        other = shift(x, axis, 1)
        return other, other
    return shift(x, axis, 1), shift(x, axis, -1)


def steps(
    latent,
    conv_weight,
    mid_weight,
    out_weight,
    inner,
    outer,
    obs_values,
    obs_weight,
    obs_index,
    obs_count,
):
    chans, rows, cols = latent.shape
    groups, hidden, taps, _ = conv_weight.shape
    levels = out_weight.shape[1]
    slots = obs_index.shape[-1]
    own = groups * levels
    wide = groups * hidden
    lev = lax.axis_index("lev")
    lev_count = lax.axis_size("lev")
    lev_arr = lev.reshape(1).astype(jnp.int32)
    portion = chans // lev_count
    index = obs_index.reshape(1, slots)
    flops = 2 * taps * wide * chans * slots

    strip = jax.ShapeDtypeStruct((cols, chans), BF16)
    tile, top, bottom, ends = call(
        turn_kernel,
        (
            jax.ShapeDtypeStruct((rows * cols, chans), BF16),
            strip,
            strip,
            jax.ShapeDtypeStruct((2, rows, chans), BF16),
        ),
        [VM],
        flops // 4,
        16,
        scratch_shapes=[
            pltpu.VMEM((chans * rows, cols), F32),
            pltpu.VMEM((2, rows, chans), F32),
        ],
    )(latent)
    above = shift(bottom, "lat", 1, wrap=False)
    below = shift(top, "lat", -1, wrap=False)
    columns = jnp.stack(
        [
            jnp.concatenate([above[at : at + 1], ends[e], below[at : at + 1]], 0)
            for e, at in enumerate((0, cols - 1))
        ]
    )
    from_left, from_right = from_sides(columns, "lon")

    x = call(
        functools.partial(gather_kernel, rows, cols),
        jax.ShapeDtypeStruct((taps, slots, chans), BF16),
        [SM, VM, VM],
        flops,
        40,
        scratch_shapes=[
            pltpu.VMEM((((rows + 2) * cols + 16) * 8, 128), F32),
            pltpu.VMEM((3, slots * 8, 128), F32),
        ],
    )(index, index, tile)
    w = jnp.transpose(conv_weight, (2, 0, 1, 3)).reshape(taps, wide, chans)
    act_shape = jax.ShapeDtypeStruct((wide, slots), F32)
    one, two, fields = call(
        functools.partial(decode_kernel, rows, cols),
        (act_shape, act_shape, jax.ShapeDtypeStruct((own, slots), BF16)),
        [VM] * 9,
        flops * 2,
        20,
        scratch_shapes=[pltpu.VMEM((2 * cols + 128, chans), BF16)],
    )(index, x, above, below, from_left, from_right, w, mid_weight, out_weight)

    blocks = [fields] + [shift(fields, "lev", -k) for k in range(1, lev_count)]
    column_shape = jax.ShapeDtypeStruct((own * lev_count, slots), F32)
    turned = call(
        prepare_kernel,
        (
            act_shape,
            act_shape,
            column_shape,
            column_shape,
            jax.ShapeDtypeStruct((own, inner.shape[0]), BF16),
            jax.ShapeDtypeStruct((outer.shape[1], outer.shape[0]), BF16),
        ),
        [SM, SM] + [VM] * 6,
        flops,
        24,
        scratch_shapes=[pltpu.VMEM((inner.shape[1], inner.shape[0]), BF16)],
    )(lev_arr, obs_count, one, two, obs_values[0, 0], obs_weight[None, :], inner, outer)
    slope_one, slope_two, obs_turned, scale, inner_turned, outer_turned = turned

    early_shape = jax.ShapeDtypeStruct((EARLY, portion, slots), BF16)
    late_shape = jax.ShapeDtypeStruct((taps - EARLY, portion, slots), BF16)
    patches = call(
        functools.partial(column_kernel, lev_count),
        (early_shape,) * lev_count + (late_shape,) * lev_count,
        [SM] + [VM] * (11 + lev_count),
        flops * 4,
        32,
        scratch_shapes=[
            pltpu.VMEM((own * lev_count, slots), BF16),
            pltpu.VMEM((own * lev_count, slots), F32),
            pltpu.VMEM((lev_count, taps, portion, slots), BF16),
        ],
    )(
        lev_arr,
        inner,
        inner_turned,
        outer,
        outer_turned,
        obs_turned,
        scale,
        slope_one,
        slope_two,
        w,
        mid_weight,
        out_weight,
        *blocks,
    )
    early = [patches[0]]
    for k in range(1, lev_count):
        early.append(shift(patches[k], "lev", k))

    line_shape = jax.ShapeDtypeStruct((lev_count, portion, cols), BF16)
    side_shape = jax.ShapeDtypeStruct((lev_count, portion, 128), BF16)
    row_edge, col_edge = call(
        functools.partial(edge_kernel, rows, cols),
        (jax.ShapeDtypeStruct((2, lev_count, portion, cols), BF16), side_shape),
        [VM] * (1 + 2 * lev_count),
        flops // 8,
        12,
    )(index, *patches)
    from_left, from_right = from_sides(col_edge, "lon")
    up, down = call(
        functools.partial(corner_kernel, rows, cols),
        (line_shape, line_shape),
        [VM] * 3,
        flops // 64,
        8,
    )(row_edge, from_left, from_right)
    onto_first = shift(down, "lat", 1, wrap=False)
    onto_last = shift(up, "lat", -1, wrap=False)
    joined = call(
        functools.partial(join_kernel, lev_count),
        (jax.ShapeDtypeStruct((taps - EARLY + 2, portion, slots), BF16),) * lev_count,
        [VM] * (4 + lev_count),
        flops // 64,
        12,
    )(*patches[lev_count:], onto_first, onto_last, from_left, from_right)
    late = [joined[0]] + [shift(joined[k], "lev", k) for k in range(1, lev_count)]

    return call(
        functools.partial(final_kernel, rows, cols, lev_count),
        jax.ShapeDtypeStruct((portion, rows, cols), F32),
        [SM, VM, ANY] + [VM] * (2 * lev_count),
        flops // 4,
        16,
        scratch_shapes=[
            pltpu.VMEM((portion, rows, cols), BF16),
            pltpu.VMEM((taps, portion, slots), F32),
            pltpu.VMEM((3, portion, 128), F32),
            pltpu.SemaphoreType.DMA,
        ],
    )(lev_arr, index, latent, *early, *late)


def solution(mesh):
    return jax.shard_map(
        steps,
        mesh=mesh,
        in_specs=(
            P(None, "lat", "lon"),
            P("lev", None, None, None),
            P("lev", None, None),
            P("lev", None, None),
            P(),
            P(),
            P("lat", "lon", None, None),
            P(),
            P("lat", "lon", None),
            P("lat", "lon"),
        ),
        out_specs=P("lev", "lat", "lon"),
        check_vma=False,
    )
```

```python
import functools

import jax
import jax.numpy as jnp
from jax import lax
from jax.experimental import pallas as pl
from jax.experimental.pallas import tpu as pltpu
from jax.sharding import PartitionSpec as P

KAPPA = 0.7978845608028654
CUBIC = 0.044715
F32 = jnp.float32
BF16 = jnp.bfloat16


def gelu_slope(pre):
    square = pre * pre
    tanh_v = jnp.tanh(KAPPA * (pre + CUBIC * square * pre))
    value = 0.5 * pre * (1.0 + tanh_v)
    slope = 0.5 * (1.0 + tanh_v) + 0.5 * pre * (1.0 - tanh_v * tanh_v) * KAPPA * (
        1.0 + 3.0 * CUBIC * square
    )
    return value, slope


def nn(a, b):
    return lax.dot_general(a, b, (((1,), (0,)), ((), ())), preferred_element_type=F32)


def nt(a, b):
    return lax.dot_general(a, b, (((1,), (1,)), ((), ())), preferred_element_type=F32)


def tn(a, b):
    return lax.dot_general(a, b, (((0,), (0,)), ((), ())), preferred_element_type=F32)


def split(index, cols):
    if cols & (cols - 1):
        return index // cols, index % cols
    bits = cols.bit_length() - 1
    return index >> bits, index & (cols - 1)


def hot(mask):
    return mask.astype(F32).astype(BF16)


def upright(index_ref):
    slots = index_ref.shape[1]
    return jnp.broadcast_to(index_ref[...], (128, slots)).T


def call(kernel, out_shape, in_specs, flops, mib, **kwargs):
    bytes_out = sum(s.size * s.dtype.itemsize for s in jax.tree.leaves(out_shape))
    return pl.pallas_call(
        kernel,
        out_shape=out_shape,
        in_specs=in_specs,
        out_specs=jax.tree.map(lambda _: VM, out_shape),
        cost_estimate=pl.CostEstimate(
            flops=flops, bytes_accessed=4 * bytes_out, transcendentals=0
        ),
        compiler_params=pltpu.CompilerParams(vmem_limit_bytes=mib << 20),
        **kwargs,
    )


LEV, INNER, TO = 0, 1, 2

VM = pl.BlockSpec(memory_space=pltpu.VMEM)
SM = pl.BlockSpec(memory_space=pltpu.SMEM)
HBM = pl.BlockSpec(memory_space=pltpu.MemorySpace.HBM)


def turn_kernel(
    _, lat_ref, tile_ref, top_ref, bottom_ref, side_ref, near_ref, wide_ref, keep_ref, sems
):
    chans, rows, cols = lat_ref.shape
    count = rows // 8
    copies = [
        pltpu.make_async_copy(lat_ref.at[:, pl.ds(8 * i, 8)], near_ref.at[i], sems.at[i])
        for i in range(count)
    ]
    for copy in copies:
        copy.start()
    for i, copy in enumerate(copies):
        copy.wait()
        wide_ref[i] = near_ref[i].reshape(chans * 8, cols).astype(F32)
        for r in range(8 * i, 8 * i + 8):
            line = wide_ref[i, pl.ds(r - 8 * i, chans, stride=8), :].astype(BF16).T
            tile_ref[r * cols : (r + 1) * cols, :] = line
            keep_ref[0, r : r + 1, :] = line[0:1].astype(F32)
            keep_ref[1, r : r + 1, :] = line[cols - 1 : cols].astype(F32)
            if r == 0:
                top_ref[...] = line
            if r == rows - 1:
                bottom_ref[...] = line
    side_ref[...] = keep_ref[...].astype(BF16)


def gather_kernel(rows, cols, index_sm, index_ref, tile_ref, out_ref, table_ref, x_ref):
    chans = tile_ref.shape[1]
    slots = index_ref.shape[1]
    halves = chans // 128
    lead = cols + 8
    for r in range(rows):
        line = tile_ref[r * cols : (r + 1) * cols, :].astype(F32)
        for b in range(3):
            for h in range(halves):
                at = (lead + r * cols - b + 1) * 8 + halves * b + h
                table_ref[pl.ds(at, cols, stride=8), :] = line[:, h * 128 : (h + 1) * 128]

    def body(i, carry):
        for j in range(8):
            s = i * 8 + j
            base = (index_sm[0, s] + (lead - cols)) * 8
            for a in range(3):
                x_ref[a, pl.ds(pl.multiple_of(s * 8, 8), 8), :] = table_ref[
                    pl.ds(pl.multiple_of(base + a * cols * 8, 8), 8), :
                ]
        return carry

    lax.fori_loop(0, slots // 8, body, 0)
    row, col = split(upright(index_ref), cols)
    for a in range(3):
        for b in range(3):
            at_row, at_col = row + (a - 1), col + (b - 1)
            inside = (at_row >= 0) & (at_row < rows) & (at_col >= 0) & (at_col < cols)
            for h in range(halves):
                x = x_ref[a, pl.ds(halves * b + h, slots, stride=8), :]
                out_ref[3 * a + b, :, h * 128 : (h + 1) * 128] = jnp.where(inside, x, 0.0).astype(
                    BF16
                )


def decode_kernel(
    rows,
    cols,
    index_ref,
    x_ref,
    above_ref,
    below_ref,
    left_ref,
    right_ref,
    w_ref,
    mid_ref,
    outw_ref,
    s1_ref,
    s2_ref,
    field_ref,
    halo_ref,
):
    slots = index_ref.shape[1]
    groups, hidden, _ = mid_ref.shape
    levels = outw_ref.shape[1]
    width = halo_ref.shape[0]
    tall = (width - 2 * cols) // 2
    halo_ref[...] = jnp.zeros_like(halo_ref)
    halo_ref[0:cols, :] = above_ref[...]
    halo_ref[cols : 2 * cols, :] = below_ref[...]
    halo_ref[2 * cols : 2 * cols + rows + 2, :] = left_ref[1]
    halo_ref[2 * cols + tall : 2 * cols + tall + rows + 2, :] = right_ref[0]
    row, col = split(upright(index_ref), cols)
    cells = lax.broadcasted_iota(jnp.int32, (slots, width), 1)
    acc = None
    for a in range(3):
        for b in range(3):
            at_row, at_col = row + (a - 1), col + (b - 1)
            rim = jnp.where(at_row < 0, at_col, jnp.where(at_row >= rows, cols + at_col, -1))
            rim = jnp.where(at_col < 0, 2 * cols + at_row + 1, rim)
            rim = jnp.where(at_col >= cols, 2 * cols + tall + at_row + 1, rim)
            rim = jnp.concatenate([rim] * (width // 128), 1)
            x = x_ref[3 * a + b] + nn(hot(cells == rim), halo_ref[...]).astype(BF16)
            part = nt(w_ref[3 * a + b], x)
            acc = part if acc is None else acc + part
    act, slope = gelu_slope(acc)
    s1_ref[...] = slope.astype(BF16)
    act = act.astype(BF16)
    for g in range(groups):
        two = nn(mid_ref[g], act[g * hidden : (g + 1) * hidden])
        value, slope = gelu_slope(two)
        s2_ref[g * hidden : (g + 1) * hidden, :] = slope.astype(BF16)
        field_ref[g * levels : (g + 1) * levels, :] = nn(
            outw_ref[g], value.astype(BF16)
        ).astype(BF16)


def prepare_kernel(
    scal_ref,
    count_ref,
    obs_ref,
    weight_ref,
    inner_ref,
    outer_ref,
    w_ref,
    obst_ref,
    scale_ref,
    innert_ref,
    outert_ref,
    wt_ref,
    turn_ref,
):
    obst_ref[...] = obs_ref[...].T
    slots = obs_ref.shape[0]
    levels = weight_ref.shape[1]
    weight = jnp.broadcast_to(weight_ref[...], (128, levels)).T
    live = lax.broadcasted_iota(jnp.int32, (levels, 128), 1)
    for h in range(slots // 128):
        scale_ref[:, h * 128 : (h + 1) * 128] = jnp.where(
            live + h * 128 < count_ref[0, 0], weight, 0.0
        )
    turn_ref[...] = inner_ref[...].T
    own = innert_ref.shape[0]
    innert_ref[...] = turn_ref[pl.ds(pl.multiple_of(scal_ref[LEV] * own, 16), own), :]
    outert_ref[...] = outer_ref[...].T
    for t in range(w_ref.shape[0]):
        wt_ref[t] = w_ref[t].T


def column_kernel(
    lev_count,
    scal_ref,
    inner_ref,
    innert_ref,
    outer_ref,
    outert_ref,
    obst_ref,
    scale_ref,
    s1_ref,
    s2_ref,
    wt_ref,
    mid_ref,
    outw_ref,
    *rest,
):
    blocks = rest[:lev_count]
    outs = rest[lev_count : 2 * lev_count]
    f_ref, mis_ref, g_ref = rest[2 * lev_count :]
    lev = scal_ref[LEV]
    own = blocks[0].shape[0]
    for k in range(lev_count):
        at = pl.multiple_of(lax.rem(lev + k, lev_count) * own, 16)
        f_ref[pl.ds(at, own), :] = blocks[k][...]
    pre_col = nn(inner_ref[...], f_ref[...])
    act, slope = gelu_slope(pre_col)
    forecast = f_ref[...].astype(F32) + nn(outer_ref[...], act.astype(BF16))
    misfit = (forecast - obst_ref[...]) * scale_ref[...]
    mis_ref[...] = misfit
    grad_act = (nn(outert_ref[...], misfit.astype(BF16)) * slope).astype(BF16)
    mine = mis_ref[pl.ds(pl.multiple_of(lev * own, 16), own), :]
    grad_fields = (mine + nn(innert_ref[...], grad_act)).astype(BF16)
    groups, hidden, _ = mid_ref.shape
    levels = outw_ref.shape[1]
    ones = []
    for g in range(groups):
        span = slice(g * hidden, (g + 1) * hidden)
        two = (
            tn(outw_ref[g], grad_fields[g * levels : (g + 1) * levels]) * s2_ref[span, :].astype(F32)
        ).astype(BF16)
        ones.append((tn(mid_ref[g], two) * s1_ref[span, :].astype(F32)).astype(BF16))
    grad_one = jnp.concatenate(ones, 0)
    taps = wt_ref.shape[0]
    portion = wt_ref.shape[1] // lev_count
    for t in range(taps):
        patch = nn(wt_ref[t], grad_one).astype(BF16)
        for d in range(lev_count):
            g_ref[d, t] = patch[d * portion : (d + 1) * portion]
    for k in range(lev_count):
        outs[k][...] = g_ref[scal_ref[TO + k]]


def edge_kernel(rows, cols, index_ref, *rest):
    blocks, (rowout_ref, colout_ref) = rest[:-2], rest[-2:]
    row, col = split(index_ref[...], cols)
    rowc, colc = split(upright(index_ref), cols)
    slots = row.shape[1]
    cells = lax.broadcasted_iota(jnp.int32, (slots, cols), 1)
    lines = lax.broadcasted_iota(jnp.int32, (slots, 128), 1)
    for k, block in enumerate(blocks):
        for e, (edge, a) in enumerate(((0, 0), (rows - 1, 2))):
            acc = None
            for b in range(3):
                part = jnp.where(row == edge, block[3 * a + b].astype(F32), 0.0).astype(BF16)
                part = nn(part, hot(colc + (b - 1) == cells))
                acc = part if acc is None else acc + part
            rowout_ref[e, k] = acc.astype(BF16)
        acc = None
        for e, (edge, b) in enumerate(((0, 0), (cols - 1, 2))):
            for a in range(3):
                part = jnp.where(col == edge, block[3 * a + b].astype(F32), 0.0).astype(BF16)
                part = nn(part, hot(rowc + (a + 64 * e) == lines))
                acc = part if acc is None else acc + part
        colout_ref[k] = acc.astype(BF16)


def corner_kernel(rows, cols, rowin_ref, left_ref, right_ref, up_ref, down_ref):
    lane = lax.broadcasted_iota(jnp.int32, up_ref.shape, 2)
    for e, (at, ref) in enumerate(((0, up_ref), (rows + 1, down_ref))):
        line = rowin_ref[e].astype(F32)
        line = line + jnp.where(lane == 0, left_ref[:, :, 64 + at : 65 + at].astype(F32), 0.0)
        line = line + jnp.where(
            lane == cols - 1, right_ref[:, :, at : at + 1].astype(F32), 0.0
        )
        ref[...] = line.astype(BF16)


def join_kernel(count, scal_ref, top_ref, bottom_ref, left_ref, right_ref, *outs):
    portion = top_ref.shape[1]
    spot = lax.broadcasted_iota(jnp.int32, (portion, 128), 1)
    for k in range(count):
        at = scal_ref[TO + count + k]
        outs[k][0] = top_ref[at]
        outs[k][1] = bottom_ref[at]
        side = jnp.where(spot < 64, right_ref[at].astype(F32), left_ref[at].astype(F32))
        outs[k][2] = side.astype(BF16)


def relay_kernel(scal_ref, block_ref, got_ref, out_ref):
    keep = jnp.where(scal_ref[INNER] == 1, 1.0, 0.0)
    out_ref[...] = (block_ref[...].astype(F32) + got_ref[...].astype(F32) * keep).astype(BF16)


def final_kernel(rows, cols, count, scal_ref, index_ref, latent_ref, *rest):
    own, relayed, parts = rest[0], rest[1], rest[2:count]
    rims, (out_ref, own_ref, sum_ref, edge_ref, sem) = rest[count:-5], rest[-5:]
    portion = out_ref.shape[0]
    fetch = pltpu.make_async_copy(
        latent_ref.at[pl.ds(pl.multiple_of(scal_ref[LEV] * portion, 8), portion)], own_ref, sem
    )
    fetch.start()
    keep = jnp.where(scal_ref[INNER] == 1, 0.0, 1.0)
    total = own[...].astype(F32) + relayed[...].astype(F32) * keep
    for block in parts:
        total = total + block[...].astype(F32)
    sum_ref[...] = total
    total = rims[0][...].astype(F32)
    for block in rims[1:]:
        total = total + block[...].astype(F32)
    edge_ref[...] = total
    fetch.wait()
    row, _ = split(index_ref[...], cols)
    _, colc = split(upright(index_ref), cols)
    slots = row.shape[1]
    cells = lax.broadcasted_iota(jnp.int32, (slots, cols), 1)
    hots = [hot(colc + (b - 1) == cells) for b in range(3)]
    lines = lax.broadcasted_iota(jnp.int32, (rows, slots), 0)
    masks = [row + (a - 1) == lines for a in range(3)]
    spot = lax.broadcasted_iota(jnp.int32, (rows, 128), 1)
    line = lax.broadcasted_iota(jnp.int32, (rows, 128), 0)
    picks = [spot == line + 1, spot == line + 65]
    lane = lax.broadcasted_iota(jnp.int32, (rows, cols), 1)
    high = lax.broadcasted_iota(jnp.int32, (rows, cols), 0)
    step = 8
    for c0 in range(0, portion, step):
        acc = None
        for b in range(3):
            parts = []
            for c in range(c0, c0 + step):
                part = jnp.zeros((rows, slots), F32)
                for a in range(3):
                    values = jnp.broadcast_to(sum_ref[3 * a + b, c : c + 1, :], (rows, slots))
                    part = jnp.where(masks[a], values, part)
                parts.append(part.astype(BF16))
            part = nn(jnp.concatenate(parts, 0), hots[b])
            acc = part if acc is None else acc + part
        for c in range(c0, c0 + step):
            field = acc[(c - c0) * rows : (c - c0 + 1) * rows] + own_ref[c].astype(F32)
            above = jnp.broadcast_to(edge_ref[0, c : c + 1, :], (rows, cols))
            below = jnp.broadcast_to(edge_ref[1, c : c + 1, :], (rows, cols))
            side = jnp.broadcast_to(edge_ref[2, c : c + 1, :], (rows, 128))
            last = jnp.sum(jnp.where(picks[0], side, 0.0), 1, keepdims=True)
            first = jnp.sum(jnp.where(picks[1], side, 0.0), 1, keepdims=True)
            field = field + jnp.where(high == 0, above, 0.0)
            field = field + jnp.where(high == rows - 1, below, 0.0)
            field = field + jnp.where(lane == 0, first, 0.0)
            out_ref[c] = field + jnp.where(lane == cols - 1, last, 0.0)


ROUTES = ((3, 2, 1), (0, 2, 3), (3, 1, 0), (0, 1, 2))


def route_table(count):
    rows = []
    for i in range(count):
        if count == 4:
            to = [i, *ROUTES[i]]
            rows.append([i, int(i in (1, 2)), *to, *(to.index(i ^ k) for k in range(4))])
        else:
            rows.append([i, 0, *((i + k) % count for k in range(count)), *range(count)])
    return rows


def shift(x, axis, by, wrap=True):
    size = lax.axis_size(axis)
    pairs = [(i, (i + by) % size) for i in range(size) if wrap or 0 <= i + by < size]
    return lax.ppermute(x, axis, pairs)


def from_sides(x, axis):
    if lax.axis_size(axis) == 2:
        other = shift(x, axis, 1)
        return other, other
    return shift(x, axis, 1), shift(x, axis, -1)


def steps(
    latent,
    conv_weight,
    mid_weight,
    out_weight,
    inner,
    outer,
    obs_values,
    obs_weight,
    obs_index,
    obs_count,
):
    chans, rows, cols = latent.shape
    groups, hidden, taps, _ = conv_weight.shape
    levels = out_weight.shape[1]
    slots = obs_index.shape[-1]
    own = groups * levels
    wide = groups * hidden
    lev_count = lax.axis_size("lev")
    scal = jnp.array(route_table(lev_count), jnp.int32)[lax.axis_index("lev")]
    portion = chans // lev_count
    index = obs_index.reshape(1, slots)
    flops = 2 * taps * wide * chans * slots

    strip = jax.ShapeDtypeStruct((cols, chans), BF16)
    tile, top, bottom, ends = call(
        turn_kernel,
        (
            jax.ShapeDtypeStruct((rows * cols, chans), BF16),
            strip,
            strip,
            jax.ShapeDtypeStruct((2, rows, chans), BF16),
        ),
        [SM, HBM],
        flops // 4,
        16,
        scratch_shapes=[
            pltpu.VMEM((rows // 8, chans, 8, cols), BF16),
            pltpu.VMEM((rows // 8, chans * 8, cols), F32),
            pltpu.VMEM((2, rows, chans), F32),
            pltpu.SemaphoreType.DMA((rows // 8,)),
        ],
    )(scal, latent)
    above = shift(bottom, "lat", 1, wrap=False)
    below = shift(top, "lat", -1, wrap=False)
    columns = jnp.stack(
        [
            jnp.concatenate([above[at : at + 1], ends[e], below[at : at + 1]], 0)
            for e, at in enumerate((0, cols - 1))
        ]
    )
    from_left, from_right = from_sides(columns, "lon")

    x = call(
        functools.partial(gather_kernel, rows, cols),
        jax.ShapeDtypeStruct((taps, slots, chans), BF16),
        [SM, VM, VM],
        flops,
        26,
        scratch_shapes=[
            pltpu.VMEM((((rows + 2) * cols + 16) * 8, 128), F32),
            pltpu.VMEM((3, slots * 8, 128), F32),
        ],
    )(index, index, tile)
    w = jnp.transpose(conv_weight, (2, 0, 1, 3)).reshape(taps, wide, chans)
    act_shape = jax.ShapeDtypeStruct((wide, slots), BF16)
    slope_one, slope_two, fields = call(
        functools.partial(decode_kernel, rows, cols),
        (act_shape, act_shape, jax.ShapeDtypeStruct((own, slots), BF16)),
        [VM] * 9,
        flops * 2,
        20,
        scratch_shapes=[pltpu.VMEM((2 * cols + 128, chans), BF16)],
    )(index, x, above, below, from_left, from_right, w, mid_weight, out_weight)

    blocks = [fields]
    for k in range(1, lev_count):
        blocks.append(shift(fields, "lev", -k))
    column_shape = jax.ShapeDtypeStruct((own * lev_count, slots), F32)
    turned = call(
        prepare_kernel,
        (
            column_shape,
            column_shape,
            jax.ShapeDtypeStruct((own, inner.shape[0]), BF16),
            jax.ShapeDtypeStruct((outer.shape[1], outer.shape[0]), BF16),
            jax.ShapeDtypeStruct((taps, chans, wide), BF16),
        ),
        [SM, SM] + [VM] * 5,
        flops,
        24,
        scratch_shapes=[pltpu.VMEM((inner.shape[1], inner.shape[0]), BF16)],
    )(scal, obs_count, obs_values[0, 0], obs_weight[None, :], inner, outer, w)
    obs_turned, scale, inner_turned, outer_turned, w_turned = turned

    patch_shape = jax.ShapeDtypeStruct((taps, portion, slots), BF16)
    patches = call(
        functools.partial(column_kernel, lev_count),
        (patch_shape,) * lev_count,
        [SM] + [VM] * (11 + lev_count),
        flops * 4,
        32,
        scratch_shapes=[
            pltpu.VMEM((own * lev_count, slots), BF16),
            pltpu.VMEM((own * lev_count, slots), F32),
            pltpu.VMEM((lev_count, taps, portion, slots), BF16),
        ],
    )(
        scal,
        inner,
        inner_turned,
        outer,
        outer_turned,
        obs_turned,
        scale,
        slope_one,
        slope_two,
        w_turned,
        mid_weight,
        out_weight,
        *blocks,
    )
    if lev_count == 4:
        relayed = lax.ppermute(patches[1], "lev", [(0, 1), (1, 0), (2, 3), (3, 2)])
        parts = [lax.ppermute(patches[2], "lev", [(1, 2), (2, 1)])]
        parts.append(lax.ppermute(patches[2], "lev", [(0, 2), (3, 1)]))
        passed = call(
            relay_kernel, patch_shape, [SM, VM, VM], flops // 64, 8
        )(scal, patches[3], relayed)
        parts.append(lax.ppermute(passed, "lev", [(0, 1), (1, 3), (3, 2), (2, 0)]))
    else:
        parts = []
        for k in range(1, lev_count):
            parts.append(shift(patches[k], "lev", k))
        relayed = parts.pop(0)

    line_shape = jax.ShapeDtypeStruct((lev_count, portion, cols), BF16)
    side_shape = jax.ShapeDtypeStruct((lev_count, portion, 128), BF16)
    row_edge, col_edge = call(
        functools.partial(edge_kernel, rows, cols),
        (jax.ShapeDtypeStruct((2, lev_count, portion, cols), BF16), side_shape),
        [VM] * (1 + lev_count),
        flops // 8,
        12,
    )(index, *patches)
    from_left, from_right = from_sides(col_edge, "lon")
    up, down = call(
        functools.partial(corner_kernel, rows, cols),
        (line_shape, line_shape),
        [VM] * 3,
        flops // 64,
        8,
    )(row_edge, from_left, from_right)
    onto_first = shift(down, "lat", 1, wrap=False)
    onto_last = shift(up, "lat", -1, wrap=False)
    joined = call(
        functools.partial(join_kernel, lev_count),
        (jax.ShapeDtypeStruct((3, portion, 128), BF16),) * lev_count,
        [SM] + [VM] * 4,
        flops // 64,
        12,
    )(scal, onto_first, onto_last, from_left, from_right)
    rims = [joined[0]]
    for k in range(1, lev_count):
        if lev_count == 4:
            rims.append(lax.ppermute(joined[k], "lev", [(i, i ^ k) for i in range(4)]))
        else:
            rims.append(shift(joined[k], "lev", k))

    return call(
        functools.partial(final_kernel, rows, cols, 2 + len(parts)),
        jax.ShapeDtypeStruct((portion, rows, cols), F32),
        [SM, VM, HBM] + [VM] * (2 + len(parts) + lev_count),
        flops // 4,
        16,
        scratch_shapes=[
            pltpu.VMEM((portion, rows, cols), BF16),
            pltpu.VMEM((taps, portion, slots), F32),
            pltpu.VMEM((3, portion, 128), F32),
            pltpu.SemaphoreType.DMA,
        ],
    )(scal, index, latent, patches[0], relayed, *parts, *rims)


def solution(mesh):
    return jax.shard_map(
        steps,
        mesh=mesh,
        in_specs=(
            P(None, "lat", "lon"),
            P("lev", None, None, None),
            P("lev", None, None),
            P("lev", None, None),
            P(),
            P(),
            P("lat", "lon", None, None),
            P(),
            P("lat", "lon", None),
            P("lat", "lon"),
        ),
        out_specs=P("lev", "lat", "lon"),
        check_vma=False,
    )
```

```python
import functools

import jax
import jax.numpy as jnp
from jax import lax
from jax.experimental import pallas as pl
from jax.experimental.pallas import tpu as pltpu
from jax.sharding import PartitionSpec as P

KAPPA = 0.7978845608028654
CUBIC = 0.044715
F32 = jnp.float32
BF16 = jnp.bfloat16


def gelu_slope(pre):
    square = pre * pre
    tanh_v = jnp.tanh(KAPPA * (pre + CUBIC * square * pre))
    value = 0.5 * pre * (1.0 + tanh_v)
    slope = 0.5 * (1.0 + tanh_v) + 0.5 * pre * (1.0 - tanh_v * tanh_v) * KAPPA * (
        1.0 + 3.0 * CUBIC * square
    )
    return value, slope


def nn(a, b):
    return lax.dot_general(a, b, (((1,), (0,)), ((), ())), preferred_element_type=F32)


def nt(a, b):
    return lax.dot_general(a, b, (((1,), (1,)), ((), ())), preferred_element_type=F32)


def tn(a, b):
    return lax.dot_general(a, b, (((0,), (0,)), ((), ())), preferred_element_type=F32)


ROUTES = ((0, 3, 2, 1), (1, 0, 2, 3), (2, 3, 1, 0), (3, 0, 1, 2))


def lookup(lev, values):
    found = jnp.int32(values[0])
    for i, value in enumerate(values[1:], 1):
        found = jnp.where(lev == i, value, found)
    return found


def relays(lev, count):
    return (lev == 1) | (lev == 2) if count == 4 else lev < 0


def target(lev, count, k):
    if count == 4:
        return lookup(lev, [ROUTES[i][k] for i in range(4)])
    return lax.rem(lev + k, count)


def place(lev, count, k):
    if count == 4:
        return lookup(lev, [ROUTES[i].index(i ^ k) for i in range(4)])
    return k


def split(index, cols):
    if cols & (cols - 1):
        return index // cols, index % cols
    bits = cols.bit_length() - 1
    return index >> bits, index & (cols - 1)


def hot(mask):
    return mask.astype(F32).astype(BF16)


def upright(index_ref):
    slots = index_ref.shape[1]
    return jnp.broadcast_to(index_ref[...], (128, slots)).T


def call(kernel, out_shape, in_specs, flops, mib, **kwargs):
    bytes_out = sum(s.size * s.dtype.itemsize for s in jax.tree.leaves(out_shape))
    return pl.pallas_call(
        kernel,
        out_shape=out_shape,
        in_specs=in_specs,
        out_specs=jax.tree.map(lambda _: VM, out_shape),
        cost_estimate=pl.CostEstimate(
            flops=flops, bytes_accessed=4 * bytes_out, transcendentals=0
        ),
        compiler_params=pltpu.CompilerParams(vmem_limit_bytes=mib << 20),
        **kwargs,
    )


VM = pl.BlockSpec(memory_space=pltpu.VMEM)
SM = pl.BlockSpec(memory_space=pltpu.SMEM)
HBM = pl.BlockSpec(memory_space=pltpu.MemorySpace.HBM)


def turn_kernel(
    _, lat_ref, tile_ref, top_ref, bottom_ref, side_ref, near_ref, wide_ref, keep_ref, sems
):
    chans, rows, cols = lat_ref.shape
    count = rows // 8
    copies = [
        pltpu.make_async_copy(lat_ref.at[:, pl.ds(8 * i, 8)], near_ref.at[i], sems.at[i])
        for i in range(count)
    ]
    for copy in copies:
        copy.start()
    for i, copy in enumerate(copies):
        copy.wait()
        wide_ref[i] = near_ref[i].reshape(chans * 8, cols).astype(F32)
        for r in range(8 * i, 8 * i + 8):
            line = wide_ref[i, pl.ds(r - 8 * i, chans, stride=8), :].astype(BF16).T
            tile_ref[r * cols : (r + 1) * cols, :] = line
            keep_ref[0, r : r + 1, :] = line[0:1].astype(F32)
            keep_ref[1, r : r + 1, :] = line[cols - 1 : cols].astype(F32)
            if r == 0:
                top_ref[...] = line
            if r == rows - 1:
                bottom_ref[...] = line
    side_ref[...] = keep_ref[...].astype(BF16)


def gather_kernel(rows, cols, index_sm, index_ref, tile_ref, out_ref, table_ref, x_ref):
    chans = tile_ref.shape[1]
    slots = index_ref.shape[1]
    halves = chans // 128
    lead = cols + 8
    for r in range(rows):
        line = tile_ref[r * cols : (r + 1) * cols, :].astype(F32)
        for b in range(3):
            for h in range(halves):
                at = (lead + r * cols - b + 1) * 8 + halves * b + h
                table_ref[pl.ds(at, cols, stride=8), :] = line[:, h * 128 : (h + 1) * 128]

    def body(i, carry):
        for j in range(8):
            s = i * 8 + j
            base = (index_sm[0, s] + (lead - cols)) * 8
            for a in range(3):
                x_ref[a, pl.ds(pl.multiple_of(s * 8, 8), 8), :] = table_ref[
                    pl.ds(pl.multiple_of(base + a * cols * 8, 8), 8), :
                ]
        return carry

    lax.fori_loop(0, slots // 8, body, 0)
    row, col = split(upright(index_ref), cols)
    for a in range(3):
        for b in range(3):
            at_row, at_col = row + (a - 1), col + (b - 1)
            inside = (at_row >= 0) & (at_row < rows) & (at_col >= 0) & (at_col < cols)
            for h in range(halves):
                x = x_ref[a, pl.ds(halves * b + h, slots, stride=8), :]
                out_ref[3 * a + b, :, h * 128 : (h + 1) * 128] = jnp.where(inside, x, 0.0).astype(
                    BF16
                )


def decode_kernel(
    rows,
    cols,
    index_ref,
    x_ref,
    above_ref,
    below_ref,
    left_ref,
    right_ref,
    w_ref,
    mid_ref,
    outw_ref,
    s1_ref,
    s2_ref,
    field_ref,
    halo_ref,
):
    slots = index_ref.shape[1]
    groups, hidden, _ = mid_ref.shape
    levels = outw_ref.shape[1]
    width = halo_ref.shape[0]
    tall = (width - 2 * cols) // 2
    halo_ref[...] = jnp.zeros_like(halo_ref)
    halo_ref[0:cols, :] = above_ref[...]
    halo_ref[cols : 2 * cols, :] = below_ref[...]
    halo_ref[2 * cols : 2 * cols + rows + 2, :] = left_ref[1]
    halo_ref[2 * cols + tall : 2 * cols + tall + rows + 2, :] = right_ref[0]
    row, col = split(upright(index_ref), cols)
    cells = lax.broadcasted_iota(jnp.int32, (slots, width), 1)
    acc = None
    for a in range(3):
        for b in range(3):
            at_row, at_col = row + (a - 1), col + (b - 1)
            rim = jnp.where(at_row < 0, at_col, jnp.where(at_row >= rows, cols + at_col, -1))
            rim = jnp.where(at_col < 0, 2 * cols + at_row + 1, rim)
            rim = jnp.where(at_col >= cols, 2 * cols + tall + at_row + 1, rim)
            rim = jnp.concatenate([rim] * (width // 128), 1)
            x = x_ref[3 * a + b] + nn(hot(cells == rim), halo_ref[...]).astype(BF16)
            part = nt(w_ref[3 * a + b], x)
            acc = part if acc is None else acc + part
    act, slope = gelu_slope(acc)
    s1_ref[...] = slope.astype(BF16)
    act = act.astype(BF16)
    for g in range(groups):
        two = nn(mid_ref[g], act[g * hidden : (g + 1) * hidden])
        value, slope = gelu_slope(two)
        s2_ref[g * hidden : (g + 1) * hidden, :] = slope.astype(BF16)
        field_ref[g * levels : (g + 1) * levels, :] = nn(
            outw_ref[g], value.astype(BF16)
        ).astype(BF16)


def prepare_kernel(
    lev_ref,
    count_ref,
    obs_ref,
    weight_ref,
    inner_ref,
    outer_ref,
    w_ref,
    obst_ref,
    scale_ref,
    innert_ref,
    outert_ref,
    wt_ref,
    turn_ref,
):
    obst_ref[...] = obs_ref[...].T
    slots = obs_ref.shape[0]
    levels = weight_ref.shape[1]
    weight = jnp.broadcast_to(weight_ref[...], (128, levels)).T
    live = lax.broadcasted_iota(jnp.int32, (levels, 128), 1)
    for h in range(slots // 128):
        scale_ref[:, h * 128 : (h + 1) * 128] = jnp.where(
            live + h * 128 < count_ref[0, 0], weight, 0.0
        )
    turn_ref[...] = inner_ref[...].T
    own = innert_ref.shape[0]
    innert_ref[...] = turn_ref[pl.ds(pl.multiple_of(lev_ref[0] * own, 16), own), :]
    outert_ref[...] = outer_ref[...].T
    for t in range(w_ref.shape[0]):
        wt_ref[t] = w_ref[t].T


def column_kernel(
    lev_count,
    lev_ref,
    inner_ref,
    innert_ref,
    outer_ref,
    outert_ref,
    obst_ref,
    scale_ref,
    s1_ref,
    s2_ref,
    wt_ref,
    mid_ref,
    outw_ref,
    *rest,
):
    blocks = rest[:lev_count]
    outs = rest[lev_count : 2 * lev_count]
    f_ref, mis_ref, g_ref = rest[2 * lev_count :]
    lev = lev_ref[0]
    own = blocks[0].shape[0]
    for k in range(lev_count):
        at = pl.multiple_of(lax.rem(lev + k, lev_count) * own, 16)
        f_ref[pl.ds(at, own), :] = blocks[k][...]
    pre_col = nn(inner_ref[...], f_ref[...])
    act, slope = gelu_slope(pre_col)
    forecast = f_ref[...].astype(F32) + nn(outer_ref[...], act.astype(BF16))
    misfit = (forecast - obst_ref[...]) * scale_ref[...]
    mis_ref[...] = misfit
    grad_act = (nn(outert_ref[...], misfit.astype(BF16)) * slope).astype(BF16)
    mine = mis_ref[pl.ds(pl.multiple_of(lev * own, 16), own), :]
    grad_fields = (mine + nn(innert_ref[...], grad_act)).astype(BF16)
    groups, hidden, _ = mid_ref.shape
    levels = outw_ref.shape[1]
    ones = []
    for g in range(groups):
        span = slice(g * hidden, (g + 1) * hidden)
        two = (
            tn(outw_ref[g], grad_fields[g * levels : (g + 1) * levels]) * s2_ref[span, :].astype(F32)
        ).astype(BF16)
        ones.append((tn(mid_ref[g], two) * s1_ref[span, :].astype(F32)).astype(BF16))
    grad_one = jnp.concatenate(ones, 0)
    taps = wt_ref.shape[0]
    portion = wt_ref.shape[1] // lev_count
    for t in range(taps):
        patch = nn(wt_ref[t], grad_one).astype(BF16)
        for d in range(lev_count):
            g_ref[d, t] = patch[d * portion : (d + 1) * portion]
    for k in range(lev_count):
        outs[k][...] = g_ref[target(lev, lev_count, k)]


def edge_kernel(rows, cols, index_ref, *rest):
    blocks, (rowout_ref, colout_ref) = rest[:-2], rest[-2:]
    row, col = split(index_ref[...], cols)
    rowc, colc = split(upright(index_ref), cols)
    slots = row.shape[1]
    cells = lax.broadcasted_iota(jnp.int32, (slots, cols), 1)
    lines = lax.broadcasted_iota(jnp.int32, (slots, 128), 1)
    for k, block in enumerate(blocks):
        for e, (edge, a) in enumerate(((0, 0), (rows - 1, 2))):
            acc = None
            for b in range(3):
                part = jnp.where(row == edge, block[3 * a + b].astype(F32), 0.0).astype(BF16)
                part = nn(part, hot(colc + (b - 1) == cells))
                acc = part if acc is None else acc + part
            rowout_ref[e, k] = acc.astype(BF16)
        acc = None
        for e, (edge, b) in enumerate(((0, 0), (cols - 1, 2))):
            for a in range(3):
                part = jnp.where(col == edge, block[3 * a + b].astype(F32), 0.0).astype(BF16)
                part = nn(part, hot(rowc + (a + 64 * e) == lines))
                acc = part if acc is None else acc + part
        colout_ref[k] = acc.astype(BF16)


def corner_kernel(rows, cols, rowin_ref, left_ref, right_ref, up_ref, down_ref):
    lane = lax.broadcasted_iota(jnp.int32, up_ref.shape, 2)
    for e, (at, ref) in enumerate(((0, up_ref), (rows + 1, down_ref))):
        line = rowin_ref[e].astype(F32)
        line = line + jnp.where(lane == 0, left_ref[:, :, 64 + at : 65 + at].astype(F32), 0.0)
        line = line + jnp.where(
            lane == cols - 1, right_ref[:, :, at : at + 1].astype(F32), 0.0
        )
        ref[...] = line.astype(BF16)


def join_kernel(count, lev_ref, top_ref, bottom_ref, left_ref, right_ref, *outs):
    portion = top_ref.shape[1]
    spot = lax.broadcasted_iota(jnp.int32, (portion, 128), 1)
    for k in range(count):
        at = place(lev_ref[0], count, k)
        outs[k][0] = top_ref[at]
        outs[k][1] = bottom_ref[at]
        side = jnp.where(spot < 64, right_ref[at].astype(F32), left_ref[at].astype(F32))
        outs[k][2] = side.astype(BF16)


def relay_kernel(count, lev_ref, block_ref, got_ref, out_ref):
    keep = jnp.where(relays(lev_ref[0], count), 1.0, 0.0)
    out_ref[...] = (block_ref[...].astype(F32) + got_ref[...].astype(F32) * keep).astype(BF16)


def final_kernel(rows, cols, count, lev_ref, index_ref, latent_ref, *rest):
    rims, own, relayed = rest[:count], rest[count], rest[count + 1]
    parts, (out_ref, own_ref, sum_ref, edge_ref, sem) = rest[count + 2 : -5], rest[-5:]
    portion = out_ref.shape[0]
    fetch = pltpu.make_async_copy(
        latent_ref.at[pl.ds(pl.multiple_of(lev_ref[0] * portion, 8), portion)], own_ref, sem
    )
    fetch.start()
    keep = jnp.where(relays(lev_ref[0], count), 0.0, 1.0)
    total = own[...].astype(F32) + relayed[...].astype(F32) * keep
    for block in parts:
        total = total + block[...].astype(F32)
    sum_ref[...] = total
    total = rims[0][...].astype(F32)
    for block in rims[1:]:
        total = total + block[...].astype(F32)
    edge_ref[...] = total
    fetch.wait()
    row, _ = split(index_ref[...], cols)
    _, colc = split(upright(index_ref), cols)
    slots = row.shape[1]
    cells = lax.broadcasted_iota(jnp.int32, (slots, cols), 1)
    hots = [hot(colc + (b - 1) == cells) for b in range(3)]
    lines = lax.broadcasted_iota(jnp.int32, (rows, slots), 0)
    masks = [row + (a - 1) == lines for a in range(3)]
    spot = lax.broadcasted_iota(jnp.int32, (rows, 128), 1)
    line = lax.broadcasted_iota(jnp.int32, (rows, 128), 0)
    picks = [spot == line + 1, spot == line + 65]
    lane = lax.broadcasted_iota(jnp.int32, (rows, cols), 1)
    high = lax.broadcasted_iota(jnp.int32, (rows, cols), 0)
    step = 8
    for c0 in range(0, portion, step):
        acc = None
        for b in range(3):
            parts = []
            for c in range(c0, c0 + step):
                part = jnp.zeros((rows, slots), F32)
                for a in range(3):
                    values = jnp.broadcast_to(sum_ref[3 * a + b, c : c + 1, :], (rows, slots))
                    part = jnp.where(masks[a], values, part)
                parts.append(part.astype(BF16))
            part = nn(jnp.concatenate(parts, 0), hots[b])
            acc = part if acc is None else acc + part
        for c in range(c0, c0 + step):
            field = acc[(c - c0) * rows : (c - c0 + 1) * rows] + own_ref[c].astype(F32)
            above = jnp.broadcast_to(edge_ref[0, c : c + 1, :], (rows, cols))
            below = jnp.broadcast_to(edge_ref[1, c : c + 1, :], (rows, cols))
            side = jnp.broadcast_to(edge_ref[2, c : c + 1, :], (rows, 128))
            last = jnp.sum(jnp.where(picks[0], side, 0.0), 1, keepdims=True)
            first = jnp.sum(jnp.where(picks[1], side, 0.0), 1, keepdims=True)
            field = field + jnp.where(high == 0, above, 0.0)
            field = field + jnp.where(high == rows - 1, below, 0.0)
            field = field + jnp.where(lane == 0, first, 0.0)
            out_ref[c] = field + jnp.where(lane == cols - 1, last, 0.0)


def shift(x, axis, by, wrap=True):
    size = lax.axis_size(axis)
    pairs = [(i, (i + by) % size) for i in range(size) if wrap or 0 <= i + by < size]
    return lax.ppermute(x, axis, pairs)


def from_sides(x, axis):
    if lax.axis_size(axis) == 2:
        other = shift(x, axis, 1)
        return other, other
    return shift(x, axis, 1), shift(x, axis, -1)


def steps(
    latent,
    conv_weight,
    mid_weight,
    out_weight,
    inner,
    outer,
    obs_values,
    obs_weight,
    obs_index,
    obs_count,
):
    chans, rows, cols = latent.shape
    groups, hidden, taps, _ = conv_weight.shape
    levels = out_weight.shape[1]
    slots = obs_index.shape[-1]
    own = groups * levels
    wide = groups * hidden
    lev_count = lax.axis_size("lev")
    lev = lax.axis_index("lev").astype(jnp.int32).reshape(1)
    portion = chans // lev_count
    index = obs_index.reshape(1, slots)
    far = pltpu.with_memory_space_constraint(latent, pltpu.MemorySpace.HBM)
    flops = 2 * taps * wide * chans * slots

    strip = jax.ShapeDtypeStruct((cols, chans), BF16)
    tile, top, bottom, ends = call(
        turn_kernel,
        (
            jax.ShapeDtypeStruct((rows * cols, chans), BF16),
            strip,
            strip,
            jax.ShapeDtypeStruct((2, rows, chans), BF16),
        ),
        [SM, HBM],
        flops // 4,
        16,
        scratch_shapes=[
            pltpu.VMEM((rows // 8, chans, 8, cols), BF16),
            pltpu.VMEM((rows // 8, chans * 8, cols), F32),
            pltpu.VMEM((2, rows, chans), F32),
            pltpu.SemaphoreType.DMA((rows // 8,)),
        ],
    )(lev, far)
    above = shift(bottom, "lat", 1, wrap=False)
    below = shift(top, "lat", -1, wrap=False)
    columns = jnp.stack(
        [
            jnp.concatenate([above[at : at + 1], ends[e], below[at : at + 1]], 0)
            for e, at in enumerate((0, cols - 1))
        ]
    )
    from_left, from_right = from_sides(columns, "lon")

    x = call(
        functools.partial(gather_kernel, rows, cols),
        jax.ShapeDtypeStruct((taps, slots, chans), BF16),
        [SM, VM, VM],
        flops,
        26,
        scratch_shapes=[
            pltpu.VMEM((((rows + 2) * cols + 16) * 8, 128), F32),
            pltpu.VMEM((3, slots * 8, 128), F32),
        ],
    )(index, index, tile)
    w = jnp.transpose(conv_weight, (2, 0, 1, 3)).reshape(taps, wide, chans)
    act_shape = jax.ShapeDtypeStruct((wide, slots), BF16)
    slope_one, slope_two, fields = call(
        functools.partial(decode_kernel, rows, cols),
        (act_shape, act_shape, jax.ShapeDtypeStruct((own, slots), BF16)),
        [VM] * 9,
        flops * 2,
        20,
        scratch_shapes=[pltpu.VMEM((2 * cols + 128, chans), BF16)],
    )(index, x, above, below, from_left, from_right, w, mid_weight, out_weight)

    blocks = [fields]
    for k in range(1, lev_count):
        blocks.append(shift(fields, "lev", -k))
    column_shape = jax.ShapeDtypeStruct((own * lev_count, slots), F32)
    turned = call(
        prepare_kernel,
        (
            column_shape,
            column_shape,
            jax.ShapeDtypeStruct((own, inner.shape[0]), BF16),
            jax.ShapeDtypeStruct((outer.shape[1], outer.shape[0]), BF16),
            jax.ShapeDtypeStruct((taps, chans, wide), BF16),
        ),
        [SM, SM] + [VM] * 5,
        flops,
        24,
        scratch_shapes=[pltpu.VMEM((inner.shape[1], inner.shape[0]), BF16)],
    )(lev, obs_count, obs_values[0, 0], obs_weight[None, :], inner, outer, w)
    obs_turned, scale, inner_turned, outer_turned, w_turned = turned

    patch_shape = jax.ShapeDtypeStruct((taps, portion, slots), BF16)
    patches = call(
        functools.partial(column_kernel, lev_count),
        (patch_shape,) * lev_count,
        [SM] + [VM] * (11 + lev_count),
        flops * 4,
        32,
        scratch_shapes=[
            pltpu.VMEM((own * lev_count, slots), BF16),
            pltpu.VMEM((own * lev_count, slots), F32),
            pltpu.VMEM((lev_count, taps, portion, slots), BF16),
        ],
    )(
        lev,
        inner,
        inner_turned,
        outer,
        outer_turned,
        obs_turned,
        scale,
        slope_one,
        slope_two,
        w_turned,
        mid_weight,
        out_weight,
        *blocks,
    )
    if lev_count == 4:
        relayed = lax.ppermute(patches[1], "lev", [(0, 1), (1, 0), (2, 3), (3, 2)])
        parts = [lax.ppermute(patches[2], "lev", [(1, 2), (2, 1)])]
        parts.append(lax.ppermute(patches[2], "lev", [(0, 2), (3, 1)]))
        passed = call(
            functools.partial(relay_kernel, lev_count), patch_shape, [SM, VM, VM], flops // 64, 8
        )(lev, patches[3], relayed)
        parts.append(lax.ppermute(passed, "lev", [(0, 1), (1, 3), (3, 2), (2, 0)]))
    else:
        parts = []
        for k in range(1, lev_count):
            parts.append(shift(patches[k], "lev", k))
        relayed = parts.pop(0)

    line_shape = jax.ShapeDtypeStruct((lev_count, portion, cols), BF16)
    side_shape = jax.ShapeDtypeStruct((lev_count, portion, 128), BF16)
    row_edge, col_edge = call(
        functools.partial(edge_kernel, rows, cols),
        (jax.ShapeDtypeStruct((2, lev_count, portion, cols), BF16), side_shape),
        [VM] * (1 + lev_count),
        flops // 8,
        12,
    )(index, *patches)
    from_left, from_right = from_sides(col_edge, "lon")
    up, down = call(
        functools.partial(corner_kernel, rows, cols),
        (line_shape, line_shape),
        [VM] * 3,
        flops // 64,
        8,
    )(row_edge, from_left, from_right)
    onto_first = shift(down, "lat", 1, wrap=False)
    onto_last = shift(up, "lat", -1, wrap=False)
    joined = call(
        functools.partial(join_kernel, lev_count),
        (jax.ShapeDtypeStruct((3, portion, 128), BF16),) * lev_count,
        [SM] + [VM] * 4,
        flops // 64,
        12,
    )(lev, onto_first, onto_last, from_left, from_right)
    rims = [joined[0]]
    for k in range(1, lev_count):
        if lev_count == 4:
            rims.append(lax.ppermute(joined[k], "lev", [(i, i ^ k) for i in range(4)]))
        else:
            rims.append(shift(joined[k], "lev", k))

    return call(
        functools.partial(final_kernel, rows, cols, lev_count),
        jax.ShapeDtypeStruct((portion, rows, cols), F32),
        [SM, VM, HBM] + [VM] * (2 + len(parts) + lev_count),
        flops // 4,
        16,
        scratch_shapes=[
            pltpu.VMEM((portion, rows, cols), BF16),
            pltpu.VMEM((taps, portion, slots), F32),
            pltpu.VMEM((3, portion, 128), F32),
            pltpu.SemaphoreType.DMA,
        ],
    )(lev, index, far, *rims, patches[0], relayed, *parts)


def solution(mesh):
    return jax.shard_map(
        steps,
        mesh=mesh,
        in_specs=(
            P(None, "lat", "lon"),
            P("lev", None, None, None),
            P("lev", None, None),
            P("lev", None, None),
            P(),
            P(),
            P("lat", "lon", None, None),
            P(),
            P("lat", "lon", None),
            P("lat", "lon"),
        ),
        out_specs=P("lev", "lat", "lon"),
        check_vma=False,
    )
```

```python
import functools

import jax
import jax.numpy as jnp
from jax import lax
from jax.experimental import pallas as pl
from jax.experimental.pallas import tpu as pltpu
from jax.sharding import PartitionSpec as P

KAPPA = 0.7978845608028654
CUBIC = 0.044715
F32 = jnp.float32
BF16 = jnp.bfloat16


def gelu_slope(pre):
    square = pre * pre
    tanh_v = jnp.tanh(KAPPA * (pre + CUBIC * square * pre))
    value = 0.5 * pre * (1.0 + tanh_v)
    slope = 0.5 * (1.0 + tanh_v) + 0.5 * pre * (1.0 - tanh_v * tanh_v) * KAPPA * (
        1.0 + 3.0 * CUBIC * square
    )
    return value, slope


def nn(a, b):
    return lax.dot_general(a, b, (((1,), (0,)), ((), ())), preferred_element_type=F32)


def nt(a, b):
    return lax.dot_general(a, b, (((1,), (1,)), ((), ())), preferred_element_type=F32)


def tn(a, b):
    return lax.dot_general(a, b, (((0,), (0,)), ((), ())), preferred_element_type=F32)


ROUTES = ((0, 3, 2, 1), (1, 0, 2, 3), (2, 3, 1, 0), (3, 0, 1, 2))


def lookup(lev, values):
    found = jnp.int32(values[0])
    for i, value in enumerate(values[1:], 1):
        found = jnp.where(lev == i, value, found)
    return found


def relays(lev, count):
    return (lev == 1) | (lev == 2) if count == 4 else lev < 0


def source(lev, count, k):
    return lax.bitwise_xor(lev, k) if count == 4 else lax.rem(lev + k, count)


def target(lev, count, k):
    if count == 4:
        return lookup(lev, [ROUTES[i][k] for i in range(4)])
    return lax.rem(lev + k, count)


def place(lev, count, k):
    if count == 4:
        return lookup(lev, [ROUTES[i].index(i ^ (0, 2, 1, 3)[k]) for i in range(4)])
    return k


def split(index, cols):
    if cols & (cols - 1):
        return index // cols, index % cols
    bits = cols.bit_length() - 1
    return index >> bits, index & (cols - 1)


def hot(mask):
    return mask.astype(F32).astype(BF16)


def upright(index_ref):
    slots = index_ref.shape[1]
    return jnp.broadcast_to(index_ref[...], (128, slots)).T


def call(kernel, out_shape, in_specs, flops, mib, out_specs=None, **kwargs):
    bytes_out = sum(s.size * s.dtype.itemsize for s in jax.tree.leaves(out_shape))
    return pl.pallas_call(
        kernel,
        out_shape=out_shape,
        in_specs=in_specs,
        out_specs=out_specs or jax.tree.map(lambda _: VM, out_shape),
        cost_estimate=pl.CostEstimate(
            flops=flops, bytes_accessed=4 * bytes_out, transcendentals=0
        ),
        compiler_params=pltpu.CompilerParams(vmem_limit_bytes=mib << 20),
        **kwargs,
    )


STEP = 8

VM = pl.BlockSpec(memory_space=pltpu.VMEM)
SM = pl.BlockSpec(memory_space=pltpu.SMEM)
HBM = pl.BlockSpec(memory_space=pltpu.MemorySpace.HBM)


def turn_kernel(
    _, lat_ref, tile_ref, top_ref, bottom_ref, side_ref, near_ref, wide_ref, keep_ref, sems
):
    chans, rows, cols = lat_ref.shape
    count = rows // 8
    copies = [
        pltpu.make_async_copy(lat_ref.at[:, pl.ds(8 * i, 8)], near_ref.at[i], sems.at[i])
        for i in range(count)
    ]
    for copy in copies:
        copy.start()
    for i, copy in enumerate(copies):
        copy.wait()
        wide_ref[i] = near_ref[i].reshape(chans * 8, cols).astype(F32)
        for r in range(8 * i, 8 * i + 8):
            line = wide_ref[i, pl.ds(r - 8 * i, chans, stride=8), :].astype(BF16).T
            tile_ref[r * cols : (r + 1) * cols, :] = line
            keep_ref[0, r : r + 1, :] = line[0:1].astype(F32)
            keep_ref[1, r : r + 1, :] = line[cols - 1 : cols].astype(F32)
            if r == 0:
                top_ref[...] = line
            if r == rows - 1:
                bottom_ref[...] = line
    side_ref[...] = keep_ref[...].astype(BF16)


def gather_kernel(rows, cols, index_sm, index_ref, tile_ref, out_ref, table_ref, x_ref):
    chans = tile_ref.shape[1]
    slots = index_ref.shape[1]
    halves = chans // 128
    lead = cols + 8
    size = table_ref.shape[0]
    margin = (lead + 1) * 8
    table_ref[0:margin, :] = jnp.zeros((margin, 128), F32)
    table_ref[size - margin : size, :] = jnp.zeros((margin, 128), F32)
    for r in range(rows):
        line = tile_ref[r * cols : (r + 1) * cols, :].astype(F32)
        for b in range(3):
            for h in range(halves):
                at = (lead + r * cols - b + 1) * 8 + halves * b + h
                table_ref[pl.ds(at, cols, stride=8), :] = line[:, h * 128 : (h + 1) * 128]

    def body(i, carry):
        for j in range(8):
            s = i * 8 + j
            base = (index_sm[0, s] + (lead - cols)) * 8
            for a in range(3):
                x_ref[a, pl.ds(pl.multiple_of(s * 8, 8), 8), :] = table_ref[
                    pl.ds(pl.multiple_of(base + a * cols * 8, 8), 8), :
                ]
        return carry

    lax.fori_loop(0, slots // 8, body, 0)
    _, col = split(upright(index_ref), cols)
    for a in range(3):
        for b in range(3):
            for h in range(halves):
                x = x_ref[a, pl.ds(halves * b + h, slots, stride=8), :]
                if b != 1:
                    x = jnp.where(col == (0 if b == 0 else cols - 1), 0.0, x)
                out_ref[3 * a + b, :, h * 128 : (h + 1) * 128] = x.astype(BF16)


def decode_kernel(
    rows,
    cols,
    index_ref,
    x_ref,
    above_ref,
    below_ref,
    left_ref,
    right_ref,
    w_ref,
    mid_ref,
    outw_ref,
    s1_ref,
    s2_ref,
    field_ref,
    halo_ref,
):
    slots = index_ref.shape[1]
    groups, hidden, _ = mid_ref.shape
    levels = outw_ref.shape[1]
    width = halo_ref.shape[0]
    tall = (width - 2 * cols) // 2
    halo_ref[...] = jnp.zeros_like(halo_ref)
    halo_ref[0:cols, :] = above_ref[...]
    halo_ref[cols : 2 * cols, :] = below_ref[...]
    halo_ref[2 * cols : 2 * cols + rows + 2, :] = left_ref[1]
    halo_ref[2 * cols + tall : 2 * cols + tall + rows + 2, :] = right_ref[0]
    row, col = split(upright(index_ref), cols)
    cells = lax.broadcasted_iota(jnp.int32, (slots, width), 1)
    lefts, rights = [], []
    for a in range(3):
        for b in range(3):
            at_row, at_col = row + (a - 1), col + (b - 1)
            rim = jnp.where(at_row < 0, at_col, jnp.where(at_row >= rows, cols + at_col, -1))
            rim = jnp.where(at_col < 0, 2 * cols + at_row + 1, rim)
            rim = jnp.where(at_col >= cols, 2 * cols + tall + at_row + 1, rim)
            rim = jnp.concatenate([rim] * (width // 128), 1)
            x = x_ref[3 * a + b] + nn(hot(cells == rim), halo_ref[...]).astype(BF16)
            lefts.append(w_ref[3 * a + b])
            rights.append(x)
    acc = nt(jnp.concatenate(lefts, 1), jnp.concatenate(rights, 1))
    act, slope = gelu_slope(acc)
    s1_ref[...] = slope.astype(BF16)
    act = act.astype(BF16)
    for g in range(groups):
        two = nn(mid_ref[g], act[g * hidden : (g + 1) * hidden])
        value, slope = gelu_slope(two)
        s2_ref[g * hidden : (g + 1) * hidden, :] = slope.astype(BF16)
        field_ref[g * levels : (g + 1) * levels, :] = nn(
            outw_ref[g], value.astype(BF16)
        ).astype(BF16)


def prepare_kernel(
    lev_ref,
    count_ref,
    obs_ref,
    weight_ref,
    inner_ref,
    outer_ref,
    w_ref,
    obst_ref,
    scale_ref,
    innert_ref,
    outert_ref,
    wt_ref,
    turn_ref,
):
    obst_ref[...] = obs_ref[...].T
    slots = obs_ref.shape[0]
    levels = weight_ref.shape[1]
    weight = jnp.broadcast_to(weight_ref[...], (128, levels)).T
    live = lax.broadcasted_iota(jnp.int32, (levels, 128), 1)
    for h in range(slots // 128):
        scale_ref[:, h * 128 : (h + 1) * 128] = jnp.where(
            live + h * 128 < count_ref[0, 0], weight, 0.0
        )
    turn_ref[...] = inner_ref[...].T
    own = innert_ref.shape[0]
    innert_ref[...] = turn_ref[pl.ds(pl.multiple_of(lev_ref[0] * own, 16), own), :]
    outert_ref[...] = outer_ref[...].T
    for t in range(w_ref.shape[0]):
        wt_ref[t] = w_ref[t].T


def column_kernel(
    lev_count,
    lev_ref,
    inner_ref,
    innert_ref,
    outer_ref,
    outert_ref,
    obst_ref,
    scale_ref,
    s1_ref,
    s2_ref,
    wt_ref,
    mid_ref,
    outw_ref,
    *rest,
):
    blocks = rest[:lev_count]
    outs = rest[lev_count : 2 * lev_count]
    f_ref, mis_ref = rest[2 * lev_count :]
    lev = lev_ref[0]
    own = blocks[0].shape[0]
    for k in range(lev_count):
        at = pl.multiple_of(source(lev, lev_count, k) * own, 16)
        f_ref[pl.ds(at, own), :] = blocks[k][...]
    wide = inner_ref.shape[0]
    fields = f_ref[...]
    acts, slopes = [], []
    for j in range(0, wide, 256):
        act, slope = gelu_slope(nn(inner_ref[j : j + 256, :], fields))
        acts.append(act.astype(BF16))
        slopes.append(slope)
    act = jnp.concatenate(acts, 0)
    misfits = []
    for j in range(0, own * lev_count, 256):
        forecast = f_ref[j : j + 256, :].astype(F32) + nn(outer_ref[j : j + 256, :], act)
        misfit = (forecast - obst_ref[j : j + 256, :]) * scale_ref[j : j + 256, :]
        mis_ref[j : j + 256, :] = misfit
        misfits.append(misfit.astype(BF16))
    misfit = jnp.concatenate(misfits, 0)
    grad_act = jnp.concatenate(
        [
            (nn(outert_ref[j : j + 256, :], misfit) * slopes[j // 256]).astype(BF16)
            for j in range(0, wide, 256)
        ],
        0,
    )
    mine = mis_ref[pl.ds(pl.multiple_of(lev * own, 16), own), :]
    grad_fields = (mine + nn(innert_ref[...], grad_act)).astype(BF16)
    groups, hidden, _ = mid_ref.shape
    levels = outw_ref.shape[1]
    ones = []
    for g in range(groups):
        span = slice(g * hidden, (g + 1) * hidden)
        two = (
            tn(outw_ref[g], grad_fields[g * levels : (g + 1) * levels]) * s2_ref[span, :].astype(F32)
        ).astype(BF16)
        ones.append((tn(mid_ref[g], two) * s1_ref[span, :].astype(F32)).astype(BF16))
    grad_one = jnp.concatenate(ones, 0)
    taps = wt_ref.shape[0]
    portion = wt_ref.shape[1] // lev_count
    for k in range(lev_count):
        at = pl.multiple_of(target(lev, lev_count, k) * portion, 16)
        left = jnp.concatenate([wt_ref[t, pl.ds(at, portion), :] for t in range(taps)], 0)
        outs[k][...] = nn(left, grad_one).astype(BF16).reshape(taps, portion, -1)


def edge_kernel(rows, cols, index_ref, *rest):
    blocks, (rowout_ref, colout_ref) = rest[:-2], rest[-2:]
    row, col = split(index_ref[...], cols)
    rowc, colc = split(upright(index_ref), cols)
    slots = row.shape[1]
    cells = lax.broadcasted_iota(jnp.int32, (slots, cols), 1)
    lines = lax.broadcasted_iota(jnp.int32, (slots, 128), 1)
    for k, block in enumerate(blocks):
        for e, (edge, a) in enumerate(((0, 0), (rows - 1, 2))):
            acc = None
            for b in range(3):
                part = jnp.where(row == edge, block[3 * a + b].astype(F32), 0.0).astype(BF16)
                part = nn(part, hot(colc + (b - 1) == cells))
                acc = part if acc is None else acc + part
            rowout_ref[e, k] = acc.astype(BF16)
        acc = None
        for e, (edge, b) in enumerate(((0, 0), (cols - 1, 2))):
            for a in range(3):
                part = jnp.where(col == edge, block[3 * a + b].astype(F32), 0.0).astype(BF16)
                part = nn(part, hot(rowc + (a + 64 * e) == lines))
                acc = part if acc is None else acc + part
        colout_ref[k] = acc.astype(BF16)


def corner_kernel(rows, cols, rowin_ref, left_ref, right_ref, up_ref, down_ref):
    lane = lax.broadcasted_iota(jnp.int32, up_ref.shape, 2)
    for e, (at, ref) in enumerate(((0, up_ref), (rows + 1, down_ref))):
        line = rowin_ref[e].astype(F32)
        line = line + jnp.where(lane == 0, left_ref[:, :, 64 + at : 65 + at].astype(F32), 0.0)
        line = line + jnp.where(
            lane == cols - 1, right_ref[:, :, at : at + 1].astype(F32), 0.0
        )
        ref[...] = line.astype(BF16)


def join_kernel(count, lev_ref, top_ref, bottom_ref, left_ref, right_ref, *outs):
    portion = top_ref.shape[1]
    spot = lax.broadcasted_iota(jnp.int32, (portion, 128), 1)
    each = count // len(outs)
    for k in range(count):
        out = outs[k // each].at[k % each]
        at = place(lev_ref[0], count, k)
        out[0] = top_ref[at]
        out[1] = bottom_ref[at]
        side = jnp.where(spot < 64, right_ref[at].astype(F32), left_ref[at].astype(F32))
        out[2] = side.astype(BF16)


def fold_kernel(kept_ref, got_ref, mine_ref, pass_ref):
    mine_ref[...] = (kept_ref[0].astype(F32) + got_ref[0].astype(F32)).astype(BF16)
    pass_ref[...] = (kept_ref[1].astype(F32) + got_ref[1].astype(F32)).astype(BF16)


def relay_kernel(count, lev_ref, block_ref, got_ref, out_ref):
    keep = jnp.where(relays(lev_ref[0], count), 1.0, 0.0)
    out_ref[...] = (block_ref[...].astype(F32) + got_ref[...].astype(F32) * keep).astype(BF16)


def final_kernel(rows, cols, count, edges, lev_ref, index_ref, latent_ref, *rest):
    rims, own, relayed = rest[:edges], rest[edges], rest[edges + 1]
    parts = rest[edges + 2 : -7]
    out_ref, own_ref, sum_ref, edge_ref, wait_ref, sem, sems = rest[-7:]
    portion = out_ref.shape[0]
    fetch = pltpu.make_async_copy(
        latent_ref.at[pl.ds(pl.multiple_of(lev_ref[0] * portion, 8), portion)], own_ref, sem
    )
    fetch.start()
    row, _ = split(index_ref[...], cols)
    _, colc = split(upright(index_ref), cols)
    slots = row.shape[1]
    total = rims[0][...].astype(F32)
    for block in rims[1:]:
        total = total + block[...].astype(F32)
    edge_ref[...] = total
    cells = lax.broadcasted_iota(jnp.int32, (slots, cols), 1)
    lane = lax.broadcasted_iota(jnp.int32, (128, cols), 0)
    spot = lax.broadcasted_iota(jnp.int32, (128, cols), 1)
    ends = hot(((lane < 64) & (spot == cols - 1)) | ((lane >= 64) & (spot == 0)))
    hots = jnp.concatenate([hot(colc + (b - 1) == cells) for b in range(3)] + [ends], 0)
    lines = lax.broadcasted_iota(jnp.int32, (rows, slots), 0)
    masks = [row + (a - 1) == lines for a in range(3)]
    place_of = lax.broadcasted_iota(jnp.int32, (rows, 128), 1)
    line_of = lax.broadcasted_iota(jnp.int32, (rows, 128), 0)
    picks = (place_of == line_of + 1) | (place_of == line_of + 65)
    high = lax.broadcasted_iota(jnp.int32, (rows, cols), 0)
    keep = jnp.where(relays(lev_ref[0], count), 0.0, 1.0)
    step = sum_ref.shape[2]
    outs = []
    fetch.wait()
    for i, c0 in enumerate(range(0, portion, step)):
        span = slice(c0, c0 + step)
        total = own[:, span, :].astype(F32) + relayed[:, span, :].astype(F32) * keep
        for block in parts:
            total = total + block[:, span, :].astype(F32)
        sum_ref[i] = total
        lefts = []
        for c in range(step):
            pieces = []
            for b in range(3):
                part = jnp.zeros((rows, slots), F32)
                for a in range(3):
                    values = jnp.broadcast_to(sum_ref[i, 3 * a + b, c : c + 1, :], (rows, slots))
                    part = jnp.where(masks[a], values, part)
                pieces.append(part.astype(BF16))
            side = jnp.broadcast_to(edge_ref[2, c0 + c : c0 + c + 1, :], (rows, 128))
            pieces.append(jnp.where(picks, side, 0.0).astype(BF16))
            lefts.append(jnp.concatenate(pieces, 1))
        acc = nn(jnp.concatenate(lefts, 0), hots)
        for c in range(step):
            field = acc[c * rows : (c + 1) * rows] + own_ref[c0 + c].astype(F32)
            above = jnp.broadcast_to(edge_ref[0, c0 + c : c0 + c + 1, :], (rows, cols))
            below = jnp.broadcast_to(edge_ref[1, c0 + c : c0 + c + 1, :], (rows, cols))
            edge = jnp.where(high == 0, above, jnp.where(high == rows - 1, below, 0.0))
            wait_ref[c0 + c] = field + edge
        out = pltpu.make_async_copy(wait_ref.at[span], out_ref.at[span], sems.at[i])
        out.start()
        outs.append(out)
    for out in outs:
        out.wait()


def shift(x, axis, by, wrap=True):
    size = lax.axis_size(axis)
    pairs = [(i, (i + by) % size) for i in range(size) if wrap or 0 <= i + by < size]
    return lax.ppermute(x, axis, pairs)


def paired(x, k):
    return lax.ppermute(x, "lev", [(i, i ^ k) for i in range(4)])


def from_sides(x, axis):
    if lax.axis_size(axis) == 2:
        other = shift(x, axis, 1)
        return other, other
    return shift(x, axis, 1), shift(x, axis, -1)


def steps(
    latent,
    conv_weight,
    mid_weight,
    out_weight,
    inner,
    outer,
    obs_values,
    obs_weight,
    obs_index,
    obs_count,
):
    chans, rows, cols = latent.shape
    groups, hidden, taps, _ = conv_weight.shape
    levels = out_weight.shape[1]
    slots = obs_index.shape[-1]
    own = groups * levels
    wide = groups * hidden
    lev_count = lax.axis_size("lev")
    lev = lax.axis_index("lev").astype(jnp.int32).reshape(1)
    portion = chans // lev_count
    index = obs_index.reshape(1, slots)
    far = pltpu.with_memory_space_constraint(latent, pltpu.MemorySpace.HBM)
    flops = 2 * taps * wide * chans * slots

    strip = jax.ShapeDtypeStruct((cols, chans), BF16)
    tile, top, bottom, ends = call(
        turn_kernel,
        (
            jax.ShapeDtypeStruct((rows * cols, chans), BF16),
            strip,
            strip,
            jax.ShapeDtypeStruct((2, rows, chans), BF16),
        ),
        [SM, HBM],
        flops // 4,
        16,
        scratch_shapes=[
            pltpu.VMEM((rows // 8, chans, 8, cols), BF16),
            pltpu.VMEM((rows // 8, chans * 8, cols), F32),
            pltpu.VMEM((2, rows, chans), F32),
            pltpu.SemaphoreType.DMA((rows // 8,)),
        ],
    )(lev, far)
    above = shift(bottom, "lat", 1, wrap=False)
    below = shift(top, "lat", -1, wrap=False)
    columns = jnp.stack(
        [
            jnp.concatenate([above[at : at + 1], ends[e], below[at : at + 1]], 0)
            for e, at in enumerate((0, cols - 1))
        ]
    )
    from_left, from_right = from_sides(columns, "lon")

    x = call(
        functools.partial(gather_kernel, rows, cols),
        jax.ShapeDtypeStruct((taps, slots, chans), BF16),
        [SM, VM, VM],
        flops,
        26,
        scratch_shapes=[
            pltpu.VMEM((((rows + 2) * cols + 16) * 8, 128), F32),
            pltpu.VMEM((3, slots * 8, 128), F32),
        ],
    )(index, index, tile)
    w = jnp.transpose(conv_weight, (2, 0, 1, 3)).reshape(taps, wide, chans)
    act_shape = jax.ShapeDtypeStruct((wide, slots), BF16)
    slope_one, slope_two, fields = call(
        functools.partial(decode_kernel, rows, cols),
        (act_shape, act_shape, jax.ShapeDtypeStruct((own, slots), BF16)),
        [VM] * 9,
        flops * 2,
        20,
        scratch_shapes=[pltpu.VMEM((2 * cols + 128, chans), BF16)],
    )(index, x, above, below, from_left, from_right, w, mid_weight, out_weight)

    blocks = [fields]
    for k in range(1, lev_count):
        blocks.append(paired(fields, k) if lev_count == 4 else shift(fields, "lev", -k))
    column_shape = jax.ShapeDtypeStruct((own * lev_count, slots), F32)
    turned = call(
        prepare_kernel,
        (
            column_shape,
            column_shape,
            jax.ShapeDtypeStruct((own, inner.shape[0]), BF16),
            jax.ShapeDtypeStruct((outer.shape[1], outer.shape[0]), BF16),
            jax.ShapeDtypeStruct((taps, chans, wide), BF16),
        ),
        [SM, SM] + [VM] * 5,
        flops,
        24,
        scratch_shapes=[pltpu.VMEM((inner.shape[1], inner.shape[0]), BF16)],
    )(lev, obs_count, obs_values[0, 0], obs_weight[None, :], inner, outer, w)
    obs_turned, scale, inner_turned, outer_turned, w_turned = turned

    patch_shape = jax.ShapeDtypeStruct((taps, portion, slots), BF16)
    patches = call(
        functools.partial(column_kernel, lev_count),
        (patch_shape,) * lev_count,
        [SM] + [VM] * (11 + lev_count),
        flops * 4,
        32,
        scratch_shapes=[
            pltpu.VMEM((own * lev_count, slots), BF16),
            pltpu.VMEM((own * lev_count, slots), F32),
        ],
    )(
        lev,
        inner,
        inner_turned,
        outer,
        outer_turned,
        obs_turned,
        scale,
        slope_one,
        slope_two,
        w_turned,
        mid_weight,
        out_weight,
        *blocks,
    )
    if lev_count == 4:
        relayed = lax.ppermute(patches[1], "lev", [(0, 1), (1, 0), (2, 3), (3, 2)])
        parts = [lax.ppermute(patches[2], "lev", [(1, 2), (2, 1)])]
        parts.append(lax.ppermute(patches[2], "lev", [(0, 2), (3, 1)]))
        passed = call(
            functools.partial(relay_kernel, lev_count), patch_shape, [SM, VM, VM], flops // 64, 8
        )(lev, patches[3], relayed)
        parts.append(lax.ppermute(passed, "lev", [(0, 1), (1, 3), (3, 2), (2, 0)]))
    else:
        parts = []
        for k in range(1, lev_count):
            parts.append(shift(patches[k], "lev", k))
        relayed = parts.pop(0)

    line_shape = jax.ShapeDtypeStruct((lev_count, portion, cols), BF16)
    side_shape = jax.ShapeDtypeStruct((lev_count, portion, 128), BF16)
    row_edge, col_edge = call(
        functools.partial(edge_kernel, rows, cols),
        (jax.ShapeDtypeStruct((2, lev_count, portion, cols), BF16), side_shape),
        [VM] * (1 + lev_count),
        flops // 8,
        12,
    )(index, *patches)
    from_left, from_right = from_sides(col_edge, "lon")
    up, down = call(
        functools.partial(corner_kernel, rows, cols),
        (line_shape, line_shape),
        [VM] * 3,
        flops // 64,
        8,
    )(row_edge, from_left, from_right)
    onto_first = shift(down, "lat", 1, wrap=False)
    onto_last = shift(up, "lat", -1, wrap=False)
    each = 2 if lev_count == 4 else 1
    joined = call(
        functools.partial(join_kernel, lev_count),
        (jax.ShapeDtypeStruct((each, 3, portion, 128), BF16),) * (lev_count // each),
        [SM] + [VM] * 4,
        flops // 64,
        12,
    )(lev, onto_first, onto_last, from_left, from_right)
    if lev_count == 4:
        got = paired(joined[1], 1)
        rim_shape = jax.ShapeDtypeStruct((3, portion, 128), BF16)
        kept, passing = call(fold_kernel, (rim_shape,) * 2, [VM] * 2, flops // 64, 8)(
            joined[0], got
        )
        rims = [kept, paired(passing, 2)]
    else:
        rims = [joined[0][0]]
        rims += [shift(joined[k], "lev", k)[0] for k in range(1, lev_count)]

    return call(
        functools.partial(final_kernel, rows, cols, lev_count, len(rims)),
        jax.ShapeDtypeStruct((portion, rows, cols), F32),
        [SM, VM, HBM] + [VM] * (2 + len(parts) + len(rims)),
        flops // 4,
        16,
        scratch_shapes=[
            pltpu.VMEM((portion, rows, cols), BF16),
            pltpu.VMEM((portion // STEP, taps, STEP, slots), F32),
            pltpu.VMEM((3, portion, 128), F32),
            pltpu.VMEM((portion, rows, cols), F32),
            pltpu.SemaphoreType.DMA,
            pltpu.SemaphoreType.DMA((portion // STEP,)),
        ],
        out_specs=HBM,
    )(lev, index, far, *rims, patches[0], relayed, *parts)


def solution(mesh):
    return jax.shard_map(
        steps,
        mesh=mesh,
        in_specs=(
            P(None, "lat", "lon"),
            P("lev", None, None, None),
            P("lev", None, None),
            P("lev", None, None),
            P(),
            P(),
            P("lat", "lon", None, None),
            P(),
            P("lat", "lon", None),
            P("lat", "lon"),
        ),
        out_specs=P("lev", "lat", "lon"),
        check_vma=False,
    )
```

```python
import functools

import jax
import jax.numpy as jnp
from jax import lax
from jax.experimental import pallas as pl
from jax.experimental.pallas import tpu as pltpu
from jax.sharding import PartitionSpec as P

KAPPA = 0.7978845608028654
CUBIC = 0.044715
F32 = jnp.float32
BF16 = jnp.bfloat16


def gelu_slope(pre):
    square = pre * pre
    tanh_v = jnp.tanh(KAPPA * (pre + CUBIC * square * pre))
    value = 0.5 * pre * (1.0 + tanh_v)
    slope = 0.5 * (1.0 + tanh_v) + 0.5 * pre * (1.0 - tanh_v * tanh_v) * KAPPA * (
        1.0 + 3.0 * CUBIC * square
    )
    return value, slope


def nn(a, b):
    return lax.dot_general(a, b, (((1,), (0,)), ((), ())), preferred_element_type=F32)


def nt(a, b):
    return lax.dot_general(a, b, (((1,), (1,)), ((), ())), preferred_element_type=F32)


def tn(a, b):
    return lax.dot_general(a, b, (((0,), (0,)), ((), ())), preferred_element_type=F32)


ROUTES = ((0, 3, 2, 1), (1, 0, 2, 3), (2, 3, 1, 0), (3, 0, 1, 2))


def lookup(lev, values):
    found = jnp.int32(values[0])
    for i, value in enumerate(values[1:], 1):
        found = jnp.where(lev == i, value, found)
    return found


def relays(lev, count):
    return (lev == 1) | (lev == 2) if count == 4 else lev < 0


def source(lev, count, k):
    return lax.bitwise_xor(lev, k) if count == 4 else lax.rem(lev + k, count)


def target(lev, count, k):
    if count == 4:
        return lookup(lev, [ROUTES[i][k] for i in range(4)])
    return lax.rem(lev + k, count)


def place(lev, count, k):
    if count == 4:
        return lookup(lev, [ROUTES[i].index(i ^ (0, 2, 1, 3)[k]) for i in range(4)])
    return k


def split(index, cols):
    if cols & (cols - 1):
        return index // cols, index % cols
    bits = cols.bit_length() - 1
    return index >> bits, index & (cols - 1)


def hot(mask):
    return mask.astype(F32).astype(BF16)


def upright(index_ref):
    slots = index_ref.shape[1]
    return jnp.broadcast_to(index_ref[...], (128, slots)).T


def call(kernel, out_shape, in_specs, flops, mib, out_specs=None, **kwargs):
    bytes_out = sum(s.size * s.dtype.itemsize for s in jax.tree.leaves(out_shape))
    return pl.pallas_call(
        kernel,
        out_shape=out_shape,
        in_specs=in_specs,
        out_specs=out_specs or jax.tree.map(lambda _: VM, out_shape),
        cost_estimate=pl.CostEstimate(
            flops=flops, bytes_accessed=4 * bytes_out, transcendentals=0
        ),
        compiler_params=pltpu.CompilerParams(vmem_limit_bytes=mib << 20),
        **kwargs,
    )


STEP = 8

VM = pl.BlockSpec(memory_space=pltpu.VMEM)
SM = pl.BlockSpec(memory_space=pltpu.SMEM)
HBM = pl.BlockSpec(memory_space=pltpu.MemorySpace.HBM)


def turn_kernel(
    _, lat_ref, tile_ref, top_ref, bottom_ref, side_ref, near_ref, wide_ref, keep_ref, sems
):
    chans, rows, cols = lat_ref.shape
    count = rows // 8
    copies = [
        pltpu.make_async_copy(lat_ref.at[:, pl.ds(8 * i, 8)], near_ref.at[i], sems.at[i])
        for i in range(count)
    ]
    for copy in copies:
        copy.start()
    for i, copy in enumerate(copies):
        copy.wait()
        wide_ref[i] = near_ref[i].reshape(chans * 8, cols).astype(F32)
        for r in range(8 * i, 8 * i + 8):
            line = wide_ref[i, pl.ds(r - 8 * i, chans, stride=8), :].astype(BF16).T
            tile_ref[r * cols : (r + 1) * cols, :] = line
            keep_ref[0, r : r + 1, :] = line[0:1].astype(F32)
            keep_ref[1, r : r + 1, :] = line[cols - 1 : cols].astype(F32)
            if r == 0:
                top_ref[...] = line
            if r == rows - 1:
                bottom_ref[...] = line
    side_ref[...] = keep_ref[...].astype(BF16)


def gather_kernel(rows, cols, index_sm, index_ref, tile_ref, out_ref, table_ref, x_ref):
    chans = tile_ref.shape[1]
    slots = index_ref.shape[1]
    halves = chans // 128
    lead = cols + 8
    size = table_ref.shape[0]
    margin = (lead + 1) * 8
    table_ref[0:margin, :] = jnp.zeros((margin, 128), F32)
    table_ref[size - margin : size, :] = jnp.zeros((margin, 128), F32)
    for r in range(rows):
        line = tile_ref[r * cols : (r + 1) * cols, :].astype(F32)
        for b in range(3):
            for h in range(halves):
                at = (lead + r * cols - b + 1) * 8 + halves * b + h
                table_ref[pl.ds(at, cols, stride=8), :] = line[:, h * 128 : (h + 1) * 128]

    def body(i, carry):
        for j in range(8):
            s = i * 8 + j
            base = (index_sm[0, s] + (lead - cols)) * 8
            for a in range(3):
                x_ref[a, pl.ds(pl.multiple_of(s * 8, 8), 8), :] = table_ref[
                    pl.ds(pl.multiple_of(base + a * cols * 8, 8), 8), :
                ]
        return carry

    lax.fori_loop(0, slots // 8, body, 0)
    _, col = split(upright(index_ref), cols)
    for a in range(3):
        for b in range(3):
            for h in range(halves):
                x = x_ref[a, pl.ds(halves * b + h, slots, stride=8), :]
                if b != 1:
                    x = jnp.where(col == (0 if b == 0 else cols - 1), 0.0, x)
                out_ref[3 * a + b, :, h * 128 : (h + 1) * 128] = x.astype(BF16)


def decode_kernel(
    rows,
    cols,
    index_ref,
    x_ref,
    above_ref,
    below_ref,
    left_ref,
    right_ref,
    w_ref,
    mid_ref,
    outw_ref,
    s1_ref,
    s2_ref,
    field_ref,
    halo_ref,
):
    slots = index_ref.shape[1]
    groups, hidden, _ = mid_ref.shape
    levels = outw_ref.shape[1]
    width = halo_ref.shape[0]
    tall = (width - 2 * cols) // 2
    halo_ref[...] = jnp.zeros_like(halo_ref)
    halo_ref[0:cols, :] = above_ref[...]
    halo_ref[cols : 2 * cols, :] = below_ref[...]
    halo_ref[2 * cols : 2 * cols + rows + 2, :] = left_ref[1]
    halo_ref[2 * cols + tall : 2 * cols + tall + rows + 2, :] = right_ref[0]
    row, col = split(upright(index_ref), cols)
    cells = lax.broadcasted_iota(jnp.int32, (slots, width), 1)
    lefts, rights = [], []
    for a in range(3):
        for b in range(3):
            at_row, at_col = row + (a - 1), col + (b - 1)
            rim = jnp.where(at_row < 0, at_col, jnp.where(at_row >= rows, cols + at_col, -1))
            rim = jnp.where(at_col < 0, 2 * cols + at_row + 1, rim)
            rim = jnp.where(at_col >= cols, 2 * cols + tall + at_row + 1, rim)
            rim = jnp.concatenate([rim] * (width // 128), 1)
            x = x_ref[3 * a + b] + nn(hot(cells == rim), halo_ref[...]).astype(BF16)
            lefts.append(w_ref[3 * a + b])
            rights.append(x)
    acc = nt(jnp.concatenate(lefts, 1), jnp.concatenate(rights, 1))
    act, slope = gelu_slope(acc)
    s1_ref[...] = slope.astype(BF16)
    act = act.astype(BF16)
    for g in range(groups):
        two = nn(mid_ref[g], act[g * hidden : (g + 1) * hidden])
        value, slope = gelu_slope(two)
        s2_ref[g * hidden : (g + 1) * hidden, :] = slope.astype(BF16)
        field_ref[g * levels : (g + 1) * levels, :] = nn(
            outw_ref[g], value.astype(BF16)
        ).astype(BF16)


def prepare_kernel(
    lev_ref,
    count_ref,
    latent_ref,
    obs_ref,
    weight_ref,
    inner_ref,
    outer_ref,
    w_ref,
    obst_ref,
    scale_ref,
    innert_ref,
    outert_ref,
    wt_ref,
    own_ref,
    turn_ref,
    sem,
):
    portion = own_ref.shape[0]
    fetch = pltpu.make_async_copy(
        latent_ref.at[pl.ds(pl.multiple_of(lev_ref[0] * portion, 8), portion)], own_ref, sem
    )
    fetch.start()
    obst_ref[...] = obs_ref[...].T
    slots = obs_ref.shape[0]
    levels = weight_ref.shape[1]
    weight = jnp.broadcast_to(weight_ref[...], (128, levels)).T
    live = lax.broadcasted_iota(jnp.int32, (levels, 128), 1)
    for h in range(slots // 128):
        scale_ref[:, h * 128 : (h + 1) * 128] = jnp.where(
            live + h * 128 < count_ref[0, 0], weight, 0.0
        )
    turn_ref[...] = inner_ref[...].T
    own = innert_ref.shape[0]
    innert_ref[...] = turn_ref[pl.ds(pl.multiple_of(lev_ref[0] * own, 16), own), :]
    outert_ref[...] = outer_ref[...].T
    for t in range(w_ref.shape[0]):
        wt_ref[t] = w_ref[t].T
    fetch.wait()


def column_kernel(
    lev_count,
    lev_ref,
    inner_ref,
    innert_ref,
    outer_ref,
    outert_ref,
    obst_ref,
    scale_ref,
    s1_ref,
    s2_ref,
    wt_ref,
    mid_ref,
    outw_ref,
    *rest,
):
    blocks = rest[:lev_count]
    outs = rest[lev_count : 2 * lev_count]
    f_ref, mis_ref = rest[2 * lev_count :]
    lev = lev_ref[0]
    own = blocks[0].shape[0]
    for k in range(lev_count):
        at = pl.multiple_of(source(lev, lev_count, k) * own, 16)
        f_ref[pl.ds(at, own), :] = blocks[k][...]
    wide = inner_ref.shape[0]
    fields = f_ref[...]
    acts, slopes = [], []
    for j in range(0, wide, 256):
        act, slope = gelu_slope(nn(inner_ref[j : j + 256, :], fields))
        acts.append(act.astype(BF16))
        slopes.append(slope)
    act = jnp.concatenate(acts, 0)
    misfits = []
    for j in range(0, own * lev_count, 256):
        forecast = f_ref[j : j + 256, :].astype(F32) + nn(outer_ref[j : j + 256, :], act)
        misfit = (forecast - obst_ref[j : j + 256, :]) * scale_ref[j : j + 256, :]
        mis_ref[j : j + 256, :] = misfit
        misfits.append(misfit.astype(BF16))
    misfit = jnp.concatenate(misfits, 0)
    grad_act = jnp.concatenate(
        [
            (nn(outert_ref[j : j + 256, :], misfit) * slopes[j // 256]).astype(BF16)
            for j in range(0, wide, 256)
        ],
        0,
    )
    mine = mis_ref[pl.ds(pl.multiple_of(lev * own, 16), own), :]
    grad_fields = (mine + nn(innert_ref[...], grad_act)).astype(BF16)
    groups, hidden, _ = mid_ref.shape
    levels = outw_ref.shape[1]
    ones = []
    for g in range(groups):
        span = slice(g * hidden, (g + 1) * hidden)
        two = (
            tn(outw_ref[g], grad_fields[g * levels : (g + 1) * levels]) * s2_ref[span, :].astype(F32)
        ).astype(BF16)
        ones.append((tn(mid_ref[g], two) * s1_ref[span, :].astype(F32)).astype(BF16))
    grad_one = jnp.concatenate(ones, 0)
    taps = wt_ref.shape[0]
    portion = wt_ref.shape[1] // lev_count
    for k in range(lev_count):
        at = pl.multiple_of(target(lev, lev_count, k) * portion, 16)
        left = jnp.concatenate([wt_ref[t, pl.ds(at, portion), :] for t in range(taps)], 0)
        outs[k][...] = nn(left, grad_one).astype(BF16).reshape(taps, portion, -1)


def edge_kernel(rows, cols, index_ref, *rest):
    blocks, (rowout_ref, colout_ref) = rest[:-2], rest[-2:]
    row, col = split(index_ref[...], cols)
    rowc, colc = split(upright(index_ref), cols)
    slots = row.shape[1]
    cells = lax.broadcasted_iota(jnp.int32, (slots, cols), 1)
    lines = lax.broadcasted_iota(jnp.int32, (slots, 128), 1)
    for k, block in enumerate(blocks):
        for e, (edge, a) in enumerate(((0, 0), (rows - 1, 2))):
            acc = None
            for b in range(3):
                part = jnp.where(row == edge, block[3 * a + b].astype(F32), 0.0).astype(BF16)
                part = nn(part, hot(colc + (b - 1) == cells))
                acc = part if acc is None else acc + part
            rowout_ref[e, k] = acc.astype(BF16)
        acc = None
        for e, (edge, b) in enumerate(((0, 0), (cols - 1, 2))):
            for a in range(3):
                part = jnp.where(col == edge, block[3 * a + b].astype(F32), 0.0).astype(BF16)
                part = nn(part, hot(rowc + (a + 64 * e) == lines))
                acc = part if acc is None else acc + part
        colout_ref[k] = acc.astype(BF16)


def corner_kernel(rows, cols, rowin_ref, left_ref, right_ref, up_ref, down_ref):
    lane = lax.broadcasted_iota(jnp.int32, up_ref.shape, 2)
    for e, (at, ref) in enumerate(((0, up_ref), (rows + 1, down_ref))):
        line = rowin_ref[e].astype(F32)
        line = line + jnp.where(lane == 0, left_ref[:, :, 64 + at : 65 + at].astype(F32), 0.0)
        line = line + jnp.where(
            lane == cols - 1, right_ref[:, :, at : at + 1].astype(F32), 0.0
        )
        ref[...] = line.astype(BF16)


def join_kernel(count, lev_ref, top_ref, bottom_ref, left_ref, right_ref, *outs):
    portion = top_ref.shape[1]
    spot = lax.broadcasted_iota(jnp.int32, (portion, 128), 1)
    each = count // len(outs)
    for k in range(count):
        out = outs[k // each].at[k % each]
        at = place(lev_ref[0], count, k)
        out[0] = top_ref[at]
        out[1] = bottom_ref[at]
        side = jnp.where(spot < 64, right_ref[at].astype(F32), left_ref[at].astype(F32))
        out[2] = side.astype(BF16)


def fold_kernel(kept_ref, got_ref, mine_ref, pass_ref):
    mine_ref[...] = (kept_ref[0].astype(F32) + got_ref[0].astype(F32)).astype(BF16)
    pass_ref[...] = (kept_ref[1].astype(F32) + got_ref[1].astype(F32)).astype(BF16)


def relay_kernel(count, lev_ref, block_ref, got_ref, out_ref):
    keep = jnp.where(relays(lev_ref[0], count), 1.0, 0.0)
    out_ref[...] = (block_ref[...].astype(F32) + got_ref[...].astype(F32) * keep).astype(BF16)


def final_kernel(rows, cols, count, edges, lev_ref, index_ref, own_ref, *rest):
    rims, own, relayed = rest[:edges], rest[edges], rest[edges + 1]
    parts = rest[edges + 2 : -5]
    out_ref, sum_ref, edge_ref, wait_ref, sems = rest[-5:]
    portion = out_ref.shape[0]
    row, _ = split(index_ref[...], cols)
    _, colc = split(upright(index_ref), cols)
    slots = row.shape[1]
    total = rims[0][...].astype(F32)
    for block in rims[1:]:
        total = total + block[...].astype(F32)
    edge_ref[...] = total
    cells = lax.broadcasted_iota(jnp.int32, (slots, cols), 1)
    lane = lax.broadcasted_iota(jnp.int32, (128, cols), 0)
    spot = lax.broadcasted_iota(jnp.int32, (128, cols), 1)
    ends = hot(((lane < 64) & (spot == cols - 1)) | ((lane >= 64) & (spot == 0)))
    hots = jnp.concatenate([hot(colc + (b - 1) == cells) for b in range(3)] + [ends], 0)
    lines = lax.broadcasted_iota(jnp.int32, (rows, slots), 0)
    masks = [row + (a - 1) == lines for a in range(3)]
    place_of = lax.broadcasted_iota(jnp.int32, (rows, 128), 1)
    line_of = lax.broadcasted_iota(jnp.int32, (rows, 128), 0)
    picks = (place_of == line_of + 1) | (place_of == line_of + 65)
    high = lax.broadcasted_iota(jnp.int32, (rows, cols), 0)
    keep = jnp.where(relays(lev_ref[0], count), 0.0, 1.0)
    step = sum_ref.shape[2]
    outs = []
    for i, c0 in enumerate(range(0, portion, step)):
        span = slice(c0, c0 + step)
        total = own[:, span, :].astype(F32) + relayed[:, span, :].astype(F32) * keep
        for block in parts:
            total = total + block[:, span, :].astype(F32)
        sum_ref[i] = total
        lefts = []
        for c in range(step):
            pieces = []
            for b in range(3):
                part = jnp.zeros((rows, slots), F32)
                for a in range(3):
                    values = jnp.broadcast_to(sum_ref[i, 3 * a + b, c : c + 1, :], (rows, slots))
                    part = jnp.where(masks[a], values, part)
                pieces.append(part.astype(BF16))
            side = jnp.broadcast_to(edge_ref[2, c0 + c : c0 + c + 1, :], (rows, 128))
            pieces.append(jnp.where(picks, side, 0.0).astype(BF16))
            lefts.append(jnp.concatenate(pieces, 1))
        acc = nn(jnp.concatenate(lefts, 0), hots)
        for c in range(step):
            field = acc[c * rows : (c + 1) * rows] + own_ref[c0 + c].astype(F32)
            above = jnp.broadcast_to(edge_ref[0, c0 + c : c0 + c + 1, :], (rows, cols))
            below = jnp.broadcast_to(edge_ref[1, c0 + c : c0 + c + 1, :], (rows, cols))
            edge = jnp.where(high == 0, above, jnp.where(high == rows - 1, below, 0.0))
            wait_ref[c0 + c] = field + edge
        out = pltpu.make_async_copy(wait_ref.at[span], out_ref.at[span], sems.at[i])
        out.start()
        outs.append(out)
    for out in outs:
        out.wait()


def shift(x, axis, by, wrap=True):
    size = lax.axis_size(axis)
    pairs = [(i, (i + by) % size) for i in range(size) if wrap or 0 <= i + by < size]
    return lax.ppermute(x, axis, pairs)


def paired(x, k):
    return lax.ppermute(x, "lev", [(i, i ^ k) for i in range(4)])


def from_sides(x, axis):
    if lax.axis_size(axis) == 2:
        other = shift(x, axis, 1)
        return other, other
    return shift(x, axis, 1), shift(x, axis, -1)


def steps(
    latent,
    conv_weight,
    mid_weight,
    out_weight,
    inner,
    outer,
    obs_values,
    obs_weight,
    obs_index,
    obs_count,
):
    chans, rows, cols = latent.shape
    groups, hidden, taps, _ = conv_weight.shape
    levels = out_weight.shape[1]
    slots = obs_index.shape[-1]
    own = groups * levels
    wide = groups * hidden
    lev_count = lax.axis_size("lev")
    lev = lax.axis_index("lev").astype(jnp.int32).reshape(1)
    portion = chans // lev_count
    index = obs_index.reshape(1, slots)
    far = pltpu.with_memory_space_constraint(latent, pltpu.MemorySpace.HBM)
    flops = 2 * taps * wide * chans * slots

    strip = jax.ShapeDtypeStruct((cols, chans), BF16)
    tile, top, bottom, ends = call(
        turn_kernel,
        (
            jax.ShapeDtypeStruct((rows * cols, chans), BF16),
            strip,
            strip,
            jax.ShapeDtypeStruct((2, rows, chans), BF16),
        ),
        [SM, HBM],
        flops // 4,
        16,
        scratch_shapes=[
            pltpu.VMEM((rows // 8, chans, 8, cols), BF16),
            pltpu.VMEM((rows // 8, chans * 8, cols), F32),
            pltpu.VMEM((2, rows, chans), F32),
            pltpu.SemaphoreType.DMA((rows // 8,)),
        ],
    )(lev, far)
    above = shift(bottom, "lat", 1, wrap=False)
    below = shift(top, "lat", -1, wrap=False)
    columns = jnp.stack(
        [
            jnp.concatenate([above[at : at + 1], ends[e], below[at : at + 1]], 0)
            for e, at in enumerate((0, cols - 1))
        ]
    )
    from_left, from_right = from_sides(columns, "lon")

    x = call(
        functools.partial(gather_kernel, rows, cols),
        jax.ShapeDtypeStruct((taps, slots, chans), BF16),
        [SM, VM, VM],
        flops,
        26,
        scratch_shapes=[
            pltpu.VMEM((((rows + 2) * cols + 16) * 8, 128), F32),
            pltpu.VMEM((3, slots * 8, 128), F32),
        ],
    )(index, index, tile)
    w = jnp.transpose(conv_weight, (2, 0, 1, 3)).reshape(taps, wide, chans)
    act_shape = jax.ShapeDtypeStruct((wide, slots), BF16)
    slope_one, slope_two, fields = call(
        functools.partial(decode_kernel, rows, cols),
        (act_shape, act_shape, jax.ShapeDtypeStruct((own, slots), BF16)),
        [VM] * 9,
        flops * 2,
        20,
        scratch_shapes=[pltpu.VMEM((2 * cols + 128, chans), BF16)],
    )(index, x, above, below, from_left, from_right, w, mid_weight, out_weight)

    blocks = [fields]
    for k in range(1, lev_count):
        blocks.append(paired(fields, k) if lev_count == 4 else shift(fields, "lev", -k))
    column_shape = jax.ShapeDtypeStruct((own * lev_count, slots), F32)
    turned = call(
        prepare_kernel,
        (
            column_shape,
            column_shape,
            jax.ShapeDtypeStruct((own, inner.shape[0]), BF16),
            jax.ShapeDtypeStruct((outer.shape[1], outer.shape[0]), BF16),
            jax.ShapeDtypeStruct((taps, chans, wide), BF16),
            jax.ShapeDtypeStruct((portion, rows, cols), BF16),
        ),
        [SM, SM, HBM] + [VM] * 5,
        flops,
        24,
        scratch_shapes=[
            pltpu.VMEM((inner.shape[1], inner.shape[0]), BF16),
            pltpu.SemaphoreType.DMA,
        ],
    )(lev, obs_count, far, obs_values[0, 0], obs_weight[None, :], inner, outer, w)
    obs_turned, scale, inner_turned, outer_turned, w_turned, mine = turned

    patch_shape = jax.ShapeDtypeStruct((taps, portion, slots), BF16)
    patches = call(
        functools.partial(column_kernel, lev_count),
        (patch_shape,) * lev_count,
        [SM] + [VM] * (11 + lev_count),
        flops * 4,
        32,
        scratch_shapes=[
            pltpu.VMEM((own * lev_count, slots), BF16),
            pltpu.VMEM((own * lev_count, slots), F32),
        ],
    )(
        lev,
        inner,
        inner_turned,
        outer,
        outer_turned,
        obs_turned,
        scale,
        slope_one,
        slope_two,
        w_turned,
        mid_weight,
        out_weight,
        *blocks,
    )
    if lev_count == 4:
        relayed = lax.ppermute(patches[1], "lev", [(0, 1), (1, 0), (2, 3), (3, 2)])
        parts = [lax.ppermute(patches[2], "lev", [(1, 2), (2, 1)])]
        parts.append(lax.ppermute(patches[2], "lev", [(0, 2), (3, 1)]))
        passed = call(
            functools.partial(relay_kernel, lev_count), patch_shape, [SM, VM, VM], flops // 64, 8
        )(lev, patches[3], relayed)
        parts.append(lax.ppermute(passed, "lev", [(0, 1), (1, 3), (3, 2), (2, 0)]))
    else:
        parts = []
        for k in range(1, lev_count):
            parts.append(shift(patches[k], "lev", k))
        relayed = parts.pop(0)

    line_shape = jax.ShapeDtypeStruct((lev_count, portion, cols), BF16)
    side_shape = jax.ShapeDtypeStruct((lev_count, portion, 128), BF16)
    row_edge, col_edge = call(
        functools.partial(edge_kernel, rows, cols),
        (jax.ShapeDtypeStruct((2, lev_count, portion, cols), BF16), side_shape),
        [VM] * (1 + lev_count),
        flops // 8,
        12,
    )(index, *patches)
    from_left, from_right = from_sides(col_edge, "lon")
    up, down = call(
        functools.partial(corner_kernel, rows, cols),
        (line_shape, line_shape),
        [VM] * 3,
        flops // 64,
        8,
    )(row_edge, from_left, from_right)
    onto_first = shift(down, "lat", 1, wrap=False)
    onto_last = shift(up, "lat", -1, wrap=False)
    each = 2 if lev_count == 4 else 1
    joined = call(
        functools.partial(join_kernel, lev_count),
        (jax.ShapeDtypeStruct((each, 3, portion, 128), BF16),) * (lev_count // each),
        [SM] + [VM] * 4,
        flops // 64,
        12,
    )(lev, onto_first, onto_last, from_left, from_right)
    if lev_count == 4:
        got = paired(joined[1], 1)
        rim_shape = jax.ShapeDtypeStruct((3, portion, 128), BF16)
        kept, passing = call(fold_kernel, (rim_shape,) * 2, [VM] * 2, flops // 64, 8)(
            joined[0], got
        )
        rims = [kept, paired(passing, 2)]
    else:
        rims = [joined[0][0]]
        rims += [shift(joined[k], "lev", k)[0] for k in range(1, lev_count)]

    return call(
        functools.partial(final_kernel, rows, cols, lev_count, len(rims)),
        jax.ShapeDtypeStruct((portion, rows, cols), F32),
        [SM, VM, VM] + [VM] * (2 + len(parts) + len(rims)),
        flops // 4,
        16,
        scratch_shapes=[
            pltpu.VMEM((portion // STEP, taps, STEP, slots), F32),
            pltpu.VMEM((3, portion, 128), F32),
            pltpu.VMEM((portion, rows, cols), F32),
            pltpu.SemaphoreType.DMA((portion // STEP,)),
        ],
        out_specs=HBM,
    )(lev, index, mine, *rims, patches[0], relayed, *parts)


def solution(mesh):
    return jax.shard_map(
        steps,
        mesh=mesh,
        in_specs=(
            P(None, "lat", "lon"),
            P("lev", None, None, None),
            P("lev", None, None),
            P("lev", None, None),
            P(),
            P(),
            P("lat", "lon", None, None),
            P(),
            P("lat", "lon", None),
            P("lat", "lon"),
        ),
        out_specs=P("lev", "lat", "lon"),
        check_vma=False,
    )
```

```python
import functools

import jax
import jax.numpy as jnp
from jax import lax
from jax.experimental import pallas as pl
from jax.experimental.pallas import tpu as pltpu
from jax.sharding import PartitionSpec as P

KAPPA = 0.7978845608028654
CUBIC = 0.044715
F32 = jnp.float32
BF16 = jnp.bfloat16


def gelu_slope(pre):
    square = pre * pre
    tanh_v = jnp.tanh(KAPPA * (pre + CUBIC * square * pre))
    value = 0.5 * pre * (1.0 + tanh_v)
    slope = 0.5 * (1.0 + tanh_v) + 0.5 * pre * (1.0 - tanh_v * tanh_v) * KAPPA * (
        1.0 + 3.0 * CUBIC * square
    )
    return value, slope


def nn(a, b):
    return lax.dot_general(a, b, (((1,), (0,)), ((), ())), preferred_element_type=F32)


def nt(a, b):
    return lax.dot_general(a, b, (((1,), (1,)), ((), ())), preferred_element_type=F32)


def tn(a, b):
    return lax.dot_general(a, b, (((0,), (0,)), ((), ())), preferred_element_type=F32)


ROUTES = ((0, 3, 2, 1), (1, 0, 2, 3), (2, 3, 1, 0), (3, 0, 1, 2))


def lookup(lev, values):
    found = jnp.int32(values[0])
    for i, value in enumerate(values[1:], 1):
        found = jnp.where(lev == i, value, found)
    return found


def relays(lev, count):
    return (lev == 1) | (lev == 2) if count == 4 else lev < 0


def source(lev, count, k):
    return lax.bitwise_xor(lev, k) if count == 4 else lax.rem(lev + k, count)


def target(lev, count, k):
    if count == 4:
        return lookup(lev, [ROUTES[i][k] for i in range(4)])
    return lax.rem(lev + k, count)


def place(lev, count, k):
    if count == 4:
        return lookup(lev, [ROUTES[i].index(i ^ (0, 2, 1, 3)[k]) for i in range(4)])
    return k


def split(index, cols):
    if cols & (cols - 1):
        return index // cols, index % cols
    bits = cols.bit_length() - 1
    return index >> bits, index & (cols - 1)


def hot(mask):
    return mask.astype(F32).astype(BF16)


def upright(index_ref):
    slots = index_ref.shape[1]
    return jnp.broadcast_to(index_ref[...], (128, slots)).T


def call(kernel, out_shape, in_specs, flops, mib, out_specs=None, **kwargs):
    bytes_out = sum(s.size * s.dtype.itemsize for s in jax.tree.leaves(out_shape))
    return pl.pallas_call(
        kernel,
        out_shape=out_shape,
        in_specs=in_specs,
        out_specs=out_specs or jax.tree.map(lambda _: VM, out_shape),
        cost_estimate=pl.CostEstimate(
            flops=flops, bytes_accessed=4 * bytes_out, transcendentals=0
        ),
        compiler_params=pltpu.CompilerParams(vmem_limit_bytes=mib << 20),
        **kwargs,
    )


STEP = 8

VM = pl.BlockSpec(memory_space=pltpu.VMEM)
SM = pl.BlockSpec(memory_space=pltpu.SMEM)
HBM = pl.BlockSpec(memory_space=pltpu.MemorySpace.HBM)


def turn_kernel(
    _, lat_ref, tile_ref, top_ref, bottom_ref, side_ref, near_ref, wide_ref, keep_ref, sems
):
    chans, rows, cols = lat_ref.shape
    count = rows // 8
    copies = [
        pltpu.make_async_copy(lat_ref.at[:, pl.ds(8 * i, 8)], near_ref.at[i], sems.at[i])
        for i in range(count)
    ]
    for copy in copies:
        copy.start()
    for i, copy in enumerate(copies):
        copy.wait()
        wide_ref[i] = near_ref[i].reshape(chans * 8, cols).astype(F32)
        for r in range(8 * i, 8 * i + 8):
            line = wide_ref[i, pl.ds(r - 8 * i, chans, stride=8), :].astype(BF16).T
            tile_ref[r * cols : (r + 1) * cols, :] = line
            keep_ref[0, r : r + 1, :] = line[0:1].astype(F32)
            keep_ref[1, r : r + 1, :] = line[cols - 1 : cols].astype(F32)
            if r == 0:
                top_ref[...] = line
            if r == rows - 1:
                bottom_ref[...] = line
    side_ref[...] = keep_ref[...].astype(BF16)


def gather_kernel(rows, cols, index_sm, index_ref, tile_ref, out_ref, table_ref, x_ref):
    chans = tile_ref.shape[1]
    slots = index_ref.shape[1]
    halves = chans // 128
    lead = cols + 8
    size = table_ref.shape[0]
    margin = (lead + 1) * 8
    table_ref[0:margin, :] = jnp.zeros((margin, 128), F32)
    table_ref[size - margin : size, :] = jnp.zeros((margin, 128), F32)
    for r in range(rows):
        line = tile_ref[r * cols : (r + 1) * cols, :].astype(F32)
        for b in range(3):
            for h in range(halves):
                at = (lead + r * cols - b + 1) * 8 + halves * b + h
                table_ref[pl.ds(at, cols, stride=8), :] = line[:, h * 128 : (h + 1) * 128]

    def body(i, carry):
        for j in range(8):
            s = i * 8 + j
            base = (index_sm[0, s] + (lead - cols)) * 8
            for a in range(3):
                x_ref[a, pl.ds(pl.multiple_of(s * 8, 8), 8), :] = table_ref[
                    pl.ds(pl.multiple_of(base + a * cols * 8, 8), 8), :
                ]
        return carry

    lax.fori_loop(0, slots // 8, body, 0)
    _, col = split(upright(index_ref), cols)
    for a in range(3):
        for b in range(3):
            for h in range(halves):
                x = x_ref[a, pl.ds(halves * b + h, slots, stride=8), :]
                if b != 1:
                    x = jnp.where(col == (0 if b == 0 else cols - 1), 0.0, x)
                out_ref[3 * a + b, :, h * 128 : (h + 1) * 128] = x.astype(BF16)


def decode_kernel(
    rows,
    cols,
    index_ref,
    x_ref,
    above_ref,
    below_ref,
    left_ref,
    right_ref,
    w_ref,
    mid_ref,
    outw_ref,
    s1_ref,
    s2_ref,
    field_ref,
    halo_ref,
):
    slots = index_ref.shape[1]
    groups, hidden, _ = mid_ref.shape
    levels = outw_ref.shape[1]
    width = halo_ref.shape[0]
    tall = (width - 2 * cols) // 2
    halo_ref[...] = jnp.zeros_like(halo_ref)
    halo_ref[0:cols, :] = above_ref[...]
    halo_ref[cols : 2 * cols, :] = below_ref[...]
    halo_ref[2 * cols : 2 * cols + rows + 2, :] = left_ref[1]
    halo_ref[2 * cols + tall : 2 * cols + tall + rows + 2, :] = right_ref[0]
    row, col = split(upright(index_ref), cols)
    starts = (0, cols, 2 * cols, width)
    cells = [
        lax.broadcasted_iota(jnp.int32, (slots, starts[i + 1] - starts[i]), 1) + starts[i]
        for i in range(3)
    ]
    lefts, rights = [], []
    for a in range(3):
        for b in range(3):
            at_row, at_col = row + (a - 1), col + (b - 1)
            rim = jnp.where(at_row < 0, at_col, jnp.where(at_row >= rows, cols + at_col, -1))
            rim = jnp.where(at_col < 0, 2 * cols + at_row + 1, rim)
            rim = jnp.where(at_col >= cols, 2 * cols + tall + at_row + 1, rim)
            x = x_ref[3 * a + b]
            reach = [i for i, near in enumerate((a == 0, a == 2, b != 1)) if near]
            if reach:
                picks, found = [], []
                for i in reach:
                    wide = jnp.concatenate([rim] * (cells[i].shape[1] // 128), 1)
                    picks.append(hot(cells[i] == wide))
                    found.append(halo_ref[starts[i] : starts[i + 1], :])
                picks, found = jnp.concatenate(picks, 1), jnp.concatenate(found, 0)
                x = x + nn(picks, found).astype(BF16)
            lefts.append(w_ref[3 * a + b])
            rights.append(x)
    acc = nt(jnp.concatenate(lefts, 1), jnp.concatenate(rights, 1))
    act, slope = gelu_slope(acc)
    s1_ref[...] = slope.astype(BF16)
    act = act.astype(BF16)
    for g in range(groups):
        two = nn(mid_ref[g], act[g * hidden : (g + 1) * hidden])
        value, slope = gelu_slope(two)
        s2_ref[g * hidden : (g + 1) * hidden, :] = slope.astype(BF16)
        field_ref[g * levels : (g + 1) * levels, :] = nn(
            outw_ref[g], value.astype(BF16)
        ).astype(BF16)


def prepare_kernel(
    lev_ref,
    count_ref,
    latent_ref,
    obs_ref,
    weight_ref,
    inner_ref,
    outer_ref,
    w_ref,
    obst_ref,
    scale_ref,
    innert_ref,
    outert_ref,
    wt_ref,
    own_ref,
    turn_ref,
    sem,
):
    portion = own_ref.shape[0]
    fetch = pltpu.make_async_copy(
        latent_ref.at[pl.ds(pl.multiple_of(lev_ref[0] * portion, 8), portion)], own_ref, sem
    )
    fetch.start()
    obst_ref[...] = obs_ref[...].T
    slots = obs_ref.shape[0]
    levels = weight_ref.shape[1]
    weight = jnp.broadcast_to(weight_ref[...], (128, levels)).T
    live = lax.broadcasted_iota(jnp.int32, (levels, 128), 1)
    for h in range(slots // 128):
        scale_ref[:, h * 128 : (h + 1) * 128] = jnp.where(
            live + h * 128 < count_ref[0, 0], weight, 0.0
        )
    turn_ref[...] = inner_ref[...].T
    own = innert_ref.shape[0]
    innert_ref[...] = turn_ref[pl.ds(pl.multiple_of(lev_ref[0] * own, 16), own), :]
    outert_ref[...] = outer_ref[...].T
    for t in range(w_ref.shape[0]):
        wt_ref[t] = w_ref[t].T
    fetch.wait()


def column_kernel(
    lev_count,
    lev_ref,
    inner_ref,
    innert_ref,
    outer_ref,
    outert_ref,
    obst_ref,
    scale_ref,
    s1_ref,
    s2_ref,
    wt_ref,
    mid_ref,
    outw_ref,
    *rest,
):
    blocks = rest[:lev_count]
    outs = rest[lev_count : 2 * lev_count]
    f_ref, mis_ref = rest[2 * lev_count :]
    lev = lev_ref[0]
    own = blocks[0].shape[0]
    for k in range(lev_count):
        at = pl.multiple_of(source(lev, lev_count, k) * own, 16)
        f_ref[pl.ds(at, own), :] = blocks[k][...]
    wide = inner_ref.shape[0]
    fields = f_ref[...]
    acts, slopes = [], []
    for j in range(0, wide, 256):
        act, slope = gelu_slope(nn(inner_ref[j : j + 256, :], fields))
        acts.append(act.astype(BF16))
        slopes.append(slope)
    act = jnp.concatenate(acts, 0)
    misfits = []
    for j in range(0, own * lev_count, 256):
        forecast = f_ref[j : j + 256, :].astype(F32) + nn(outer_ref[j : j + 256, :], act)
        misfit = (forecast - obst_ref[j : j + 256, :]) * scale_ref[j : j + 256, :]
        mis_ref[j : j + 256, :] = misfit
        misfits.append(misfit.astype(BF16))
    misfit = jnp.concatenate(misfits, 0)
    grad_act = jnp.concatenate(
        [
            (nn(outert_ref[j : j + 256, :], misfit) * slopes[j // 256]).astype(BF16)
            for j in range(0, wide, 256)
        ],
        0,
    )
    mine = mis_ref[pl.ds(pl.multiple_of(lev * own, 16), own), :]
    grad_fields = (mine + nn(innert_ref[...], grad_act)).astype(BF16)
    groups, hidden, _ = mid_ref.shape
    levels = outw_ref.shape[1]
    ones = []
    for g in range(groups):
        span = slice(g * hidden, (g + 1) * hidden)
        two = (
            tn(outw_ref[g], grad_fields[g * levels : (g + 1) * levels]) * s2_ref[span, :].astype(F32)
        ).astype(BF16)
        ones.append((tn(mid_ref[g], two) * s1_ref[span, :].astype(F32)).astype(BF16))
    grad_one = jnp.concatenate(ones, 0)
    taps = wt_ref.shape[0]
    portion = wt_ref.shape[1] // lev_count
    for k in range(lev_count):
        at = pl.multiple_of(target(lev, lev_count, k) * portion, 16)
        left = jnp.concatenate([wt_ref[t, pl.ds(at, portion), :] for t in range(taps)], 0)
        outs[k][...] = nn(left, grad_one).astype(BF16).reshape(taps, portion, -1)


def edge_kernel(rows, cols, index_ref, *rest):
    blocks, (rowout_ref, colout_ref) = rest[:-2], rest[-2:]
    row, col = split(index_ref[...], cols)
    rowc, colc = split(upright(index_ref), cols)
    slots = row.shape[1]
    cells = lax.broadcasted_iota(jnp.int32, (slots, cols), 1)
    lines = lax.broadcasted_iota(jnp.int32, (slots, 128), 1)
    portion = rowout_ref.shape[2]
    across = jnp.concatenate([hot(colc + (b - 1) == cells) for b in range(3)], 0)
    down = jnp.concatenate([hot(rowc + (a + 64 * e) == lines) for e in (0, 1) for a in range(3)], 0)

    def take(taps, where):
        return jnp.concatenate(
            [
                jnp.concatenate(
                    [jnp.where(where[i], block[t].astype(F32), 0.0).astype(BF16) for i, t in enumerate(taps)],
                    1,
                )
                for block in blocks
            ],
            0,
        )

    for e, (edge, a) in enumerate(((0, 0), (rows - 1, 2))):
        out = nn(take([3 * a + b for b in range(3)], [row == edge] * 3), across)
        rowout_ref[e] = out.astype(BF16).reshape(len(blocks), portion, cols)
    taps = [3 * a + b for b in (0, 2) for a in range(3)]
    out = nn(take(taps, [col == 0] * 3 + [col == cols - 1] * 3), down)
    colout_ref[...] = out.astype(BF16).reshape(len(blocks), portion, 128)


def corner_kernel(rows, cols, rowin_ref, left_ref, right_ref, up_ref, down_ref):
    lane = lax.broadcasted_iota(jnp.int32, up_ref.shape, 2)
    for e, (at, ref) in enumerate(((0, up_ref), (rows + 1, down_ref))):
        line = rowin_ref[e].astype(F32)
        line = line + jnp.where(lane == 0, left_ref[:, :, 64 + at : 65 + at].astype(F32), 0.0)
        line = line + jnp.where(
            lane == cols - 1, right_ref[:, :, at : at + 1].astype(F32), 0.0
        )
        ref[...] = line.astype(BF16)


def join_kernel(count, lev_ref, top_ref, bottom_ref, left_ref, right_ref, *outs):
    portion = top_ref.shape[1]
    spot = lax.broadcasted_iota(jnp.int32, (portion, 128), 1)
    each = count // len(outs)
    for k in range(count):
        out = outs[k // each].at[k % each]
        at = place(lev_ref[0], count, k)
        out[0] = top_ref[at]
        out[1] = bottom_ref[at]
        side = jnp.where(spot < 64, right_ref[at].astype(F32), left_ref[at].astype(F32))
        out[2] = side.astype(BF16)


def fold_kernel(kept_ref, got_ref, mine_ref, pass_ref):
    mine_ref[...] = (kept_ref[0].astype(F32) + got_ref[0].astype(F32)).astype(BF16)
    pass_ref[...] = (kept_ref[1].astype(F32) + got_ref[1].astype(F32)).astype(BF16)


def relay_kernel(count, lev_ref, block_ref, got_ref, out_ref):
    keep = jnp.where(relays(lev_ref[0], count), 1.0, 0.0)
    out_ref[...] = (block_ref[...].astype(F32) + got_ref[...].astype(F32) * keep).astype(BF16)


def final_kernel(rows, cols, count, edges, lev_ref, index_ref, own_ref, *rest):
    rims, own, relayed = rest[:edges], rest[edges], rest[edges + 1]
    parts = rest[edges + 2 : -5]
    out_ref, sum_ref, edge_ref, wait_ref, sems = rest[-5:]
    portion = out_ref.shape[0]
    row, _ = split(index_ref[...], cols)
    _, colc = split(upright(index_ref), cols)
    slots = row.shape[1]
    total = rims[0][...].astype(F32)
    for block in rims[1:]:
        total = total + block[...].astype(F32)
    edge_ref[...] = total
    cells = lax.broadcasted_iota(jnp.int32, (slots, cols), 1)
    lane = lax.broadcasted_iota(jnp.int32, (128, cols), 0)
    spot = lax.broadcasted_iota(jnp.int32, (128, cols), 1)
    ends = hot(((lane < 64) & (spot == cols - 1)) | ((lane >= 64) & (spot == 0)))
    hots = jnp.concatenate([hot(colc + (b - 1) == cells) for b in range(3)] + [ends], 0)
    lines = lax.broadcasted_iota(jnp.int32, (rows, slots), 0)
    masks = [row + (a - 1) == lines for a in range(3)]
    place_of = lax.broadcasted_iota(jnp.int32, (rows, 128), 1)
    line_of = lax.broadcasted_iota(jnp.int32, (rows, 128), 0)
    picks = (place_of == line_of + 1) | (place_of == line_of + 65)
    high = lax.broadcasted_iota(jnp.int32, (rows, cols), 0)
    keep = jnp.where(relays(lev_ref[0], count), 0.0, 1.0)
    step = sum_ref.shape[2]
    outs = []
    for i, c0 in enumerate(range(0, portion, step)):
        span = slice(c0, c0 + step)
        total = own[:, span, :].astype(F32) + relayed[:, span, :].astype(F32) * keep
        for block in parts:
            total = total + block[:, span, :].astype(F32)
        sum_ref[i] = total
        lefts = []
        for c in range(step):
            pieces = []
            for b in range(3):
                part = jnp.zeros((rows, slots), F32)
                for a in range(3):
                    values = jnp.broadcast_to(sum_ref[i, 3 * a + b, c : c + 1, :], (rows, slots))
                    part = jnp.where(masks[a], values, part)
                pieces.append(part.astype(BF16))
            side = jnp.broadcast_to(edge_ref[2, c0 + c : c0 + c + 1, :], (rows, 128))
            pieces.append(jnp.where(picks, side, 0.0).astype(BF16))
            lefts.append(jnp.concatenate(pieces, 1))
        acc = nn(jnp.concatenate(lefts, 0), hots)
        for c in range(step):
            field = acc[c * rows : (c + 1) * rows] + own_ref[c0 + c].astype(F32)
            above = jnp.broadcast_to(edge_ref[0, c0 + c : c0 + c + 1, :], (rows, cols))
            below = jnp.broadcast_to(edge_ref[1, c0 + c : c0 + c + 1, :], (rows, cols))
            edge = jnp.where(high == 0, above, jnp.where(high == rows - 1, below, 0.0))
            wait_ref[c0 + c] = field + edge
        out = pltpu.make_async_copy(wait_ref.at[span], out_ref.at[span], sems.at[i])
        out.start()
        outs.append(out)
    for out in outs:
        out.wait()


def shift(x, axis, by, wrap=True):
    size = lax.axis_size(axis)
    pairs = [(i, (i + by) % size) for i in range(size) if wrap or 0 <= i + by < size]
    return lax.ppermute(x, axis, pairs)


def paired(x, k):
    return lax.ppermute(x, "lev", [(i, i ^ k) for i in range(4)])


def from_sides(x, axis):
    if lax.axis_size(axis) == 2:
        other = shift(x, axis, 1)
        return other, other
    return shift(x, axis, 1), shift(x, axis, -1)


def steps(
    latent,
    conv_weight,
    mid_weight,
    out_weight,
    inner,
    outer,
    obs_values,
    obs_weight,
    obs_index,
    obs_count,
):
    chans, rows, cols = latent.shape
    groups, hidden, taps, _ = conv_weight.shape
    levels = out_weight.shape[1]
    slots = obs_index.shape[-1]
    own = groups * levels
    wide = groups * hidden
    lev_count = lax.axis_size("lev")
    lev = lax.axis_index("lev").astype(jnp.int32).reshape(1)
    portion = chans // lev_count
    index = obs_index.reshape(1, slots)
    far = pltpu.with_memory_space_constraint(latent, pltpu.MemorySpace.HBM)
    flops = 2 * taps * wide * chans * slots

    strip = jax.ShapeDtypeStruct((cols, chans), BF16)
    tile, top, bottom, ends = call(
        turn_kernel,
        (
            jax.ShapeDtypeStruct((rows * cols, chans), BF16),
            strip,
            strip,
            jax.ShapeDtypeStruct((2, rows, chans), BF16),
        ),
        [SM, HBM],
        flops // 4,
        16,
        scratch_shapes=[
            pltpu.VMEM((rows // 8, chans, 8, cols), BF16),
            pltpu.VMEM((rows // 8, chans * 8, cols), F32),
            pltpu.VMEM((2, rows, chans), F32),
            pltpu.SemaphoreType.DMA((rows // 8,)),
        ],
    )(lev, far)
    above = shift(bottom, "lat", 1, wrap=False)
    below = shift(top, "lat", -1, wrap=False)
    columns = jnp.stack(
        [
            jnp.concatenate([above[at : at + 1], ends[e], below[at : at + 1]], 0)
            for e, at in enumerate((0, cols - 1))
        ]
    )
    from_left, from_right = from_sides(columns, "lon")

    x = call(
        functools.partial(gather_kernel, rows, cols),
        jax.ShapeDtypeStruct((taps, slots, chans), BF16),
        [SM, VM, VM],
        flops,
        26,
        scratch_shapes=[
            pltpu.VMEM((((rows + 2) * cols + 16) * 8, 128), F32),
            pltpu.VMEM((3, slots * 8, 128), F32),
        ],
    )(index, index, tile)
    w = jnp.transpose(conv_weight, (2, 0, 1, 3)).reshape(taps, wide, chans)
    act_shape = jax.ShapeDtypeStruct((wide, slots), BF16)
    slope_one, slope_two, fields = call(
        functools.partial(decode_kernel, rows, cols),
        (act_shape, act_shape, jax.ShapeDtypeStruct((own, slots), BF16)),
        [VM] * 9,
        flops * 2,
        20,
        scratch_shapes=[pltpu.VMEM((2 * cols + 128, chans), BF16)],
    )(index, x, above, below, from_left, from_right, w, mid_weight, out_weight)

    blocks = [fields]
    for k in range(1, lev_count):
        blocks.append(paired(fields, k) if lev_count == 4 else shift(fields, "lev", -k))
    column_shape = jax.ShapeDtypeStruct((own * lev_count, slots), F32)
    turned = call(
        prepare_kernel,
        (
            column_shape,
            column_shape,
            jax.ShapeDtypeStruct((own, inner.shape[0]), BF16),
            jax.ShapeDtypeStruct((outer.shape[1], outer.shape[0]), BF16),
            jax.ShapeDtypeStruct((taps, chans, wide), BF16),
            jax.ShapeDtypeStruct((portion, rows, cols), BF16),
        ),
        [SM, SM, HBM] + [VM] * 5,
        flops,
        24,
        scratch_shapes=[
            pltpu.VMEM((inner.shape[1], inner.shape[0]), BF16),
            pltpu.SemaphoreType.DMA,
        ],
    )(lev, obs_count, far, obs_values[0, 0], obs_weight[None, :], inner, outer, w)
    obs_turned, scale, inner_turned, outer_turned, w_turned, mine = turned

    patch_shape = jax.ShapeDtypeStruct((taps, portion, slots), BF16)
    patches = call(
        functools.partial(column_kernel, lev_count),
        (patch_shape,) * lev_count,
        [SM] + [VM] * (11 + lev_count),
        flops * 4,
        32,
        scratch_shapes=[
            pltpu.VMEM((own * lev_count, slots), BF16),
            pltpu.VMEM((own * lev_count, slots), F32),
        ],
    )(
        lev,
        inner,
        inner_turned,
        outer,
        outer_turned,
        obs_turned,
        scale,
        slope_one,
        slope_two,
        w_turned,
        mid_weight,
        out_weight,
        *blocks,
    )
    if lev_count == 4:
        relayed = lax.ppermute(patches[1], "lev", [(0, 1), (1, 0), (2, 3), (3, 2)])
        parts = [lax.ppermute(patches[2], "lev", [(1, 2), (2, 1)])]
        parts.append(lax.ppermute(patches[2], "lev", [(0, 2), (3, 1)]))
        passed = call(
            functools.partial(relay_kernel, lev_count), patch_shape, [SM, VM, VM], flops // 64, 8
        )(lev, patches[3], relayed)
        parts.append(lax.ppermute(passed, "lev", [(0, 1), (1, 3), (3, 2), (2, 0)]))
    else:
        parts = []
        for k in range(1, lev_count):
            parts.append(shift(patches[k], "lev", k))
        relayed = parts.pop(0)

    line_shape = jax.ShapeDtypeStruct((lev_count, portion, cols), BF16)
    side_shape = jax.ShapeDtypeStruct((lev_count, portion, 128), BF16)
    row_edge, col_edge = call(
        functools.partial(edge_kernel, rows, cols),
        (jax.ShapeDtypeStruct((2, lev_count, portion, cols), BF16), side_shape),
        [VM] * (1 + lev_count),
        flops // 8,
        12,
    )(index, *patches)
    from_left, from_right = from_sides(col_edge, "lon")
    up, down = call(
        functools.partial(corner_kernel, rows, cols),
        (line_shape, line_shape),
        [VM] * 3,
        flops // 64,
        8,
    )(row_edge, from_left, from_right)
    onto_first = shift(down, "lat", 1, wrap=False)
    onto_last = shift(up, "lat", -1, wrap=False)
    each = 2 if lev_count == 4 else 1
    joined = call(
        functools.partial(join_kernel, lev_count),
        (jax.ShapeDtypeStruct((each, 3, portion, 128), BF16),) * (lev_count // each),
        [SM] + [VM] * 4,
        flops // 64,
        12,
    )(lev, onto_first, onto_last, from_left, from_right)
    if lev_count == 4:
        got = paired(joined[1], 1)
        rim_shape = jax.ShapeDtypeStruct((3, portion, 128), BF16)
        kept, passing = call(fold_kernel, (rim_shape,) * 2, [VM] * 2, flops // 64, 8)(
            joined[0], got
        )
        rims = [kept, paired(passing, 2)]
    else:
        rims = [joined[0][0]]
        rims += [shift(joined[k], "lev", k)[0] for k in range(1, lev_count)]

    return call(
        functools.partial(final_kernel, rows, cols, lev_count, len(rims)),
        jax.ShapeDtypeStruct((portion, rows, cols), F32),
        [SM, VM, VM] + [VM] * (2 + len(parts) + len(rims)),
        flops // 4,
        16,
        scratch_shapes=[
            pltpu.VMEM((portion // STEP, taps, STEP, slots), F32),
            pltpu.VMEM((3, portion, 128), F32),
            pltpu.VMEM((portion, rows, cols), F32),
            pltpu.SemaphoreType.DMA((portion // STEP,)),
        ],
        out_specs=HBM,
    )(lev, index, mine, *rims, patches[0], relayed, *parts)


def solution(mesh):
    return jax.shard_map(
        steps,
        mesh=mesh,
        in_specs=(
            P(None, "lat", "lon"),
            P("lev", None, None, None),
            P("lev", None, None),
            P("lev", None, None),
            P(),
            P(),
            P("lat", "lon", None, None),
            P(),
            P("lat", "lon", None),
            P("lat", "lon"),
        ),
        out_specs=P("lev", "lat", "lon"),
        check_vma=False,
    )
```

```python
import functools

import jax
import jax.numpy as jnp
from jax import lax
from jax.experimental import pallas as pl
from jax.experimental.pallas import tpu as pltpu
from jax.sharding import PartitionSpec as P

KAPPA = 0.7978845608028654
CUBIC = 0.044715
F32 = jnp.float32
BF16 = jnp.bfloat16


def gelu_slope(pre):
    square = pre * pre
    tanh_v = jnp.tanh(KAPPA * (pre + CUBIC * square * pre))
    value = 0.5 * pre * (1.0 + tanh_v)
    slope = 0.5 * (1.0 + tanh_v) + 0.5 * pre * (1.0 - tanh_v * tanh_v) * KAPPA * (
        1.0 + 3.0 * CUBIC * square
    )
    return value, slope


def nn(a, b):
    return lax.dot_general(a, b, (((1,), (0,)), ((), ())), preferred_element_type=F32)


def nt(a, b):
    return lax.dot_general(a, b, (((1,), (1,)), ((), ())), preferred_element_type=F32)


def tn(a, b):
    return lax.dot_general(a, b, (((0,), (0,)), ((), ())), preferred_element_type=F32)


ROUTES = ((0, 3, 2, 1), (1, 0, 2, 3), (2, 3, 1, 0), (3, 0, 1, 2))


def lookup(lev, values):
    found = jnp.int32(values[0])
    for i, value in enumerate(values[1:], 1):
        found = jnp.where(lev == i, value, found)
    return found


def relays(lev, count):
    return (lev == 1) | (lev == 2) if count == 4 else lev < 0


def source(lev, count, k):
    return lax.bitwise_xor(lev, k) if count == 4 else lax.rem(lev + k, count)


def target(lev, count, k):
    if count == 4:
        return lookup(lev, [ROUTES[i][k] for i in range(4)])
    return lax.rem(lev + k, count)


def place(lev, count, k):
    if count == 4:
        return lookup(lev, [ROUTES[i].index(i ^ (0, 2, 1, 3)[k]) for i in range(4)])
    return k


def split(index, cols):
    if cols & (cols - 1):
        return index // cols, index % cols
    bits = cols.bit_length() - 1
    return index >> bits, index & (cols - 1)


def hot(mask):
    return mask.astype(F32).astype(BF16)


def upright(index_ref):
    slots = index_ref.shape[1]
    return jnp.broadcast_to(index_ref[...], (128, slots)).T


def call(kernel, out_shape, in_specs, flops, mib, out_specs=None, **kwargs):
    bytes_out = sum(s.size * s.dtype.itemsize for s in jax.tree.leaves(out_shape))
    return pl.pallas_call(
        kernel,
        out_shape=out_shape,
        in_specs=in_specs,
        out_specs=out_specs or jax.tree.map(lambda _: VM, out_shape),
        cost_estimate=pl.CostEstimate(
            flops=flops, bytes_accessed=4 * bytes_out, transcendentals=0
        ),
        compiler_params=pltpu.CompilerParams(vmem_limit_bytes=mib << 20),
        **kwargs,
    )


STEP = 16

VM = pl.BlockSpec(memory_space=pltpu.VMEM)
SM = pl.BlockSpec(memory_space=pltpu.SMEM)
HBM = pl.BlockSpec(memory_space=pltpu.MemorySpace.HBM)


def turn_kernel(
    _, lat_ref, tile_ref, top_ref, bottom_ref, side_ref, near_ref, wide_ref, keep_ref, sems
):
    chans, rows, cols = lat_ref.shape
    count = rows // 8
    copies = [
        pltpu.make_async_copy(lat_ref.at[:, pl.ds(8 * i, 8)], near_ref.at[i], sems.at[i])
        for i in range(count)
    ]
    for copy in copies:
        copy.start()
    for i, copy in enumerate(copies):
        copy.wait()
        wide_ref[i] = near_ref[i].reshape(chans * 8, cols).astype(F32)
        for r in range(8 * i, 8 * i + 8):
            line = wide_ref[i, pl.ds(r - 8 * i, chans, stride=8), :].astype(BF16).T
            tile_ref[r * cols : (r + 1) * cols, :] = line
            keep_ref[0, r : r + 1, :] = line[0:1].astype(F32)
            keep_ref[1, r : r + 1, :] = line[cols - 1 : cols].astype(F32)
            if r == 0:
                top_ref[...] = line
            if r == rows - 1:
                bottom_ref[...] = line
    side_ref[...] = keep_ref[...].astype(BF16)


def gather_kernel(rows, cols, index_sm, index_ref, tile_ref, out_ref, table_ref, x_ref):
    chans = tile_ref.shape[1]
    slots = index_ref.shape[1]
    halves = chans // 128
    lead = cols + 8
    size = table_ref.shape[0]
    margin = (lead + 1) * 8
    table_ref[0:margin, :] = jnp.zeros((margin, 128), F32)
    table_ref[size - margin : size, :] = jnp.zeros((margin, 128), F32)
    for r in range(rows):
        line = tile_ref[r * cols : (r + 1) * cols, :].astype(F32)
        for b in range(3):
            for h in range(halves):
                at = (lead + r * cols - b + 1) * 8 + halves * b + h
                table_ref[pl.ds(at, cols, stride=8), :] = line[:, h * 128 : (h + 1) * 128]

    def body(i, carry):
        for j in range(8):
            s = i * 8 + j
            base = (index_sm[0, s] + (lead - cols)) * 8
            for a in range(3):
                x_ref[a, pl.ds(pl.multiple_of(s * 8, 8), 8), :] = table_ref[
                    pl.ds(pl.multiple_of(base + a * cols * 8, 8), 8), :
                ]
        return carry

    lax.fori_loop(0, slots // 8, body, 0)
    _, col = split(upright(index_ref), cols)
    for a in range(3):
        for b in range(3):
            for h in range(halves):
                x = x_ref[a, pl.ds(halves * b + h, slots, stride=8), :]
                if b != 1:
                    x = jnp.where(col == (0 if b == 0 else cols - 1), 0.0, x)
                out_ref[3 * a + b, :, h * 128 : (h + 1) * 128] = x.astype(BF16)


def decode_kernel(
    rows,
    cols,
    index_ref,
    x_ref,
    above_ref,
    below_ref,
    left_ref,
    right_ref,
    w_ref,
    mid_ref,
    outw_ref,
    s1_ref,
    s2_ref,
    field_ref,
    halo_ref,
):
    slots = index_ref.shape[1]
    groups, hidden, _ = mid_ref.shape
    levels = outw_ref.shape[1]
    width = halo_ref.shape[0]
    tall = (width - 2 * cols) // 2
    halo_ref[...] = jnp.zeros_like(halo_ref)
    halo_ref[0:cols, :] = above_ref[...]
    halo_ref[cols : 2 * cols, :] = below_ref[...]
    halo_ref[2 * cols : 2 * cols + rows + 2, :] = left_ref[1]
    halo_ref[2 * cols + tall : 2 * cols + tall + rows + 2, :] = right_ref[0]
    row, col = split(upright(index_ref), cols)
    starts = (0, cols, 2 * cols, width)
    cells = [
        lax.broadcasted_iota(jnp.int32, (slots, starts[i + 1] - starts[i]), 1) + starts[i]
        for i in range(3)
    ]
    lefts, rights = [], []
    for a in range(3):
        for b in range(3):
            at_row, at_col = row + (a - 1), col + (b - 1)
            rim = jnp.where(at_row < 0, at_col, jnp.where(at_row >= rows, cols + at_col, -1))
            rim = jnp.where(at_col < 0, 2 * cols + at_row + 1, rim)
            rim = jnp.where(at_col >= cols, 2 * cols + tall + at_row + 1, rim)
            x = x_ref[3 * a + b]
            reach = [i for i, near in enumerate((a == 0, a == 2, b != 1)) if near]
            if reach:
                picks, found = [], []
                for i in reach:
                    wide = jnp.concatenate([rim] * (cells[i].shape[1] // 128), 1)
                    picks.append(hot(cells[i] == wide))
                    found.append(halo_ref[starts[i] : starts[i + 1], :])
                picks, found = jnp.concatenate(picks, 1), jnp.concatenate(found, 0)
                x = x + nn(picks, found).astype(BF16)
            lefts.append(w_ref[3 * a + b])
            rights.append(x)
    acc = nt(jnp.concatenate(lefts, 1), jnp.concatenate(rights, 1))
    act, slope = gelu_slope(acc)
    s1_ref[...] = slope.astype(BF16)
    act = act.astype(BF16)
    for g in range(groups):
        two = nn(mid_ref[g], act[g * hidden : (g + 1) * hidden])
        value, slope = gelu_slope(two)
        s2_ref[g * hidden : (g + 1) * hidden, :] = slope.astype(BF16)
        field_ref[g * levels : (g + 1) * levels, :] = nn(
            outw_ref[g], value.astype(BF16)
        ).astype(BF16)


def prepare_kernel(
    lev_ref,
    count_ref,
    index_ref,
    latent_ref,
    obs_ref,
    weight_ref,
    inner_ref,
    outer_ref,
    w_ref,
    obst_ref,
    scale_ref,
    innert_ref,
    outert_ref,
    wt_ref,
    own_ref,
    across_ref,
    down_ref,
    turn_ref,
    sem,
):
    portion, _, cols = own_ref.shape
    rowc, colc = split(upright(index_ref), cols)
    count = index_ref.shape[1]
    cells = lax.broadcasted_iota(jnp.int32, (count, cols), 1)
    lines = lax.broadcasted_iota(jnp.int32, (count, 128), 1)
    for b in range(3):
        across_ref[b * count : (b + 1) * count, :] = hot(colc + (b - 1) == cells)
    for i, (e, a) in enumerate((e, a) for e in (0, 1) for a in range(3)):
        down_ref[i * count : (i + 1) * count, :] = hot(rowc + (a + 64 * e) == lines)
    fetch = pltpu.make_async_copy(
        latent_ref.at[pl.ds(pl.multiple_of(lev_ref[0] * portion, 8), portion)], own_ref, sem
    )
    fetch.start()
    obst_ref[...] = obs_ref[...].T
    slots = obs_ref.shape[0]
    levels = weight_ref.shape[1]
    weight = jnp.broadcast_to(weight_ref[...], (128, levels)).T
    live = lax.broadcasted_iota(jnp.int32, (levels, 128), 1)
    for h in range(slots // 128):
        scale_ref[:, h * 128 : (h + 1) * 128] = jnp.where(
            live + h * 128 < count_ref[0, 0], weight, 0.0
        )
    turn_ref[...] = inner_ref[...].T
    own = innert_ref.shape[0]
    innert_ref[...] = turn_ref[pl.ds(pl.multiple_of(lev_ref[0] * own, 16), own), :]
    outert_ref[...] = outer_ref[...].T
    for t in range(w_ref.shape[0]):
        wt_ref[t] = w_ref[t].T
    fetch.wait()


def column_kernel(
    lev_count,
    lev_ref,
    inner_ref,
    innert_ref,
    outer_ref,
    outert_ref,
    obst_ref,
    scale_ref,
    s1_ref,
    s2_ref,
    wt_ref,
    mid_ref,
    outw_ref,
    *rest,
):
    blocks = rest[:lev_count]
    outs = rest[lev_count : 2 * lev_count]
    f_ref, mis_ref = rest[2 * lev_count :]
    lev = lev_ref[0]
    own = blocks[0].shape[0]
    for k in range(lev_count):
        at = pl.multiple_of(source(lev, lev_count, k) * own, 16)
        f_ref[pl.ds(at, own), :] = blocks[k][...]
    wide = inner_ref.shape[0]
    fields = f_ref[...]
    acts, slopes = [], []
    for j in range(0, wide, 256):
        act, slope = gelu_slope(nn(inner_ref[j : j + 256, :], fields))
        acts.append(act.astype(BF16))
        slopes.append(slope)
    act = jnp.concatenate(acts, 0)
    misfits = []
    for j in range(0, own * lev_count, 256):
        forecast = f_ref[j : j + 256, :].astype(F32) + nn(outer_ref[j : j + 256, :], act)
        misfit = (forecast - obst_ref[j : j + 256, :]) * scale_ref[j : j + 256, :]
        mis_ref[j : j + 256, :] = misfit
        misfits.append(misfit.astype(BF16))
    misfit = jnp.concatenate(misfits, 0)
    grad_act = jnp.concatenate(
        [
            (nn(outert_ref[j : j + 256, :], misfit) * slopes[j // 256]).astype(BF16)
            for j in range(0, wide, 256)
        ],
        0,
    )
    mine = mis_ref[pl.ds(pl.multiple_of(lev * own, 16), own), :]
    grad_fields = (mine + nn(innert_ref[...], grad_act)).astype(BF16)
    groups, hidden, _ = mid_ref.shape
    levels = outw_ref.shape[1]
    ones = []
    for g in range(groups):
        span = slice(g * hidden, (g + 1) * hidden)
        two = (
            tn(outw_ref[g], grad_fields[g * levels : (g + 1) * levels]) * s2_ref[span, :].astype(F32)
        ).astype(BF16)
        ones.append((tn(mid_ref[g], two) * s1_ref[span, :].astype(F32)).astype(BF16))
    grad_one = jnp.concatenate(ones, 0)
    taps = wt_ref.shape[0]
    portion = wt_ref.shape[1] // lev_count
    for k in range(lev_count):
        at = pl.multiple_of(target(lev, lev_count, k) * portion, 16)
        left = jnp.concatenate([wt_ref[t, pl.ds(at, portion), :] for t in range(taps)], 0)
        outs[k][...] = nn(left, grad_one).astype(BF16).reshape(taps, portion, -1)


def edge_kernel(rows, cols, index_ref, across_ref, down_ref, *rest):
    blocks, (rowout_ref, colout_ref) = rest[:-2], rest[-2:]
    row, col = split(index_ref[...], cols)
    portion = rowout_ref.shape[2]

    def take(taps, where):
        return jnp.concatenate(
            [
                jnp.concatenate(
                    [jnp.where(where[i], block[t].astype(F32), 0.0).astype(BF16) for i, t in enumerate(taps)],
                    1,
                )
                for block in blocks
            ],
            0,
        )

    for e, (edge, a) in enumerate(((0, 0), (rows - 1, 2))):
        out = nn(take([3 * a + b for b in range(3)], [row == edge] * 3), across_ref[...])
        rowout_ref[e] = out.astype(BF16).reshape(len(blocks), portion, cols)
    taps = [3 * a + b for b in (0, 2) for a in range(3)]
    out = nn(take(taps, [col == 0] * 3 + [col == cols - 1] * 3), down_ref[...])
    colout_ref[...] = out.astype(BF16).reshape(len(blocks), portion, 128)


def corner_kernel(rows, cols, rowin_ref, left_ref, right_ref, up_ref, down_ref):
    lane = lax.broadcasted_iota(jnp.int32, up_ref.shape, 2)
    for e, (at, ref) in enumerate(((0, up_ref), (rows + 1, down_ref))):
        line = rowin_ref[e].astype(F32)
        line = line + jnp.where(lane == 0, left_ref[:, :, 64 + at : 65 + at].astype(F32), 0.0)
        line = line + jnp.where(
            lane == cols - 1, right_ref[:, :, at : at + 1].astype(F32), 0.0
        )
        ref[...] = line.astype(BF16)


def join_kernel(count, lev_ref, top_ref, bottom_ref, left_ref, right_ref, *outs):
    portion = top_ref.shape[1]
    spot = lax.broadcasted_iota(jnp.int32, (portion, 128), 1)
    each = count // len(outs)
    for k in range(count):
        out = outs[k // each].at[k % each]
        at = place(lev_ref[0], count, k)
        out[0] = top_ref[at]
        out[1] = bottom_ref[at]
        side = jnp.where(spot < 64, right_ref[at].astype(F32), left_ref[at].astype(F32))
        out[2] = side.astype(BF16)


def fold_kernel(kept_ref, got_ref, mine_ref, pass_ref):
    mine_ref[...] = (kept_ref[0].astype(F32) + got_ref[0].astype(F32)).astype(BF16)
    pass_ref[...] = (kept_ref[1].astype(F32) + got_ref[1].astype(F32)).astype(BF16)


def relay_kernel(count, lev_ref, block_ref, got_ref, out_ref):
    keep = jnp.where(relays(lev_ref[0], count), 1.0, 0.0)
    out_ref[...] = (block_ref[...].astype(F32) + got_ref[...].astype(F32) * keep).astype(BF16)


def final_kernel(rows, cols, count, edges, lev_ref, index_ref, own_ref, across_ref, *rest):
    rims, own, relayed = rest[:edges], rest[edges], rest[edges + 1]
    parts = rest[edges + 2 : -5]
    out_ref, sum_ref, edge_ref, wait_ref, sems = rest[-5:]
    portion = out_ref.shape[0]
    row, _ = split(index_ref[...], cols)
    slots = row.shape[1]
    total = rims[0][...].astype(F32)
    for block in rims[1:]:
        total = total + block[...].astype(F32)
    edge_ref[...] = total
    lane = lax.broadcasted_iota(jnp.int32, (128, cols), 0)
    spot = lax.broadcasted_iota(jnp.int32, (128, cols), 1)
    ends = hot(((lane < 64) & (spot == cols - 1)) | ((lane >= 64) & (spot == 0)))
    hots = jnp.concatenate([across_ref[...], ends], 0)
    lines = lax.broadcasted_iota(jnp.int32, (rows, slots), 0)
    masks = [row + (a - 1) == lines for a in range(3)]
    place_of = lax.broadcasted_iota(jnp.int32, (rows, 128), 1)
    line_of = lax.broadcasted_iota(jnp.int32, (rows, 128), 0)
    picks = (place_of == line_of + 1) | (place_of == line_of + 65)
    high = lax.broadcasted_iota(jnp.int32, (rows, cols), 0)
    keep = jnp.where(relays(lev_ref[0], count), 0.0, 1.0)
    step = sum_ref.shape[2]
    outs = []
    for i, c0 in enumerate(range(0, portion, step)):
        span = slice(c0, c0 + step)
        total = own[:, span, :].astype(F32) + relayed[:, span, :].astype(F32) * keep
        for block in parts:
            total = total + block[:, span, :].astype(F32)
        sum_ref[i] = total
        lefts = []
        for c in range(step):
            pieces = []
            for b in range(3):
                part = jnp.zeros((rows, slots), F32)
                for a in range(3):
                    values = jnp.broadcast_to(sum_ref[i, 3 * a + b, c : c + 1, :], (rows, slots))
                    part = jnp.where(masks[a], values, part)
                pieces.append(part.astype(BF16))
            side = jnp.broadcast_to(edge_ref[2, c0 + c : c0 + c + 1, :], (rows, 128))
            pieces.append(jnp.where(picks, side, 0.0).astype(BF16))
            lefts.append(jnp.concatenate(pieces, 1))
        acc = nn(jnp.concatenate(lefts, 0), hots)
        for c in range(step):
            field = acc[c * rows : (c + 1) * rows] + own_ref[c0 + c].astype(F32)
            above = jnp.broadcast_to(edge_ref[0, c0 + c : c0 + c + 1, :], (rows, cols))
            below = jnp.broadcast_to(edge_ref[1, c0 + c : c0 + c + 1, :], (rows, cols))
            edge = jnp.where(high == 0, above, jnp.where(high == rows - 1, below, 0.0))
            wait_ref[c0 + c] = field + edge
        out = pltpu.make_async_copy(wait_ref.at[span], out_ref.at[span], sems.at[i])
        out.start()
        outs.append(out)
    for out in outs:
        out.wait()


def shift(x, axis, by, wrap=True):
    size = lax.axis_size(axis)
    pairs = [(i, (i + by) % size) for i in range(size) if wrap or 0 <= i + by < size]
    return lax.ppermute(x, axis, pairs)


def paired(x, k):
    return lax.ppermute(x, "lev", [(i, i ^ k) for i in range(4)])


def from_sides(x, axis):
    if lax.axis_size(axis) == 2:
        other = shift(x, axis, 1)
        return other, other
    return shift(x, axis, 1), shift(x, axis, -1)


def steps(
    latent,
    conv_weight,
    mid_weight,
    out_weight,
    inner,
    outer,
    obs_values,
    obs_weight,
    obs_index,
    obs_count,
):
    chans, rows, cols = latent.shape
    groups, hidden, taps, _ = conv_weight.shape
    levels = out_weight.shape[1]
    slots = obs_index.shape[-1]
    own = groups * levels
    wide = groups * hidden
    lev_count = lax.axis_size("lev")
    lev = lax.axis_index("lev").astype(jnp.int32).reshape(1)
    portion = chans // lev_count
    index = obs_index.reshape(1, slots)
    far = pltpu.with_memory_space_constraint(latent, pltpu.MemorySpace.HBM)
    flops = 2 * taps * wide * chans * slots

    strip = jax.ShapeDtypeStruct((cols, chans), BF16)
    tile, top, bottom, ends = call(
        turn_kernel,
        (
            jax.ShapeDtypeStruct((rows * cols, chans), BF16),
            strip,
            strip,
            jax.ShapeDtypeStruct((2, rows, chans), BF16),
        ),
        [SM, HBM],
        flops // 4,
        16,
        scratch_shapes=[
            pltpu.VMEM((rows // 8, chans, 8, cols), BF16),
            pltpu.VMEM((rows // 8, chans * 8, cols), F32),
            pltpu.VMEM((2, rows, chans), F32),
            pltpu.SemaphoreType.DMA((rows // 8,)),
        ],
    )(lev, far)
    above = shift(bottom, "lat", 1, wrap=False)
    below = shift(top, "lat", -1, wrap=False)
    columns = jnp.stack(
        [
            jnp.concatenate([above[at : at + 1], ends[e], below[at : at + 1]], 0)
            for e, at in enumerate((0, cols - 1))
        ]
    )
    from_left, from_right = from_sides(columns, "lon")

    x = call(
        functools.partial(gather_kernel, rows, cols),
        jax.ShapeDtypeStruct((taps, slots, chans), BF16),
        [SM, VM, VM],
        flops,
        26,
        scratch_shapes=[
            pltpu.VMEM((((rows + 2) * cols + 16) * 8, 128), F32),
            pltpu.VMEM((3, slots * 8, 128), F32),
        ],
    )(index, index, tile)
    w = jnp.transpose(conv_weight, (2, 0, 1, 3)).reshape(taps, wide, chans)
    act_shape = jax.ShapeDtypeStruct((wide, slots), BF16)
    slope_one, slope_two, fields = call(
        functools.partial(decode_kernel, rows, cols),
        (act_shape, act_shape, jax.ShapeDtypeStruct((own, slots), BF16)),
        [VM] * 9,
        flops * 2,
        20,
        scratch_shapes=[pltpu.VMEM((2 * cols + 128, chans), BF16)],
    )(index, x, above, below, from_left, from_right, w, mid_weight, out_weight)

    blocks = [fields]
    for k in range(1, lev_count):
        blocks.append(paired(fields, k) if lev_count == 4 else shift(fields, "lev", -k))
    column_shape = jax.ShapeDtypeStruct((own * lev_count, slots), F32)
    turned = call(
        prepare_kernel,
        (
            column_shape,
            column_shape,
            jax.ShapeDtypeStruct((own, inner.shape[0]), BF16),
            jax.ShapeDtypeStruct((outer.shape[1], outer.shape[0]), BF16),
            jax.ShapeDtypeStruct((taps, chans, wide), BF16),
            jax.ShapeDtypeStruct((portion, rows, cols), BF16),
            jax.ShapeDtypeStruct((3 * slots, cols), BF16),
            jax.ShapeDtypeStruct((6 * slots, 128), BF16),
        ),
        [SM, SM, VM, HBM] + [VM] * 5,
        flops,
        24,
        scratch_shapes=[
            pltpu.VMEM((inner.shape[1], inner.shape[0]), BF16),
            pltpu.SemaphoreType.DMA,
        ],
    )(lev, obs_count, index, far, obs_values[0, 0], obs_weight[None, :], inner, outer, w)
    obs_turned, scale, inner_turned, outer_turned, w_turned, mine, across, down = turned

    patch_shape = jax.ShapeDtypeStruct((taps, portion, slots), BF16)
    patches = call(
        functools.partial(column_kernel, lev_count),
        (patch_shape,) * lev_count,
        [SM] + [VM] * (11 + lev_count),
        flops * 4,
        32,
        scratch_shapes=[
            pltpu.VMEM((own * lev_count, slots), BF16),
            pltpu.VMEM((own * lev_count, slots), F32),
        ],
    )(
        lev,
        inner,
        inner_turned,
        outer,
        outer_turned,
        obs_turned,
        scale,
        slope_one,
        slope_two,
        w_turned,
        mid_weight,
        out_weight,
        *blocks,
    )
    if lev_count == 4:
        relayed = lax.ppermute(patches[1], "lev", [(0, 1), (1, 0), (2, 3), (3, 2)])
        parts = [lax.ppermute(patches[2], "lev", [(1, 2), (2, 1)])]
        parts.append(lax.ppermute(patches[2], "lev", [(0, 2), (3, 1)]))
        passed = call(
            functools.partial(relay_kernel, lev_count), patch_shape, [SM, VM, VM], flops // 64, 8
        )(lev, patches[3], relayed)
        parts.append(lax.ppermute(passed, "lev", [(0, 1), (1, 3), (3, 2), (2, 0)]))
    else:
        parts = []
        for k in range(1, lev_count):
            parts.append(shift(patches[k], "lev", k))
        relayed = parts.pop(0)

    line_shape = jax.ShapeDtypeStruct((lev_count, portion, cols), BF16)
    side_shape = jax.ShapeDtypeStruct((lev_count, portion, 128), BF16)
    row_edge, col_edge = call(
        functools.partial(edge_kernel, rows, cols),
        (jax.ShapeDtypeStruct((2, lev_count, portion, cols), BF16), side_shape),
        [VM] * (3 + lev_count),
        flops // 8,
        12,
    )(index, across, down, *patches)
    from_left, from_right = from_sides(col_edge, "lon")
    up, down = call(
        functools.partial(corner_kernel, rows, cols),
        (line_shape, line_shape),
        [VM] * 3,
        flops // 64,
        8,
    )(row_edge, from_left, from_right)
    onto_first = shift(down, "lat", 1, wrap=False)
    onto_last = shift(up, "lat", -1, wrap=False)
    each = 2 if lev_count == 4 else 1
    joined = call(
        functools.partial(join_kernel, lev_count),
        (jax.ShapeDtypeStruct((each, 3, portion, 128), BF16),) * (lev_count // each),
        [SM] + [VM] * 4,
        flops // 64,
        12,
    )(lev, onto_first, onto_last, from_left, from_right)
    if lev_count == 4:
        got = paired(joined[1], 1)
        rim_shape = jax.ShapeDtypeStruct((3, portion, 128), BF16)
        kept, passing = call(fold_kernel, (rim_shape,) * 2, [VM] * 2, flops // 64, 8)(
            joined[0], got
        )
        rims = [kept, paired(passing, 2)]
    else:
        rims = [joined[0][0]]
        rims += [shift(joined[k], "lev", k)[0] for k in range(1, lev_count)]

    return call(
        functools.partial(final_kernel, rows, cols, lev_count, len(rims)),
        jax.ShapeDtypeStruct((portion, rows, cols), F32),
        [SM, VM, VM, VM] + [VM] * (2 + len(parts) + len(rims)),
        flops // 4,
        16,
        scratch_shapes=[
            pltpu.VMEM((portion // STEP, taps, STEP, slots), F32),
            pltpu.VMEM((3, portion, 128), F32),
            pltpu.VMEM((portion, rows, cols), F32),
            pltpu.SemaphoreType.DMA((portion // STEP,)),
        ],
        out_specs=HBM,
    )(lev, index, mine, across, *rims, patches[0], relayed, *parts)


def solution(mesh):
    return jax.shard_map(
        steps,
        mesh=mesh,
        in_specs=(
            P(None, "lat", "lon"),
            P("lev", None, None, None),
            P("lev", None, None),
            P("lev", None, None),
            P(),
            P(),
            P("lat", "lon", None, None),
            P(),
            P("lat", "lon", None),
            P("lat", "lon"),
        ),
        out_specs=P("lev", "lat", "lon"),
        check_vma=False,
    )
```

```python
import functools

import jax
import jax.numpy as jnp
from jax import lax
from jax.experimental import pallas as pl
from jax.experimental.pallas import tpu as pltpu
from jax.sharding import PartitionSpec as P

KAPPA = 0.7978845608028654
CUBIC = 0.044715
F32 = jnp.float32
BF16 = jnp.bfloat16


def gelu_slope(pre):
    square = pre * pre
    tanh_v = jnp.tanh(KAPPA * (pre + CUBIC * square * pre))
    value = 0.5 * pre * (1.0 + tanh_v)
    slope = 0.5 * (1.0 + tanh_v) + 0.5 * pre * (1.0 - tanh_v * tanh_v) * KAPPA * (
        1.0 + 3.0 * CUBIC * square
    )
    return value, slope


def nn(a, b):
    return lax.dot_general(a, b, (((1,), (0,)), ((), ())), preferred_element_type=F32)


def nt(a, b):
    return lax.dot_general(a, b, (((1,), (1,)), ((), ())), preferred_element_type=F32)


def tn(a, b):
    return lax.dot_general(a, b, (((0,), (0,)), ((), ())), preferred_element_type=F32)


ROUTES = ((0, 3, 2, 1), (1, 0, 2, 3), (2, 3, 1, 0), (3, 0, 1, 2))


def lookup(lev, values):
    found = jnp.int32(values[0])
    for i, value in enumerate(values[1:], 1):
        found = jnp.where(lev == i, value, found)
    return found


def relays(lev, count):
    return (lev == 1) | (lev == 2) if count == 4 else lev < 0


def source(lev, count, k):
    return lax.bitwise_xor(lev, k) if count == 4 else lax.rem(lev + k, count)


def target(lev, count, k):
    if count == 4:
        return lookup(lev, [ROUTES[i][k] for i in range(4)])
    return lax.rem(lev + k, count)


def place(lev, count, k):
    if count == 4:
        return lookup(lev, [ROUTES[i].index(i ^ (0, 2, 1, 3)[k]) for i in range(4)])
    return k


def split(index, cols):
    if cols & (cols - 1):
        return index // cols, index % cols
    bits = cols.bit_length() - 1
    return index >> bits, index & (cols - 1)


def hot(mask):
    return mask.astype(F32).astype(BF16)


def upright(index_ref):
    slots = index_ref.shape[1]
    return jnp.broadcast_to(index_ref[...], (128, slots)).T


def call(kernel, out_shape, in_specs, flops, mib, out_specs=None, **kwargs):
    bytes_out = sum(s.size * s.dtype.itemsize for s in jax.tree.leaves(out_shape))
    return pl.pallas_call(
        kernel,
        out_shape=out_shape,
        in_specs=in_specs,
        out_specs=out_specs or jax.tree.map(lambda _: VM, out_shape),
        cost_estimate=pl.CostEstimate(
            flops=flops, bytes_accessed=4 * bytes_out, transcendentals=0
        ),
        compiler_params=pltpu.CompilerParams(vmem_limit_bytes=mib << 20),
        **kwargs,
    )


STEP = 16

VM = pl.BlockSpec(memory_space=pltpu.VMEM)
SM = pl.BlockSpec(memory_space=pltpu.SMEM)
HBM = pl.BlockSpec(memory_space=pltpu.MemorySpace.HBM)


def turn_kernel(
    _, lat_ref, tile_ref, top_ref, bottom_ref, side_ref, near_ref, wide_ref, keep_ref, sems
):
    chans, rows, cols = lat_ref.shape
    count = rows // 8
    copies = [
        pltpu.make_async_copy(lat_ref.at[:, pl.ds(8 * i, 8)], near_ref.at[i], sems.at[i])
        for i in range(count)
    ]
    for copy in copies:
        copy.start()
    for i, copy in enumerate(copies):
        copy.wait()
        wide_ref[i] = near_ref[i].reshape(chans * 8, cols).astype(F32)
        for r in range(8 * i, 8 * i + 8):
            line = wide_ref[i, pl.ds(r - 8 * i, chans, stride=8), :].astype(BF16).T
            tile_ref[r * cols : (r + 1) * cols, :] = line
            keep_ref[0, r : r + 1, :] = line[0:1].astype(F32)
            keep_ref[1, r : r + 1, :] = line[cols - 1 : cols].astype(F32)
            if r == 0:
                top_ref[...] = line
            if r == rows - 1:
                bottom_ref[...] = line
    side_ref[...] = keep_ref[...].astype(BF16)


def gather_kernel(rows, cols, index_sm, index_ref, tile_ref, out_ref, table_ref, x_ref):
    chans = tile_ref.shape[1]
    slots = index_ref.shape[1]
    halves = chans // 128
    lead = cols + 8
    size = table_ref.shape[0]
    margin = (lead + 1) * 8
    table_ref[0:margin, :] = jnp.zeros((margin, 128), F32)
    table_ref[size - margin : size, :] = jnp.zeros((margin, 128), F32)
    for r in range(rows):
        line = tile_ref[r * cols : (r + 1) * cols, :].astype(F32)
        for b in range(3):
            for h in range(halves):
                at = (lead + r * cols - b + 1) * 8 + halves * b + h
                table_ref[pl.ds(at, cols, stride=8), :] = line[:, h * 128 : (h + 1) * 128]

    def body(i, carry):
        for j in range(8):
            s = i * 8 + j
            base = (index_sm[0, s] + (lead - cols)) * 8
            for a in range(3):
                x_ref[a, pl.ds(pl.multiple_of(s * 8, 8), 8), :] = table_ref[
                    pl.ds(pl.multiple_of(base + a * cols * 8, 8), 8), :
                ]
        return carry

    lax.fori_loop(0, slots // 8, body, 0)
    _, col = split(upright(index_ref), cols)
    for a in range(3):
        for b in range(3):
            for h in range(halves):
                x = x_ref[a, pl.ds(halves * b + h, slots, stride=8), :]
                if b != 1:
                    x = jnp.where(col == (0 if b == 0 else cols - 1), 0.0, x)
                out_ref[3 * a + b, :, h * 128 : (h + 1) * 128] = x.astype(BF16)


def decode_kernel(
    rows,
    cols,
    index_ref,
    x_ref,
    above_ref,
    below_ref,
    left_ref,
    right_ref,
    w_ref,
    mid_ref,
    outw_ref,
    s1_ref,
    s2_ref,
    field_ref,
    halo_ref,
):
    slots = index_ref.shape[1]
    groups, hidden, _ = mid_ref.shape
    levels = outw_ref.shape[1]
    width = halo_ref.shape[0]
    tall = (width - 2 * cols) // 2
    halo_ref[...] = jnp.zeros_like(halo_ref)
    halo_ref[0:cols, :] = above_ref[...]
    halo_ref[cols : 2 * cols, :] = below_ref[...]
    halo_ref[2 * cols : 2 * cols + rows + 2, :] = left_ref[1]
    halo_ref[2 * cols + tall : 2 * cols + tall + rows + 2, :] = right_ref[0]
    row, col = split(upright(index_ref), cols)
    starts = (0, cols, 2 * cols, width)
    cells = [
        lax.broadcasted_iota(jnp.int32, (slots, starts[i + 1] - starts[i]), 1) + starts[i]
        for i in range(3)
    ]
    lefts, rights = [], []
    for a in range(3):
        for b in range(3):
            at_row, at_col = row + (a - 1), col + (b - 1)
            rim = jnp.where(at_row < 0, at_col, jnp.where(at_row >= rows, cols + at_col, -1))
            rim = jnp.where(at_col < 0, 2 * cols + at_row + 1, rim)
            rim = jnp.where(at_col >= cols, 2 * cols + tall + at_row + 1, rim)
            x = x_ref[3 * a + b]
            reach = [i for i, near in enumerate((a == 0, a == 2, b != 1)) if near]
            if reach:
                picks, found = [], []
                for i in reach:
                    wide = jnp.concatenate([rim] * (cells[i].shape[1] // 128), 1)
                    picks.append(hot(cells[i] == wide))
                    found.append(halo_ref[starts[i] : starts[i + 1], :])
                picks, found = jnp.concatenate(picks, 1), jnp.concatenate(found, 0)
                x = x + nn(picks, found).astype(BF16)
            lefts.append(w_ref[3 * a + b])
            rights.append(x)
    acc = nt(jnp.concatenate(lefts, 1), jnp.concatenate(rights, 1))
    act, slope = gelu_slope(acc)
    s1_ref[...] = slope.astype(BF16)
    act = act.astype(BF16)
    for g in range(groups):
        two = nn(mid_ref[g], act[g * hidden : (g + 1) * hidden])
        value, slope = gelu_slope(two)
        s2_ref[g * hidden : (g + 1) * hidden, :] = slope.astype(BF16)
        field_ref[g * levels : (g + 1) * levels, :] = nn(
            outw_ref[g], value.astype(BF16)
        ).astype(BF16)


def prepare_kernel(
    lev_ref,
    count_ref,
    index_ref,
    latent_ref,
    obs_ref,
    weight_ref,
    inner_ref,
    outer_ref,
    w_ref,
    obst_ref,
    scale_ref,
    innert_ref,
    outert_ref,
    wt_ref,
    own_ref,
    across_ref,
    down_ref,
    turn_ref,
    sem,
):
    portion, _, cols = own_ref.shape
    rowc, colc = split(upright(index_ref), cols)
    count = index_ref.shape[1]
    cells = lax.broadcasted_iota(jnp.int32, (count, cols), 1)
    lines = lax.broadcasted_iota(jnp.int32, (count, 128), 1)
    for b in range(3):
        across_ref[b * count : (b + 1) * count, :] = hot(colc + (b - 1) == cells)
    for i, (e, a) in enumerate((e, a) for e in (0, 1) for a in range(3)):
        down_ref[i * count : (i + 1) * count, :] = hot(rowc + (a + 64 * e) == lines)
    fetch = pltpu.make_async_copy(
        latent_ref.at[pl.ds(pl.multiple_of(lev_ref[0] * portion, 8), portion)], own_ref, sem
    )
    fetch.start()
    obst_ref[...] = obs_ref[...].T
    slots = obs_ref.shape[0]
    levels = weight_ref.shape[1]
    weight = jnp.broadcast_to(weight_ref[...], (128, levels)).T
    live = lax.broadcasted_iota(jnp.int32, (levels, 128), 1)
    for h in range(slots // 128):
        scale_ref[:, h * 128 : (h + 1) * 128] = jnp.where(
            live + h * 128 < count_ref[0, 0], weight, 0.0
        )
    turn_ref[...] = inner_ref[...].T
    own = innert_ref.shape[0]
    innert_ref[...] = turn_ref[pl.ds(pl.multiple_of(lev_ref[0] * own, 16), own), :]
    outert_ref[...] = outer_ref[...].T
    for t in range(w_ref.shape[0]):
        wt_ref[t] = w_ref[t].T
    fetch.wait()


def column_kernel(
    lev_count,
    lev_ref,
    inner_ref,
    innert_ref,
    outer_ref,
    outert_ref,
    obst_ref,
    scale_ref,
    s1_ref,
    s2_ref,
    wt_ref,
    mid_ref,
    outw_ref,
    *rest,
):
    blocks = rest[:lev_count]
    outs = rest[lev_count : 2 * lev_count]
    f_ref, mis_ref = rest[2 * lev_count :]
    lev = lev_ref[0]
    own = blocks[0].shape[0]
    for k in range(lev_count):
        at = pl.multiple_of(source(lev, lev_count, k) * own, 16)
        f_ref[pl.ds(at, own), :] = blocks[k][...]
    wide = inner_ref.shape[0]
    fields = f_ref[...]
    acts, slopes = [], []
    for j in range(0, wide, 256):
        act, slope = gelu_slope(nn(inner_ref[j : j + 256, :], fields))
        acts.append(act.astype(BF16))
        slopes.append(slope)
    act = jnp.concatenate(acts, 0)
    misfits = []
    for j in range(0, own * lev_count, 256):
        forecast = f_ref[j : j + 256, :].astype(F32) + nn(outer_ref[j : j + 256, :], act)
        misfit = (forecast - obst_ref[j : j + 256, :]) * scale_ref[j : j + 256, :]
        mis_ref[j : j + 256, :] = misfit
        misfits.append(misfit.astype(BF16))
    misfit = jnp.concatenate(misfits, 0)
    grad_act = jnp.concatenate(
        [
            (nn(outert_ref[j : j + 256, :], misfit) * slopes[j // 256]).astype(BF16)
            for j in range(0, wide, 256)
        ],
        0,
    )
    mine = mis_ref[pl.ds(pl.multiple_of(lev * own, 16), own), :]
    grad_fields = (mine + nn(innert_ref[...], grad_act)).astype(BF16)
    groups, hidden, _ = mid_ref.shape
    levels = outw_ref.shape[1]
    ones = []
    for g in range(groups):
        span = slice(g * hidden, (g + 1) * hidden)
        two = (
            tn(outw_ref[g], grad_fields[g * levels : (g + 1) * levels]) * s2_ref[span, :].astype(F32)
        ).astype(BF16)
        ones.append((tn(mid_ref[g], two) * s1_ref[span, :].astype(F32)).astype(BF16))
    grad_one = jnp.concatenate(ones, 0)
    taps = wt_ref.shape[0]
    portion = wt_ref.shape[1] // lev_count
    for k in range(lev_count):
        at = pl.multiple_of(target(lev, lev_count, k) * portion, 16)
        left = jnp.concatenate([wt_ref[t, pl.ds(at, portion), :] for t in range(taps)], 0)
        outs[k][...] = nn(left, grad_one).astype(BF16).reshape(taps, portion, -1)


def edge_kernel(rows, cols, index_ref, across_ref, down_ref, *rest):
    blocks, (rowout_ref, colout_ref) = rest[:-2], rest[-2:]
    row, col = split(index_ref[...], cols)
    portion = rowout_ref.shape[2]

    def take(taps, where):
        return jnp.concatenate(
            [
                jnp.concatenate(
                    [jnp.where(where[i], block[t].astype(F32), 0.0).astype(BF16) for i, t in enumerate(taps)],
                    1,
                )
                for block in blocks
            ],
            0,
        )

    for e, (edge, a) in enumerate(((0, 0), (rows - 1, 2))):
        out = nn(take([3 * a + b for b in range(3)], [row == edge] * 3), across_ref[...])
        rowout_ref[e] = out.astype(BF16).reshape(len(blocks), portion, cols)
    taps = [3 * a + b for b in (0, 2) for a in range(3)]
    out = nn(take(taps, [col == 0] * 3 + [col == cols - 1] * 3), down_ref[...])
    colout_ref[...] = out.astype(BF16).reshape(len(blocks), portion, 128)


def corner_kernel(rows, cols, rowin_ref, left_ref, right_ref, up_ref, down_ref):
    lane = lax.broadcasted_iota(jnp.int32, up_ref.shape, 2)
    for e, (at, ref) in enumerate(((0, up_ref), (rows + 1, down_ref))):
        line = rowin_ref[e].astype(F32)
        line = line + jnp.where(lane == 0, left_ref[:, :, 64 + at : 65 + at].astype(F32), 0.0)
        line = line + jnp.where(
            lane == cols - 1, right_ref[:, :, at : at + 1].astype(F32), 0.0
        )
        ref[...] = line.astype(BF16)


def join_kernel(count, lev_ref, top_ref, bottom_ref, left_ref, right_ref, *outs):
    portion = top_ref.shape[1]
    spot = lax.broadcasted_iota(jnp.int32, (portion, 128), 1)
    each = count // len(outs)
    for k in range(count):
        out = outs[k // each].at[k % each]
        at = place(lev_ref[0], count, k)
        out[0] = top_ref[at]
        out[1] = bottom_ref[at]
        side = jnp.where(spot < 64, right_ref[at].astype(F32), left_ref[at].astype(F32))
        out[2] = side.astype(BF16)


def fold_kernel(kept_ref, got_ref, mine_ref, pass_ref):
    mine_ref[...] = (kept_ref[0].astype(F32) + got_ref[0].astype(F32)).astype(BF16)
    pass_ref[...] = (kept_ref[1].astype(F32) + got_ref[1].astype(F32)).astype(BF16)


def relay_kernel(count, lev_ref, block_ref, got_ref, out_ref):
    keep = jnp.where(relays(lev_ref[0], count), 1.0, 0.0)
    out_ref[...] = (block_ref[...].astype(F32) + got_ref[...].astype(F32) * keep).astype(BF16)


def partial_kernel(count, lev_ref, own_ref, relayed_ref, *rest):
    parts, out_ref = rest[:-1], rest[-1]
    keep = jnp.where(relays(lev_ref[0], count), 0.0, 1.0)
    total = own_ref[...].astype(F32) + relayed_ref[...].astype(F32) * keep
    for block in parts:
        total = total + block[...].astype(F32)
    out_ref[...] = total


def final_kernel(rows, cols, edges, lev_ref, index_ref, own_ref, across_ref, *rest):
    rims, early, last = rest[:edges], rest[edges], rest[edges + 1]
    out_ref, sum_ref, edge_ref, wait_ref, sems = rest[-5:]
    portion = out_ref.shape[0]
    row, _ = split(index_ref[...], cols)
    slots = row.shape[1]
    total = rims[0][...].astype(F32)
    for block in rims[1:]:
        total = total + block[...].astype(F32)
    edge_ref[...] = total
    lane = lax.broadcasted_iota(jnp.int32, (128, cols), 0)
    spot = lax.broadcasted_iota(jnp.int32, (128, cols), 1)
    ends = hot(((lane < 64) & (spot == cols - 1)) | ((lane >= 64) & (spot == 0)))
    hots = jnp.concatenate([across_ref[...], ends], 0)
    lines = lax.broadcasted_iota(jnp.int32, (rows, slots), 0)
    masks = [row + (a - 1) == lines for a in range(3)]
    place_of = lax.broadcasted_iota(jnp.int32, (rows, 128), 1)
    line_of = lax.broadcasted_iota(jnp.int32, (rows, 128), 0)
    picks = (place_of == line_of + 1) | (place_of == line_of + 65)
    high = lax.broadcasted_iota(jnp.int32, (rows, cols), 0)
    step = sum_ref.shape[2]
    outs = []
    for i, c0 in enumerate(range(0, portion, step)):
        span = slice(c0, c0 + step)
        sum_ref[i] = early[:, span, :] + last[:, span, :].astype(F32)
        lefts = []
        for c in range(step):
            pieces = []
            for b in range(3):
                part = jnp.zeros((rows, slots), F32)
                for a in range(3):
                    values = jnp.broadcast_to(sum_ref[i, 3 * a + b, c : c + 1, :], (rows, slots))
                    part = jnp.where(masks[a], values, part)
                pieces.append(part.astype(BF16))
            side = jnp.broadcast_to(edge_ref[2, c0 + c : c0 + c + 1, :], (rows, 128))
            pieces.append(jnp.where(picks, side, 0.0).astype(BF16))
            lefts.append(jnp.concatenate(pieces, 1))
        acc = nn(jnp.concatenate(lefts, 0), hots)
        for c in range(step):
            field = acc[c * rows : (c + 1) * rows] + own_ref[c0 + c].astype(F32)
            above = jnp.broadcast_to(edge_ref[0, c0 + c : c0 + c + 1, :], (rows, cols))
            below = jnp.broadcast_to(edge_ref[1, c0 + c : c0 + c + 1, :], (rows, cols))
            edge = jnp.where(high == 0, above, jnp.where(high == rows - 1, below, 0.0))
            wait_ref[c0 + c] = field + edge
        out = pltpu.make_async_copy(wait_ref.at[span], out_ref.at[span], sems.at[i])
        out.start()
        outs.append(out)
    for out in outs:
        out.wait()


def shift(x, axis, by, wrap=True):
    size = lax.axis_size(axis)
    pairs = [(i, (i + by) % size) for i in range(size) if wrap or 0 <= i + by < size]
    return lax.ppermute(x, axis, pairs)


def paired(x, k):
    return lax.ppermute(x, "lev", [(i, i ^ k) for i in range(4)])


def from_sides(x, axis):
    if lax.axis_size(axis) == 2:
        other = shift(x, axis, 1)
        return other, other
    return shift(x, axis, 1), shift(x, axis, -1)


def steps(
    latent,
    conv_weight,
    mid_weight,
    out_weight,
    inner,
    outer,
    obs_values,
    obs_weight,
    obs_index,
    obs_count,
):
    chans, rows, cols = latent.shape
    groups, hidden, taps, _ = conv_weight.shape
    levels = out_weight.shape[1]
    slots = obs_index.shape[-1]
    own = groups * levels
    wide = groups * hidden
    lev_count = lax.axis_size("lev")
    lev = lax.axis_index("lev").astype(jnp.int32).reshape(1)
    portion = chans // lev_count
    index = obs_index.reshape(1, slots)
    far = pltpu.with_memory_space_constraint(latent, pltpu.MemorySpace.HBM)
    flops = 2 * taps * wide * chans * slots

    strip = jax.ShapeDtypeStruct((cols, chans), BF16)
    tile, top, bottom, ends = call(
        turn_kernel,
        (
            jax.ShapeDtypeStruct((rows * cols, chans), BF16),
            strip,
            strip,
            jax.ShapeDtypeStruct((2, rows, chans), BF16),
        ),
        [SM, HBM],
        flops // 4,
        16,
        scratch_shapes=[
            pltpu.VMEM((rows // 8, chans, 8, cols), BF16),
            pltpu.VMEM((rows // 8, chans * 8, cols), F32),
            pltpu.VMEM((2, rows, chans), F32),
            pltpu.SemaphoreType.DMA((rows // 8,)),
        ],
    )(lev, far)
    above = shift(bottom, "lat", 1, wrap=False)
    below = shift(top, "lat", -1, wrap=False)
    columns = jnp.stack(
        [
            jnp.concatenate([above[at : at + 1], ends[e], below[at : at + 1]], 0)
            for e, at in enumerate((0, cols - 1))
        ]
    )
    from_left, from_right = from_sides(columns, "lon")

    x = call(
        functools.partial(gather_kernel, rows, cols),
        jax.ShapeDtypeStruct((taps, slots, chans), BF16),
        [SM, VM, VM],
        flops,
        26,
        scratch_shapes=[
            pltpu.VMEM((((rows + 2) * cols + 16) * 8, 128), F32),
            pltpu.VMEM((3, slots * 8, 128), F32),
        ],
    )(index, index, tile)
    w = jnp.transpose(conv_weight, (2, 0, 1, 3)).reshape(taps, wide, chans)
    act_shape = jax.ShapeDtypeStruct((wide, slots), BF16)
    slope_one, slope_two, fields = call(
        functools.partial(decode_kernel, rows, cols),
        (act_shape, act_shape, jax.ShapeDtypeStruct((own, slots), BF16)),
        [VM] * 9,
        flops * 2,
        20,
        scratch_shapes=[pltpu.VMEM((2 * cols + 128, chans), BF16)],
    )(index, x, above, below, from_left, from_right, w, mid_weight, out_weight)

    blocks = [fields]
    for k in range(1, lev_count):
        blocks.append(paired(fields, k) if lev_count == 4 else shift(fields, "lev", -k))
    column_shape = jax.ShapeDtypeStruct((own * lev_count, slots), F32)
    turned = call(
        prepare_kernel,
        (
            column_shape,
            column_shape,
            jax.ShapeDtypeStruct((own, inner.shape[0]), BF16),
            jax.ShapeDtypeStruct((outer.shape[1], outer.shape[0]), BF16),
            jax.ShapeDtypeStruct((taps, chans, wide), BF16),
            jax.ShapeDtypeStruct((portion, rows, cols), BF16),
            jax.ShapeDtypeStruct((3 * slots, cols), BF16),
            jax.ShapeDtypeStruct((6 * slots, 128), BF16),
        ),
        [SM, SM, VM, HBM] + [VM] * 5,
        flops,
        24,
        scratch_shapes=[
            pltpu.VMEM((inner.shape[1], inner.shape[0]), BF16),
            pltpu.SemaphoreType.DMA,
        ],
    )(lev, obs_count, index, far, obs_values[0, 0], obs_weight[None, :], inner, outer, w)
    obs_turned, scale, inner_turned, outer_turned, w_turned, mine, across, down = turned

    patch_shape = jax.ShapeDtypeStruct((taps, portion, slots), BF16)
    patches = call(
        functools.partial(column_kernel, lev_count),
        (patch_shape,) * lev_count,
        [SM] + [VM] * (11 + lev_count),
        flops * 4,
        32,
        scratch_shapes=[
            pltpu.VMEM((own * lev_count, slots), BF16),
            pltpu.VMEM((own * lev_count, slots), F32),
        ],
    )(
        lev,
        inner,
        inner_turned,
        outer,
        outer_turned,
        obs_turned,
        scale,
        slope_one,
        slope_two,
        w_turned,
        mid_weight,
        out_weight,
        *blocks,
    )
    if lev_count == 4:
        relayed = lax.ppermute(patches[1], "lev", [(0, 1), (1, 0), (2, 3), (3, 2)])
        parts = [lax.ppermute(patches[2], "lev", [(1, 2), (2, 1)])]
        parts.append(lax.ppermute(patches[2], "lev", [(0, 2), (3, 1)]))
        passed = call(
            functools.partial(relay_kernel, lev_count), patch_shape, [SM, VM, VM], flops // 64, 8
        )(lev, patches[3], relayed)
        parts.append(lax.ppermute(passed, "lev", [(0, 1), (1, 3), (3, 2), (2, 0)]))
    else:
        parts = []
        for k in range(1, lev_count):
            parts.append(shift(patches[k], "lev", k))
        relayed = parts.pop(0)

    line_shape = jax.ShapeDtypeStruct((lev_count, portion, cols), BF16)
    side_shape = jax.ShapeDtypeStruct((lev_count, portion, 128), BF16)
    row_edge, col_edge = call(
        functools.partial(edge_kernel, rows, cols),
        (jax.ShapeDtypeStruct((2, lev_count, portion, cols), BF16), side_shape),
        [VM] * (3 + lev_count),
        flops // 8,
        12,
    )(index, across, down, *patches)
    from_left, from_right = from_sides(col_edge, "lon")
    up, down = call(
        functools.partial(corner_kernel, rows, cols),
        (line_shape, line_shape),
        [VM] * 3,
        flops // 64,
        8,
    )(row_edge, from_left, from_right)
    onto_first = shift(down, "lat", 1, wrap=False)
    onto_last = shift(up, "lat", -1, wrap=False)
    each = 2 if lev_count == 4 else 1
    joined = call(
        functools.partial(join_kernel, lev_count),
        (jax.ShapeDtypeStruct((each, 3, portion, 128), BF16),) * (lev_count // each),
        [SM] + [VM] * 4,
        flops // 64,
        12,
    )(lev, onto_first, onto_last, from_left, from_right)
    if lev_count == 4:
        got = paired(joined[1], 1)
        rim_shape = jax.ShapeDtypeStruct((3, portion, 128), BF16)
        kept, passing = call(fold_kernel, (rim_shape,) * 2, [VM] * 2, flops // 64, 8)(
            joined[0], got
        )
        rims = [kept, paired(passing, 2)]
    else:
        rims = [joined[0][0]]
        rims += [shift(joined[k], "lev", k)[0] for k in range(1, lev_count)]

    early = call(
        functools.partial(partial_kernel, lev_count),
        jax.ShapeDtypeStruct((taps, portion, slots), F32),
        [SM] + [VM] * (1 + len(parts)),
        flops // 64,
        8,
    )(lev, patches[0], relayed, *parts[:-1])

    return call(
        functools.partial(final_kernel, rows, cols, len(rims)),
        jax.ShapeDtypeStruct((portion, rows, cols), F32),
        [SM, VM, VM, VM] + [VM] * (2 + len(rims)),
        flops // 4,
        16,
        scratch_shapes=[
            pltpu.VMEM((portion // STEP, taps, STEP, slots), F32),
            pltpu.VMEM((3, portion, 128), F32),
            pltpu.VMEM((portion, rows, cols), F32),
            pltpu.SemaphoreType.DMA((portion // STEP,)),
        ],
        out_specs=HBM,
    )(lev, index, mine, across, *rims, early, parts[-1])


def solution(mesh):
    return jax.shard_map(
        steps,
        mesh=mesh,
        in_specs=(
            P(None, "lat", "lon"),
            P("lev", None, None, None),
            P("lev", None, None),
            P("lev", None, None),
            P(),
            P(),
            P("lat", "lon", None, None),
            P(),
            P("lat", "lon", None),
            P("lat", "lon"),
        ),
        out_specs=P("lev", "lat", "lon"),
        check_vma=False,
    )
```
